32 devices in a mesh: src: 4 (over y, x), cell: 8 (over z, core).
Axes of the slice: x: 2, y: 2, z: 4, core: 2. Of those that a mesh axis runs over, the one named last changes fastest.
Arguments:
- green_source: bfloat16 [32, 8192], P('src', 'cell'), may hold values from -6 to 6
- green_receiver: bfloat16 [64, 8192], P('src', 'cell'), may hold values from -6 to 6
- pair_source: int32 [2048], P('src'), may hold values from 0 to 7
- pair_receiver: int32 [2048], P('src'), may hold values from 0 to 63
- cell_order: int32 [8, 1024], P('cell'), may hold values from 0 to 1023, each once within a row
- test_models: bfloat16 [128, 8192], P(None, 'cell'), may hold values from -6 to 6
- data_noise: bfloat16 [2048, 128], P('src'), may hold values from -8 to 8
Outputs:
- recovered: float32 [128, 8192], P('src', 'cell')
- data_residual: float32 [2048, 128], P(('src', 'cell'))
The draws below stay inside these ranges and needn't reach their ends.
Inputs may be any that keep to these rules, and one draw needn't show every extreme that they name: Each row of cell_order holds every number of 0 to 1023 once.
All inputs are finite; a program needn't handle non-finite values.
Results may differ from the reference program's by a relative error of at most 0.012.
Values may be sent and summed in bfloat16 or wider, within the bound.
A program may use at most 64 MiB of HBM per device.

```python
import math
import jax
import jax.numpy as jnp
from jax import lax

S_DEV = 8
R = 64
CD = 1024
NM = 128
HSTEPS = 2
PD = 512
PAIRS = 2048
TILES = 8
CELLS = 8192
SOURCES = 32


def place_ends(values, rng, smallest, top_value):
    longest = values.shape.index(max(values.shape))
    spots = []
    for shift in (0, 1):
        where = [jax.random.randint(jax.random.fold_in(rng, axis), (), 0, length) for axis, length in enumerate(values.shape)]
        where[longest] = (where[longest] + shift) % values.shape[longest]
        spots.append(tuple(where))
    return values.at[spots[0]].set(smallest).at[spots[1]].set(top_value)


def block_levels(rng, dims, shards, low, high):
    factor_of = 1.0
    for position, blocks in shards:
        draws = jax.random.uniform(jax.random.fold_in(jax.random.fold_in(rng, 6), position), (blocks,), jnp.float32, low / len(shards), high / len(shards))
        factor_of = factor_of * jnp.repeat(jnp.exp(draws), dims[position] // blocks).reshape((-1,) + (1,) * (len(dims) - 1 - position))
    return factor_of


def noise(rng, shape, scale, most, cuts=(), kind=jnp.bfloat16):
    drawn = scale * jax.random.normal(rng, shape, jnp.float32)
    if cuts:
        drawn = drawn * block_levels(rng, shape, cuts, -0.22, 0.18)
    return jnp.clip(drawn, -most, most).astype(kind)


def setup_inputs(seed: int = 0) -> dict:
    key_of = jax.random.split(jax.random.key(seed), 8)
    green_source = noise(key_of[0], (SOURCES, CELLS), 1.0, 6.0, ((0, 4), (1, 8)))
    green_receiver = noise(key_of[1], (R, CELLS), 1.0, 6.0, ((0, 4), (1, 8)))
    pair_source = place_ends(jax.random.randint(key_of[2], (PAIRS,), 0, S_DEV), jax.random.fold_in(key_of[2], 1), 0, S_DEV - 1).astype(jnp.int32)
    pair_receiver = place_ends(jax.random.randint(key_of[3], (PAIRS,), 0, R), jax.random.fold_in(key_of[3], 1), 0, R - 1).astype(jnp.int32)
    cell_order = jax.vmap(lambda own: jax.random.permutation(own, CD))(jax.random.split(key_of[4], TILES)).reshape((TILES, CD)).astype(jnp.int32)
    test_models = noise(key_of[5], (NM, CELLS), 1.0, 6.0, ((1, 8),))
    data_noise = noise(key_of[6], (PAIRS, NM), 0.5, 8.0, ((0, 4),))
    return dict(green_source=green_source, green_receiver=green_receiver, pair_source=pair_source, pair_receiver=pair_receiver, cell_order=cell_order, test_models=test_models, data_noise=data_noise)


def reference(green_source, green_receiver, pair_source, pair_receiver, cell_order, test_models, data_noise):
    scale = 1.0 / math.sqrt(CELLS)
    columns = (jnp.arange(TILES, dtype=jnp.int32)[:, None] * CD + cell_order).reshape(-1).astype(jnp.int32)
    source_tiles = jnp.take(green_source, columns, axis=1).reshape(SOURCES, TILES, CD).transpose(1, 0, 2)
    receiver_tiles = jnp.take(green_receiver, columns, axis=1).reshape(R, TILES, CD).transpose(1, 0, 2)
    source_rows = (jnp.arange(PAIRS, dtype=jnp.int32) // PD * S_DEV + pair_source).astype(jnp.int32)

    def tile_kernel(tile):
        left = jnp.take(source_tiles[tile], source_rows, axis=0).astype(jnp.float32)
        right = jnp.take(receiver_tiles[tile], pair_receiver, axis=0).astype(jnp.float32)
        rounded = lax.optimization_barrier((left * right).astype(jnp.bfloat16))
        return rounded.astype(jnp.float32)

    def forward(models):
        model_tiles = models.reshape(NM, TILES, CD).transpose(1, 0, 2)

        def add_tile(total, tile):
            kernel = tile_kernel(tile)
            return (total + jnp.dot(kernel, model_tiles[tile].T, precision=lax.Precision.HIGHEST), None)
        total, unused = lax.scan(add_tile, jnp.zeros((PAIRS, NM), jnp.float32), jnp.arange(TILES, dtype=jnp.int32))
        return total * scale

    def adjoint(weighted):

        def one_tile(tile):
            return jnp.dot(weighted.T, tile_kernel(tile), precision=lax.Precision.HIGHEST)
        parts = lax.map(one_tile, jnp.arange(TILES, dtype=jnp.int32))
        return parts.transpose(1, 0, 2).reshape(NM, CELLS) * scale
    observed = forward(test_models.astype(jnp.float32)) + data_noise.astype(jnp.float32)
    residual = -observed
    recovered = jnp.zeros((NM, CELLS), jnp.float32)
    for step in range(HSTEPS):
        spread = lax.optimization_barrier(jnp.sum(residual * residual, axis=0))
        delta = 1.0 * jnp.sqrt(spread / PAIRS + 1e-06)
        weight = delta[None, :] / jnp.maximum(jnp.abs(residual), delta[None, :])
        weighted = lax.optimization_barrier((weight * residual).astype(jnp.bfloat16)).astype(jnp.float32)
        grad = adjoint(weighted)
        grad_low = lax.optimization_barrier(grad.astype(jnp.bfloat16)).astype(jnp.float32)
        image = forward(grad_low)
        curvature = lax.optimization_barrier(jnp.sum(weight * image * image, axis=0))
        numer = lax.optimization_barrier(jnp.sum(grad * grad, axis=1))
        alpha = numer / (curvature + 1e-06)
        recovered = recovered - alpha[:, None] * grad
        residual = residual - alpha[None, :] * image
    return (recovered, residual)
```

```python
import functools
import math

import jax
import jax.numpy as jnp
from jax import lax
from jax.experimental import pallas as pl
from jax.experimental.pallas import tpu as pltpu
from jax.sharding import PartitionSpec as P

HSTEPS = 2
MESH = pl.DeviceIdType.MESH
F32 = jnp.float32
BF16 = jnp.bfloat16
NT = (((1,), (1,)), ((), ()))


def each(count, body):
    if count <= 8:
        for i in range(count - 1, 0, -1):
            body(i)
    else:

        def step(i, carry):
            body(count - i)
            return carry

        lax.fori_loop(1, count, step, 0)


def kernel_body(
    n_s, n_c,
    gs, gr, ps, pr, order, models, noise,
    rec_out, res_out,
    gs_in, gr_in, order_in, models_in, noise_in,
    fields, indices, nz_send, nz_recv,
    picks, oper, rs_send, rs_recv, ag, stat_send, stat_recv,
    fin_send, fin_recv, wlow, res, grads,
    load, in_send, in_recv, rs_ssem, rs_rsem, ag_ssem, ag_rsem, st_ssem, st_rsem, fin_ssem, fin_rsem,
):
    s = lax.axis_index("src")
    c = lax.axis_index("cell")
    group_pairs = ps.shape[1]
    cells = gs.shape[1]
    models_count = models.shape[0]
    own = models_count // n_s
    share = group_pairs // n_c
    chunk = share * n_s
    pairs_all = group_pairs * n_s
    s_dev = gs.shape[0]
    r_dev = gr.shape[0]
    scale = 1.0 / math.sqrt(cells * n_c)

    def src_peer(j):
        return jnp.bitwise_xor(s, j)

    def cell_peer(j):
        return jnp.bitwise_xor(c, j)

    def to_src(src_ref, dst_ref, ssem, rsem, peer):
        return pltpu.make_async_remote_copy(
            src_ref=src_ref, dst_ref=dst_ref, send_sem=ssem, recv_sem=rsem,
            device_id={"src": peer}, device_id_type=MESH,
        )

    def to_cell(src_ref, dst_ref, ssem, rsem, peer):
        return pltpu.make_async_remote_copy(
            src_ref=src_ref, dst_ref=dst_ref, send_sem=ssem, recv_sem=rsem,
            device_id={"cell": peer}, device_id_type=MESH,
        )

    barrier = pltpu.get_barrier_semaphore()
    each(n_s, lambda j: pl.semaphore_signal(
        barrier, inc=1, device_id={"src": src_peer(j)}, device_id_type=MESH))
    each(n_c, lambda j: pl.semaphore_signal(
        barrier, inc=1, device_id={"cell": cell_peer(j)}, device_id_type=MESH))

    loads = [
        pltpu.make_async_copy(order, order_in, load.at[0]),
        pltpu.make_async_copy(gs, gs_in, load.at[1]),
        pltpu.make_async_copy(gr, gr_in, load.at[2]),
        pltpu.make_async_copy(ps, indices.at[s, 0], load.at[3]),
        pltpu.make_async_copy(pr, indices.at[s, 1], load.at[4]),
        pltpu.make_async_copy(
            noise.at[pl.ds(pl.multiple_of(c * share, share), share), :], noise_in, load.at[5]),
        pltpu.make_async_copy(
            models.at[pl.ds(pl.multiple_of(s * own, own), own), :], models_in, load.at[6]),
    ]
    for copy in loads:
        copy.start()
    for copy in loads:
        copy.wait()
    rows = lax.broadcasted_iota(jnp.int32, (cells, cells), 0)
    select = jnp.where(rows == order_in[...], 1.0, 0.0).astype(BF16)
    raw = jnp.concatenate([gs_in[...].astype(F32), gr_in[...].astype(F32)], axis=0).astype(BF16)
    fields[s] = jnp.dot(raw, select, preferred_element_type=F32).astype(BF16)
    nz_send[...] = noise_in[...].astype(F32).T.reshape(n_s, own, share).astype(BF16)
    nz_recv[s] = nz_send[s]

    pl.semaphore_wait(barrier, n_s + n_c - 2)

    def in_copies(j, slot, which=(0, 1, 2)):
        peer = src_peer(j)
        makers = [
            lambda: to_src(fields.at[slot], fields.at[slot], in_send.at[0, j], in_recv.at[0, j], peer),
            lambda: to_src(indices.at[slot], indices.at[slot], in_send.at[1, j], in_recv.at[1, j], peer),
            lambda: to_src(nz_send.at[peer], nz_recv.at[slot], in_send.at[2, j], in_recv.at[2, j], peer),
        ]
        return [makers[n]() for n in which]

    each(n_s, lambda j: in_copies(j, s, (1,))[0].start())
    each(n_s, lambda j: in_copies(j, s, (0,))[0].start())
    each(n_s, lambda j: in_copies(j, s, (2,))[0].start())

    dev_rows = s_dev + r_dev
    field_rows = n_s * dev_rows
    row = lax.broadcasted_iota(jnp.int32, (field_rows, 1), 0)
    group = jnp.zeros((field_rows, 1), jnp.int32)
    for k in range(1, n_s):
        group = group + jnp.where(row >= k * dev_rows, 1, 0)
    within = row - group * dev_rows
    is_source = within < s_dev
    source_id = jnp.where(is_source, group * s_dev + within, -1)
    receiver_id = jnp.where(is_source, -1, group * r_dev + within - s_dev)

    each(n_s, lambda j: in_copies(j, src_peer(j), (1,))[0].wait_recv())

    for k in range(n_s):
        hit = (source_id == indices[k, 0] + k * s_dev) | (receiver_id == indices[k, 1])
        pick = jnp.where(hit, 1.0, 0.0).T.astype(BF16)
        for t in range(n_c):
            at = t * chunk + k * share
            picks[at : at + share, :] = pick[t * share : (t + 1) * share]
    each(n_s, lambda j: in_copies(j, src_peer(j), (0,))[0].wait_recv())
    every = fields[...].astype(F32).reshape(field_rows, cells)
    source_cols = jnp.where(is_source, every, 0.0).astype(BF16)
    receiver_cols = jnp.where(is_source, 0.0, every).astype(BF16)

    def build(k):
        at = pl.multiple_of(k * chunk, chunk)
        pick = picks[pl.ds(at, chunk), :]
        block = (
            jnp.dot(pick, source_cols, preferred_element_type=F32)
            * jnp.dot(pick, receiver_cols, preferred_element_type=F32)
        ).astype(BF16)
        oper[pl.ds(at, chunk), :] = block
        return block

    def rs_copy(phase, j, target):
        return to_cell(
            rs_send.at[phase, target], rs_recv.at[phase, j],
            rs_ssem.at[phase, j], rs_rsem.at[phase, j], target,
        )

    def forward(phase, low, after_sends):
        def part(k):
            at = pl.multiple_of(k * chunk, chunk)
            block = build(k) if phase == 0 else oper[pl.ds(at, chunk), :]
            return lax.dot_general(low, block, NT, preferred_element_type=F32)

        def one(j):
            target = cell_peer(j)
            rs_send[phase, target] = part(target).astype(BF16)
            rs_copy(phase, j, target).start()

        each(n_c, one)
        after_sends()
        rs_total = part(c)
        each(n_c, lambda j: rs_copy(phase, j, cell_peer(j)).wait_recv())
        for j in range(1, n_c):
            rs_total = rs_total + rs_recv[phase, j].astype(F32)
        return rs_total * scale

    def ag_copy(phase, j, slot):
        return to_cell(
            ag.at[phase, slot], ag.at[phase, slot],
            ag_ssem.at[phase, j], ag_rsem.at[phase, j], cell_peer(j),
        )

    def gather(phase, value):
        ag[phase, c] = value.astype(BF16)
        each(n_c, lambda j: ag_copy(phase, j, c).start())
        each(n_c, lambda j: ag_copy(phase, j, cell_peer(j)).wait_recv())
        return ag[phase].astype(F32)

    def stat_copy(step, j):
        return to_cell(
            stat_send.at[step], stat_recv.at[step, j],
            st_ssem.at[step, j], st_rsem.at[step, j], cell_peer(j),
        )

    diagonal = lax.broadcasted_iota(jnp.int32, (own, own), 0) == lax.broadcasted_iota(
        jnp.int32, (own, own), 1
    )

    def to_row(column):
        return jnp.sum(jnp.where(diagonal, column, 0.0), axis=0, keepdims=True)

    def to_column(row):
        return jnp.sum(jnp.where(diagonal, row, 0.0), axis=1, keepdims=True)

    def stat_start(step, first, second):
        top = lax.broadcasted_iota(jnp.int32, (8, own), 0) == 0
        stat_send[step] = jnp.where(top, to_row(first), to_row(second))
        each(n_c, lambda j: stat_copy(step, j).start())

    def stat_total(step):
        each(n_c, lambda j: stat_copy(step, j).wait_recv())
        total = stat_send[step]
        for j in range(1, n_c):
            total = total + stat_recv[step, j]
        return to_column(total[0:1]), to_column(total[1:2])

    own_models = models_in[...]
    first_data = forward(0, own_models, lambda: None)
    each(n_s, lambda j: in_copies(j, src_peer(j), (2,))[0].wait_recv())
    own_noise = jnp.concatenate([nz_recv[k].astype(F32) for k in range(n_s)], axis=1)
    chunk_res = -(first_data + own_noise)
    res[...] = gather(0, chunk_res)

    def pair_sum(values):
        return jnp.sum(jnp.sum(values, axis=0), axis=1, keepdims=True)

    alphas = []
    for step in range(HSTEPS):
        last = step == HSTEPS - 1
        full = res[...]
        spread = pair_sum(full * full)
        delta = jnp.sqrt(spread / pairs_all + 1e-06)
        weight = delta[None] / jnp.maximum(jnp.abs(full), delta[None])
        weighted = weight * full
        for k in range(n_c):
            wlow[:, k * chunk : (k + 1) * chunk] = weighted[k].astype(BF16)
        grad = jnp.dot(wlow[...], oper[...], preferred_element_type=F32) * scale
        after = []

        def send_numer():
            grads[step] = grad
            numer_own = jnp.sum(grad * grad, axis=1, keepdims=True)
            after.append(numer_own)
            if last:
                after.append(delta / jnp.maximum(jnp.abs(chunk_res), delta))
            else:
                stat_start(step, numer_own, numer_own)

        image = forward(step + 1, grad.astype(BF16), send_numer)
        if last:
            curve_own = jnp.sum(after[1] * image * image, axis=1, keepdims=True)
            stat_start(step, after[0], curve_own)
            numer, curvature = stat_total(step)
            alpha = numer / (curvature + 1e-06)
        else:
            images = gather(step + 1, image)
            numer, _ = stat_total(step)
            curvature = pair_sum(weight * images * images)
            alpha = numer / (curvature + 1e-06)
            res[...] = full - alpha[None] * images
        chunk_res = chunk_res - alpha * image
        alphas.append(alpha)

    for k in range(n_s):
        fin_send[k] = chunk_res[:, k * share : (k + 1) * share]

    def fin_copy(j, slot):
        return to_src(
            fin_send.at[src_peer(j)], fin_recv.at[slot], fin_ssem.at[j], fin_rsem.at[j], src_peer(j)
        )

    each(n_s, lambda j: fin_copy(j, s).start())
    fin_recv[s] = fin_send[s]
    total_rec = -(alphas[0] * grads[0])
    for step in range(1, HSTEPS):
        total_rec = total_rec - alphas[step] * grads[step]
    rec_out[...] = total_rec

    def in_done(j):
        for copy in in_copies(j, s):
            copy.wait_send()

    each(n_s, in_done)
    for phase in range(HSTEPS + 1):
        each(n_c, lambda j, phase=phase: rs_copy(phase, j, cell_peer(j)).wait_send())
    for phase in range(HSTEPS):
        each(n_c, lambda j, phase=phase: ag_copy(phase, j, c).wait_send())
        each(n_c, lambda j, phase=phase: stat_copy(phase, j).wait_send())
    each(n_s, lambda j: fin_copy(j, src_peer(j)).wait_recv())
    res_out[...] = fin_recv[...].reshape(models_count, share).T
    each(n_s, lambda j: fin_copy(j, s).wait_send())


def split_pair(value, lanes):
    high = value.astype(BF16).astype(F32)
    lane = lax.broadcasted_iota(jnp.int32, value.shape, 1)
    return jnp.where(lane < lanes, high, value - high)


def gathered_body(
    n_s, n_c,
    gs, gr, ps, pr, order, models, noise,
    rec_out, res_out,
    gs_in, gr_in, order_in, models_in, noise_in,
    fields, indices, nz_send, nz_recv, md_send, md_recv,
    select, gs_all, gr_all, mask, onehot,
    x_send, x_recv, fin_send, fin_recv,
    load, f_ssem, f_rsem, i_ssem, i_rsem, m_ssem, m_rsem, x_ssem, x_rsem, fin_ssem, fin_rsem,
):
    s = lax.axis_index("src")
    c = lax.axis_index("cell")
    pairs = ps.shape[1]
    cells = gs.shape[1]
    s_dev = gs.shape[0]
    r_dev = gr.shape[0]
    own = models.shape[0] // n_s
    mine = own // n_c
    half = cells // 2
    sources = n_s * s_dev
    receivers = n_s * r_dev
    pairs_all = pairs * n_s
    scale = 1.0 / math.sqrt(cells * n_c)

    def src_peer(j):
        return jnp.bitwise_xor(s, j)

    def cell_peer(j):
        return jnp.bitwise_xor(c, j)

    def remote(src_ref, dst_ref, ssem, rsem, ds, dc):
        return pltpu.make_async_remote_copy(
            src_ref=src_ref, dst_ref=dst_ref, send_sem=ssem, recv_sem=rsem,
            device_id={"src": src_peer(ds), "cell": cell_peer(dc)}, device_id_type=MESH,
        )

    barrier = pltpu.get_barrier_semaphore()
    each(n_s, lambda j: pl.semaphore_signal(
        barrier, inc=1, device_id={"src": src_peer(j)}, device_id_type=MESH))
    each(n_c, lambda j: pl.semaphore_signal(
        barrier, inc=1, device_id={"cell": cell_peer(j)}, device_id_type=MESH))

    loads = [
        pltpu.make_async_copy(gs, gs_in, load.at[0]),
        pltpu.make_async_copy(gr, gr_in, load.at[1]),
        pltpu.make_async_copy(order, order_in, load.at[2]),
        pltpu.make_async_copy(
            models.at[pl.ds(pl.multiple_of(s * own, own), own), :], models_in, load.at[3]),
        pltpu.make_async_copy(noise, noise_in, load.at[4]),
        pltpu.make_async_copy(ps, indices.at[s, 0], load.at[5]),
        pltpu.make_async_copy(pr, indices.at[s, 1], load.at[6]),
    ]
    for copy in loads:
        copy.start()
    for copy in loads:
        copy.wait()
    fields[c, s] = jnp.concatenate(
        [gs_in[...].astype(F32), gr_in[...].astype(F32)], axis=0).astype(BF16)

    rows = lax.broadcasted_iota(jnp.int32, (cells, cells), 0)
    select[...] = jnp.where(rows == order_in[...], 1.0, 0.0).astype(BF16)
    wide = 2 * mine
    q = lax.broadcasted_iota(jnp.int32, (n_c * wide, own), 0)
    m = lax.broadcasted_iota(jnp.int32, (n_c * wide, own), 1)
    spread_rows = jnp.where((q // wide) * mine + q % mine == m, 1.0, 0.0).astype(BF16)
    wide_models = jnp.dot(spread_rows, models_in[...], preferred_element_type=F32).astype(BF16)
    placed = lax.dot_general(wide_models, select[...], NT, preferred_element_type=F32)
    low = lax.broadcasted_iota(jnp.int32, (n_c * wide, half), 0) % wide < mine
    placed = jnp.where(low, placed[:, :half], placed[:, half:])
    md_send[...] = placed.astype(BF16).reshape(n_c, wide, half)
    md_recv[c] = md_send[c]
    q = lax.broadcasted_iota(jnp.int32, (n_s * wide, models.shape[0]), 0)
    m = lax.broadcasted_iota(jnp.int32, (n_s * wide, models.shape[0]), 1)
    columns = jnp.where(
        ((q // wide) * own + c * mine + q % wide == m) & (q % wide < mine), 1.0, 0.0).astype(BF16)
    nz = lax.dot_general(columns, noise_in[...], NT, preferred_element_type=F32)
    nz_send[...] = nz.astype(BF16).reshape(n_s, wide, pairs)
    nz_recv[s] = nz_send[s]

    pl.semaphore_wait(barrier, n_s + n_c - 2)

    done = []
    count = [0]

    def send_block(t, g, ds, dc):
        at = count[0]
        count[0] += 1
        copy = remote(fields.at[t, g], fields.at[t, g], f_ssem.at[at], f_rsem.at[t, g], ds, dc)
        copy.start()
        done.append(copy.wait_send)

    def got_block(t, g):
        remote(fields.at[t, g], fields.at[t, g], f_ssem.at[0], f_rsem.at[t, g], 0, 1).wait_recv()

    def index_copy(j, slot):
        return remote(indices.at[slot], indices.at[slot], i_ssem.at[0, j], i_rsem.at[0, j], j, 0)

    def noise_copy(j):
        return remote(
            nz_send.at[src_peer(j)], nz_recv.at[s], i_ssem.at[1, j], i_rsem.at[1, j], j, 0)

    def noise_got(j):
        g = src_peer(j)
        remote(nz_send.at[g], nz_recv.at[g], i_ssem.at[1, j], i_rsem.at[1, j], j, 0).wait_recv()

    def model_copy(j):
        return remote(md_send.at[cell_peer(j)], md_recv.at[c], m_ssem.at[j], m_rsem.at[j], 0, j)

    def model_got(j):
        t = cell_peer(j)
        remote(md_send.at[t], md_recv.at[t], m_ssem.at[j], m_rsem.at[j], 0, j).wait_recv()

    steps = range(2, n_c, 2)
    for d in reversed(steps):
        send_block(c, s, 0, d)
    for j in range(n_s - 1, 0, -1):
        send_block(c, s, j, 0)
    send_block(c, s, 0, 1)
    each(n_s, lambda j: index_copy(j, s).start())
    each(n_c, lambda j: model_copy(j).start())
    each(n_s, lambda j: noise_copy(j).start())

    for d in steps:
        t = cell_peer(d)
        got_block(t, s)
        for j in range(n_s - 1, 0, -1):
            send_block(t, s, j, 0)
        send_block(t, s, 0, 1)

    each(n_s, lambda j: index_copy(j, src_peer(j)).wait_recv())
    row = lax.broadcasted_iota(jnp.int32, (2 * receivers, pairs), 0)
    row = jnp.where(row < receivers, row, row - receivers)
    source = lax.broadcasted_iota(jnp.int32, (s_dev, pairs), 0)
    for g in range(n_s):
        mask[g] = jnp.where(source == indices[g, 0], 1.0, 0.0)
        onehot[g] = jnp.where(row == indices[g, 1], 1.0, 0.0).astype(BF16)
    each(n_c, model_got)

    def unpack(t):
        block = fields[t].astype(F32)
        gs_all[t] = block[:, :s_dev].reshape(sources, cells)
        part = block[:, s_dev:].reshape(receivers, cells).astype(BF16)
        gr_all[t] = jnp.concatenate([part, part], axis=0)

    def forward(t, lines):
        base = gs_all[t]
        left = jnp.concatenate([(base * line).astype(BF16) for line in lines], axis=0)
        return lax.dot_general(left, gr_all[t], NT, preferred_element_type=F32)

    data = [None]

    def first(d):
        t = cell_peer(d)
        unpack(t)
        line = md_recv[t].astype(F32)
        lines = [
            jnp.concatenate([line[j : j + 1], line[mine + j : mine + j + 1]], axis=1)
            for j in range(mine)
        ]
        part = forward(t, lines)
        data[0] = part if data[0] is None else data[0] + part

    def own_core(d):
        t = cell_peer(d)
        for j in range(1, n_s):
            g = src_peer(j)
            got_block(t, g)
            send_block(t, g, 0, 1)
        first(d)

    def other_core(d):
        t = cell_peer(d + 1)
        for j in range(n_s):
            got_block(t, src_peer(j))
        first(d + 1)

    own_core(0)
    for d in steps:
        own_core(d)
        other_core(d - 2)
    other_core(n_c - 2)

    def to_pairs(value):
        mixed = split_pair(value * scale, receivers).reshape(mine, n_s, s_dev, 2 * receivers)
        out = []
        for g in range(n_s):
            left = mixed[:, g].reshape(mine * s_dev, 2 * receivers).astype(BF16)
            at_pairs = jnp.dot(left, onehot[g], preferred_element_type=F32)
            out.append(at_pairs.reshape(mine, s_dev, pairs) * mask[g][None])
        return out

    def from_pairs(values):
        out = [
            lax.dot_general(
                values[g].reshape(mine * s_dev, pairs).astype(BF16), onehot[g], NT,
                preferred_element_type=F32).reshape(mine, 1, s_dev, 2 * receivers)
            for g in range(n_s)
        ]
        whole = jnp.concatenate(out, axis=1).reshape(mine * sources, 2 * receivers)
        return split_pair(whole * scale, receivers).astype(BF16)

    def pair_sum(values):
        total = values[0]
        for value in values[1:]:
            total = total + value
        return jnp.sum(jnp.sum(total, axis=2, keepdims=True), axis=1, keepdims=True)

    def x_copy(step, j):
        return remote(
            x_send.at[step, cell_peer(j)], x_recv.at[step, c],
            x_ssem.at[step, j], x_rsem.at[step, j], 0, j)

    def x_got(step, j):
        t = cell_peer(j)
        remote(
            x_send.at[step, t], x_recv.at[step, t],
            x_ssem.at[step, j], x_rsem.at[step, j], 0, j).wait_recv()

    each(n_s, noise_got)
    first_data = to_pairs(data[0])
    res = []
    for g in range(n_s):
        line = nz_recv[g].astype(F32)
        lines = jnp.concatenate([line[j : j + 1][None] for j in range(mine)], axis=0)
        res.append(-(first_data[g] + lines * mask[g][None]))

    place = lax.broadcasted_iota(jnp.int32, (wide, half), 0)
    alphas = []
    for step in range(HSTEPS):
        delta = jnp.sqrt(pair_sum([value * value for value in res]) / pairs_all + 1e-06)
        weight = [delta / jnp.maximum(jnp.abs(value), delta) for value in res]
        back = from_pairs([w * value for w, value in zip(weight, res)])
        numer = None
        data = None
        for d in range(n_c):
            t = cell_peer(d)
            fan = jnp.dot(back, gr_all[t], preferred_element_type=F32)
            grad = jnp.sum(
                fan.reshape(mine, sources, cells) * gs_all[t][None], axis=1, keepdims=True)
            square = grad * grad
            numer = square if numer is None else numer + square
            low = grad.astype(BF16).astype(F32)
            part = forward(t, [low[j] for j in range(mine)])
            data = part if data is None else data + part
            packed = jnp.zeros((wide, half), F32)
            for j in range(mine):
                packed = jnp.where(place == j, low[j][:, :half], packed)
                packed = jnp.where(place == mine + j, low[j][:, half:], packed)
            if d == 0:
                x_recv[step, t] = packed.astype(BF16)
            else:
                x_send[step, t] = packed.astype(BF16)
                x_copy(step, d).start()
        image = to_pairs(data)
        curvature = pair_sum([w * value * value for w, value in zip(weight, image)])
        alpha = jnp.sum(numer, axis=2, keepdims=True) / (curvature + 1e-06)
        res = [value - alpha * other for value, other in zip(res, image)]
        alphas.append(alpha)

    odd = c % 2
    two = 2 * (pairs // n_c)
    place = lax.broadcasted_iota(jnp.int32, (wide, pairs), 0)
    lane = lax.broadcasted_iota(jnp.int32, (wide, pairs), 1) % two < two // 2
    marks = jnp.zeros((wide, pairs), F32)
    for j in range(mine):
        marks = jnp.where(
            place == (1 - odd) * mine + j, jnp.where(lane, alphas[0][j], alphas[1][j]), marks)
    for g in range(n_s):
        lines = jnp.sum(res[g], axis=1, keepdims=True)
        note = marks
        for j in range(mine):
            note = jnp.where(place == odd * mine + j, lines[j], note)
        for h in range(n_c // 2):
            fin_send[g, h] = note[:, h * two : (h + 1) * two]

    def fin_copy(a, b):
        return remote(
            fin_send.at[src_peer(a), cell_peer(b) // 2], fin_recv.at[s, c],
            fin_ssem.at[a, b], fin_rsem.at[a, b], a, b)

    def fin_got(a, b):
        g, t = src_peer(a), cell_peer(b)
        remote(
            fin_send.at[g, t // 2], fin_recv.at[g, t],
            fin_ssem.at[a, b], fin_rsem.at[a, b], a, b).wait_recv()

    others = n_s * n_c

    def over_others(act):
        def one(i, carry):
            at = others - i
            act(at // n_c, at % n_c)
            return carry

        lax.fori_loop(1, others, one, 0)

    over_others(lambda a, b: fin_copy(a, b).start())
    fin_recv[s, c] = fin_send[s, c // 2]

    for step in range(HSTEPS):
        each(n_c, lambda j, step=step: x_got(step, j))
    got = x_recv[...].astype(F32).reshape(HSTEPS * n_c // 2, 2, wide, half)
    first_of, second_of = got[:, 0], got[:, 1]

    def turned(value):
        return jnp.concatenate([value[:, mine:], value[:, :mine]], axis=1)

    top = lax.broadcasted_iota(jnp.int32, first_of.shape, 1) < mine
    lower = jnp.where(top, first_of, turned(second_of)).reshape(HSTEPS * own, half)
    upper = jnp.where(top, turned(first_of), second_of).reshape(HSTEPS * own, half)
    grads = jnp.concatenate([lower, upper], axis=1).astype(BF16)
    grads = jnp.dot(grads, select[...], preferred_element_type=F32)

    for wait in done:
        wait()
    each(n_s, lambda j: index_copy(j, s).wait_send())
    each(n_c, lambda j: model_copy(j).wait_send())
    each(n_s, lambda j: noise_copy(j).wait_send())
    for step in range(HSTEPS):
        each(n_c, lambda j, step=step: x_copy(step, j).wait_send())

    over_others(fin_got)
    notes = fin_recv[s].reshape(n_c // 2, 2, wide, two)
    top = lax.broadcasted_iota(jnp.int32, (n_c // 2, wide, two), 1) < mine
    factor = turned(jnp.where(top, notes[:, 1], notes[:, 0])).reshape(own, two)
    rec_out[...] = -(
        factor[:, :1] * grads[:own] + factor[:, two // 2 : two // 2 + 1] * grads[own:])
    notes = fin_recv[...].reshape(n_s * n_c // 2, 2, wide, two)
    top = lax.broadcasted_iota(jnp.int32, (n_s * n_c // 2, wide, two), 1) < mine
    lines = jnp.where(top, notes[:, 0], notes[:, 1]).reshape(n_s * own, two).T
    res_out[...] = jnp.where(odd == 0, lines[: two // 2], lines[two // 2 :])
    over_others(lambda a, b: fin_copy(a, b).wait_send())


def gathered_call(n_s, n_c, *arrays):
    gs, gr, ps, _, order, models, noise = arrays
    s_dev, cells = gs.shape
    r_dev = gr.shape[0]
    pairs = ps.shape[1]
    models_count = models.shape[0]
    own = models_count // n_s
    wide = 2 * (own // n_c)
    share = pairs // n_c
    dma = pltpu.SemaphoreType.DMA
    return pl.pallas_call(
        functools.partial(gathered_body, n_s, n_c),
        out_shape=(
            pltpu.VMEM((own, cells), F32),
            pltpu.VMEM((share, models_count), F32),
        ),
        in_specs=[pl.BlockSpec(memory_space=pltpu.HBM)] * 7,
        out_specs=[pl.BlockSpec(memory_space=pltpu.VMEM)] * 2,
        scratch_shapes=[
            pltpu.VMEM((s_dev, cells), BF16),
            pltpu.VMEM((r_dev, cells), BF16),
            pltpu.VMEM((1, cells), jnp.int32),
            pltpu.VMEM((own, cells), BF16),
            pltpu.VMEM((pairs, models_count), BF16),
            pltpu.VMEM((n_c, n_s, s_dev + r_dev, cells), BF16),
            pltpu.VMEM((n_s, 2, 1, pairs), jnp.int32),
            pltpu.VMEM((n_s, wide, pairs), BF16),
            pltpu.VMEM((n_s, wide, pairs), BF16),
            pltpu.VMEM((n_c, wide, cells // 2), BF16),
            pltpu.VMEM((n_c, wide, cells // 2), BF16),
            pltpu.VMEM((cells, cells), BF16),
            pltpu.VMEM((n_c, n_s * s_dev, cells), F32),
            pltpu.VMEM((n_c, 2 * n_s * r_dev, cells), BF16),
            pltpu.VMEM((n_s, s_dev, pairs), F32),
            pltpu.VMEM((n_s, 2 * n_s * r_dev, pairs), BF16),
            pltpu.VMEM((HSTEPS, n_c, wide, cells // 2), BF16),
            pltpu.VMEM((HSTEPS, n_c, wide, cells // 2), BF16),
            pltpu.VMEM((n_s, n_c // 2, wide, 2 * share), F32),
            pltpu.VMEM((n_s, n_c, wide, 2 * share), F32),
            dma((7,)), dma((n_s * n_c,)), dma((n_c, n_s)),
            dma((2, n_s)), dma((2, n_s)),
            dma((n_c,)), dma((n_c,)),
            dma((HSTEPS, n_c)), dma((HSTEPS, n_c)),
            dma((n_s, n_c)), dma((n_s, n_c)),
        ],
        compiler_params=pltpu.CompilerParams(
            collective_id=0, has_side_effects=True, vmem_limit_bytes=60 * 1024 * 1024
        ),
    )(*arrays)


def fits_gathered(n_s, n_c, s_dev, r_dev, cells, pairs, models_count):
    return (
        n_c & (n_c - 1) == 0 and n_s & (n_s - 1) == 0
        and models_count == 4 * n_s * n_c
        and s_dev == 8 and r_dev % 8 == 0 and 2 * n_s * r_dev == 128
        and pairs == 64 * n_c and cells % 256 == 0
    )


def shards(
    green_source, green_receiver, pair_source, pair_receiver, cell_order, test_models, data_noise
):
    n_s = lax.axis_size("src")
    n_c = lax.axis_size("cell")
    s_dev, cells = green_source.shape
    r_dev = green_receiver.shape[0]
    group_pairs = pair_source.shape[0]
    models_count = test_models.shape[0]
    own = models_count // n_s
    share = group_pairs // n_c
    chunk = share * n_s
    pairs_all = group_pairs * n_s
    arrays = (
        green_source, green_receiver, pair_source[None, :], pair_receiver[None, :],
        cell_order, test_models, data_noise,
    )
    if fits_gathered(n_s, n_c, s_dev, r_dev, cells, group_pairs, models_count):
        return gathered_call(n_s, n_c, *arrays)
    dma = pltpu.SemaphoreType.DMA
    return pl.pallas_call(
        functools.partial(kernel_body, n_s, n_c),
        out_shape=(
            pltpu.VMEM((own, cells), F32),
            pltpu.VMEM((share, models_count), F32),
        ),
        in_specs=[pl.BlockSpec(memory_space=pltpu.HBM)] * 7,
        out_specs=[pl.BlockSpec(memory_space=pltpu.VMEM)] * 2,
        scratch_shapes=[
            pltpu.VMEM((s_dev, cells), BF16),
            pltpu.VMEM((r_dev, cells), BF16),
            pltpu.VMEM((1, cells), jnp.int32),
            pltpu.VMEM((own, cells), BF16),
            pltpu.VMEM((share, models_count), BF16),
            pltpu.VMEM((n_s, s_dev + r_dev, cells), BF16),
            pltpu.VMEM((n_s, 2, 1, group_pairs), jnp.int32),
            pltpu.VMEM((n_s, own, share), BF16),
            pltpu.VMEM((n_s, own, share), BF16),
            pltpu.VMEM((pairs_all, n_s * (s_dev + r_dev)), BF16),
            pltpu.VMEM((pairs_all, cells), BF16),
            pltpu.VMEM((HSTEPS + 1, n_c, own, chunk), BF16),
            pltpu.VMEM((HSTEPS + 1, n_c, own, chunk), BF16),
            pltpu.VMEM((HSTEPS, n_c, own, chunk), BF16),
            pltpu.VMEM((HSTEPS, 8, own), F32),
            pltpu.VMEM((HSTEPS, n_c, 8, own), F32),
            pltpu.VMEM((n_s, own, share), F32),
            pltpu.VMEM((n_s, own, share), F32),
            pltpu.VMEM((own, pairs_all), BF16),
            pltpu.VMEM((n_c, own, chunk), F32),
            pltpu.VMEM((HSTEPS, own, cells), F32),
            dma((7,)), dma((3, n_s)), dma((3, n_s)),
            dma((HSTEPS + 1, n_c)), dma((HSTEPS + 1, n_c)),
            dma((HSTEPS, n_c)), dma((HSTEPS, n_c)),
            dma((HSTEPS, n_c)), dma((HSTEPS, n_c)),
            dma((n_s,)), dma((n_s,)),
        ],
        compiler_params=pltpu.CompilerParams(
            collective_id=0, has_side_effects=True, vmem_limit_bytes=60 * 1024 * 1024
        ),
    )(*arrays)


def solution(mesh):
    return jax.shard_map(
        shards,
        mesh=mesh,
        in_specs=(
            P("src", "cell"),
            P("src", "cell"),
            P("src"),
            P("src"),
            P("cell", None),
            P(None, "cell"),
            P("src", None),
        ),
        out_specs=(P("src", "cell"), P(("src", "cell"), None)),
        check_vma=False,
    )
```

```python
import functools
import math

import jax
import jax.numpy as jnp
from jax import lax
from jax.experimental import pallas as pl
from jax.experimental.pallas import tpu as pltpu
from jax.sharding import PartitionSpec as P

HSTEPS = 2
MESH = pl.DeviceIdType.MESH
F32 = jnp.float32
BF16 = jnp.bfloat16
NT = (((1,), (1,)), ((), ()))


def each(count, body):
    if count <= 8:
        for i in range(count - 1, 0, -1):
            body(i)
    else:

        def step(i, carry):
            body(count - i)
            return carry

        lax.fori_loop(1, count, step, 0)


def kernel_body(
    n_s, n_c,
    gs, gr, ps, pr, order, models, noise,
    rec_out, res_out,
    gs_in, gr_in, order_in, models_in, noise_in,
    fields, indices, nz_send, nz_recv,
    picks, oper, rs_send, rs_recv, ag, stat_send, stat_recv,
    fin_send, fin_recv, wlow, res, grads,
    load, in_send, in_recv, rs_ssem, rs_rsem, ag_ssem, ag_rsem, st_ssem, st_rsem, fin_ssem, fin_rsem,
):
    s = lax.axis_index("src")
    c = lax.axis_index("cell")
    group_pairs = ps.shape[1]
    cells = gs.shape[1]
    models_count = models.shape[0]
    own = models_count // n_s
    share = group_pairs // n_c
    chunk = share * n_s
    pairs_all = group_pairs * n_s
    s_dev = gs.shape[0]
    r_dev = gr.shape[0]
    scale = 1.0 / math.sqrt(cells * n_c)

    def src_peer(j):
        return jnp.bitwise_xor(s, j)

    def cell_peer(j):
        return jnp.bitwise_xor(c, j)

    def to_src(src_ref, dst_ref, ssem, rsem, peer):
        return pltpu.make_async_remote_copy(
            src_ref=src_ref, dst_ref=dst_ref, send_sem=ssem, recv_sem=rsem,
            device_id={"src": peer}, device_id_type=MESH,
        )

    def to_cell(src_ref, dst_ref, ssem, rsem, peer):
        return pltpu.make_async_remote_copy(
            src_ref=src_ref, dst_ref=dst_ref, send_sem=ssem, recv_sem=rsem,
            device_id={"cell": peer}, device_id_type=MESH,
        )

    barrier = pltpu.get_barrier_semaphore()
    each(n_s, lambda j: pl.semaphore_signal(
        barrier, inc=1, device_id={"src": src_peer(j)}, device_id_type=MESH))
    each(n_c, lambda j: pl.semaphore_signal(
        barrier, inc=1, device_id={"cell": cell_peer(j)}, device_id_type=MESH))

    loads = [
        pltpu.make_async_copy(order, order_in, load.at[0]),
        pltpu.make_async_copy(gs, gs_in, load.at[1]),
        pltpu.make_async_copy(gr, gr_in, load.at[2]),
        pltpu.make_async_copy(ps, indices.at[s, 0], load.at[3]),
        pltpu.make_async_copy(pr, indices.at[s, 1], load.at[4]),
        pltpu.make_async_copy(
            noise.at[pl.ds(pl.multiple_of(c * share, share), share), :], noise_in, load.at[5]),
        pltpu.make_async_copy(
            models.at[pl.ds(pl.multiple_of(s * own, own), own), :], models_in, load.at[6]),
    ]
    for copy in loads:
        copy.start()
    for copy in loads:
        copy.wait()
    rows = lax.broadcasted_iota(jnp.int32, (cells, cells), 0)
    select = jnp.where(rows == order_in[...], 1.0, 0.0).astype(BF16)
    raw = jnp.concatenate([gs_in[...].astype(F32), gr_in[...].astype(F32)], axis=0).astype(BF16)
    fields[s] = jnp.dot(raw, select, preferred_element_type=F32).astype(BF16)
    nz_send[...] = noise_in[...].astype(F32).T.reshape(n_s, own, share).astype(BF16)
    nz_recv[s] = nz_send[s]

    pl.semaphore_wait(barrier, n_s + n_c - 2)

    def in_copies(j, slot, which=(0, 1, 2)):
        peer = src_peer(j)
        makers = [
            lambda: to_src(fields.at[slot], fields.at[slot], in_send.at[0, j], in_recv.at[0, j], peer),
            lambda: to_src(indices.at[slot], indices.at[slot], in_send.at[1, j], in_recv.at[1, j], peer),
            lambda: to_src(nz_send.at[peer], nz_recv.at[slot], in_send.at[2, j], in_recv.at[2, j], peer),
        ]
        return [makers[n]() for n in which]

    each(n_s, lambda j: in_copies(j, s, (1,))[0].start())
    each(n_s, lambda j: in_copies(j, s, (0,))[0].start())
    each(n_s, lambda j: in_copies(j, s, (2,))[0].start())

    dev_rows = s_dev + r_dev
    field_rows = n_s * dev_rows
    row = lax.broadcasted_iota(jnp.int32, (field_rows, 1), 0)
    group = jnp.zeros((field_rows, 1), jnp.int32)
    for k in range(1, n_s):
        group = group + jnp.where(row >= k * dev_rows, 1, 0)
    within = row - group * dev_rows
    is_source = within < s_dev
    source_id = jnp.where(is_source, group * s_dev + within, -1)
    receiver_id = jnp.where(is_source, -1, group * r_dev + within - s_dev)

    each(n_s, lambda j: in_copies(j, src_peer(j), (1,))[0].wait_recv())

    for k in range(n_s):
        hit = (source_id == indices[k, 0] + k * s_dev) | (receiver_id == indices[k, 1])
        pick = jnp.where(hit, 1.0, 0.0).T.astype(BF16)
        for t in range(n_c):
            at = t * chunk + k * share
            picks[at : at + share, :] = pick[t * share : (t + 1) * share]
    each(n_s, lambda j: in_copies(j, src_peer(j), (0,))[0].wait_recv())
    every = fields[...].astype(F32).reshape(field_rows, cells)
    source_cols = jnp.where(is_source, every, 0.0).astype(BF16)
    receiver_cols = jnp.where(is_source, 0.0, every).astype(BF16)

    def build(k):
        at = pl.multiple_of(k * chunk, chunk)
        pick = picks[pl.ds(at, chunk), :]
        block = (
            jnp.dot(pick, source_cols, preferred_element_type=F32)
            * jnp.dot(pick, receiver_cols, preferred_element_type=F32)
        ).astype(BF16)
        oper[pl.ds(at, chunk), :] = block
        return block

    def rs_copy(phase, j, target):
        return to_cell(
            rs_send.at[phase, target], rs_recv.at[phase, j],
            rs_ssem.at[phase, j], rs_rsem.at[phase, j], target,
        )

    def forward(phase, low, after_sends):
        def part(k):
            at = pl.multiple_of(k * chunk, chunk)
            block = build(k) if phase == 0 else oper[pl.ds(at, chunk), :]
            return lax.dot_general(low, block, NT, preferred_element_type=F32)

        def one(j):
            target = cell_peer(j)
            rs_send[phase, target] = part(target).astype(BF16)
            rs_copy(phase, j, target).start()

        each(n_c, one)
        after_sends()
        rs_total = part(c)
        each(n_c, lambda j: rs_copy(phase, j, cell_peer(j)).wait_recv())
        for j in range(1, n_c):
            rs_total = rs_total + rs_recv[phase, j].astype(F32)
        return rs_total * scale

    def ag_copy(phase, j, slot):
        return to_cell(
            ag.at[phase, slot], ag.at[phase, slot],
            ag_ssem.at[phase, j], ag_rsem.at[phase, j], cell_peer(j),
        )

    def gather(phase, value):
        ag[phase, c] = value.astype(BF16)
        each(n_c, lambda j: ag_copy(phase, j, c).start())
        each(n_c, lambda j: ag_copy(phase, j, cell_peer(j)).wait_recv())
        return ag[phase].astype(F32)

    def stat_copy(step, j):
        return to_cell(
            stat_send.at[step], stat_recv.at[step, j],
            st_ssem.at[step, j], st_rsem.at[step, j], cell_peer(j),
        )

    diagonal = lax.broadcasted_iota(jnp.int32, (own, own), 0) == lax.broadcasted_iota(
        jnp.int32, (own, own), 1
    )

    def to_row(column):
        return jnp.sum(jnp.where(diagonal, column, 0.0), axis=0, keepdims=True)

    def to_column(row):
        return jnp.sum(jnp.where(diagonal, row, 0.0), axis=1, keepdims=True)

    def stat_start(step, first, second):
        top = lax.broadcasted_iota(jnp.int32, (8, own), 0) == 0
        stat_send[step] = jnp.where(top, to_row(first), to_row(second))
        each(n_c, lambda j: stat_copy(step, j).start())

    def stat_total(step):
        each(n_c, lambda j: stat_copy(step, j).wait_recv())
        total = stat_send[step]
        for j in range(1, n_c):
            total = total + stat_recv[step, j]
        return to_column(total[0:1]), to_column(total[1:2])

    own_models = models_in[...]
    first_data = forward(0, own_models, lambda: None)
    each(n_s, lambda j: in_copies(j, src_peer(j), (2,))[0].wait_recv())
    own_noise = jnp.concatenate([nz_recv[k].astype(F32) for k in range(n_s)], axis=1)
    chunk_res = -(first_data + own_noise)
    res[...] = gather(0, chunk_res)

    def pair_sum(values):
        return jnp.sum(jnp.sum(values, axis=0), axis=1, keepdims=True)

    alphas = []
    for step in range(HSTEPS):
        last = step == HSTEPS - 1
        full = res[...]
        spread = pair_sum(full * full)
        delta = jnp.sqrt(spread / pairs_all + 1e-06)
        weight = delta[None] / jnp.maximum(jnp.abs(full), delta[None])
        weighted = weight * full
        for k in range(n_c):
            wlow[:, k * chunk : (k + 1) * chunk] = weighted[k].astype(BF16)
        grad = jnp.dot(wlow[...], oper[...], preferred_element_type=F32) * scale
        after = []

        def send_numer():
            grads[step] = grad
            numer_own = jnp.sum(grad * grad, axis=1, keepdims=True)
            after.append(numer_own)
            if last:
                after.append(delta / jnp.maximum(jnp.abs(chunk_res), delta))
            else:
                stat_start(step, numer_own, numer_own)

        image = forward(step + 1, grad.astype(BF16), send_numer)
        if last:
            curve_own = jnp.sum(after[1] * image * image, axis=1, keepdims=True)
            stat_start(step, after[0], curve_own)
            numer, curvature = stat_total(step)
            alpha = numer / (curvature + 1e-06)
        else:
            images = gather(step + 1, image)
            numer, _ = stat_total(step)
            curvature = pair_sum(weight * images * images)
            alpha = numer / (curvature + 1e-06)
            res[...] = full - alpha[None] * images
        chunk_res = chunk_res - alpha * image
        alphas.append(alpha)

    for k in range(n_s):
        fin_send[k] = chunk_res[:, k * share : (k + 1) * share]

    def fin_copy(j, slot):
        return to_src(
            fin_send.at[src_peer(j)], fin_recv.at[slot], fin_ssem.at[j], fin_rsem.at[j], src_peer(j)
        )

    each(n_s, lambda j: fin_copy(j, s).start())
    fin_recv[s] = fin_send[s]
    total_rec = -(alphas[0] * grads[0])
    for step in range(1, HSTEPS):
        total_rec = total_rec - alphas[step] * grads[step]
    rec_out[...] = total_rec

    def in_done(j):
        for copy in in_copies(j, s):
            copy.wait_send()

    each(n_s, in_done)
    for phase in range(HSTEPS + 1):
        each(n_c, lambda j, phase=phase: rs_copy(phase, j, cell_peer(j)).wait_send())
    for phase in range(HSTEPS):
        each(n_c, lambda j, phase=phase: ag_copy(phase, j, c).wait_send())
        each(n_c, lambda j, phase=phase: stat_copy(phase, j).wait_send())
    each(n_s, lambda j: fin_copy(j, src_peer(j)).wait_recv())
    res_out[...] = fin_recv[...].reshape(models_count, share).T
    each(n_s, lambda j: fin_copy(j, s).wait_send())


def split_pair(value, lanes):
    high = value.astype(BF16).astype(F32)
    lane = lax.broadcasted_iota(jnp.int32, value.shape, 1)
    return jnp.where(lane < lanes, high, value - high)


def gathered_body(
    n_s, n_c,
    gs, gr, ps, pr, order, models, noise,
    rec_out, res_out,
    gs_in, gr_in, order_in, models_in, noise_in,
    fields, indices, nz_send, nz_recv, md_send, md_recv,
    gs_all, gr_all, mask, onehot,
    x_send, x_recv, fin_send, fin_recv,
    load, f_ssem, f_rsem, i_ssem, i_rsem, m_ssem, m_rsem, x_ssem, x_rsem, fin_ssem, fin_rsem,
):
    s = lax.axis_index("src")
    c = lax.axis_index("cell")
    pairs = ps.shape[1]
    cells = gs.shape[1]
    s_dev = gs.shape[0]
    r_dev = gr.shape[0]
    own = models.shape[0] // n_s
    mine = own // n_c
    half = cells // 2
    sources = n_s * s_dev
    receivers = n_s * r_dev
    pairs_all = pairs * n_s
    scale = 1.0 / math.sqrt(cells * n_c)

    def src_peer(j):
        return jnp.bitwise_xor(s, j)

    def cell_peer(j):
        return jnp.bitwise_xor(c, j)

    def remote(src_ref, dst_ref, ssem, rsem, ds, dc):
        return pltpu.make_async_remote_copy(
            src_ref=src_ref, dst_ref=dst_ref, send_sem=ssem, recv_sem=rsem,
            device_id={"src": src_peer(ds), "cell": cell_peer(dc)}, device_id_type=MESH,
        )

    barrier = pltpu.get_barrier_semaphore()
    each(n_s, lambda j: pl.semaphore_signal(
        barrier, inc=1, device_id={"src": src_peer(j)}, device_id_type=MESH))
    each(n_c, lambda j: pl.semaphore_signal(
        barrier, inc=1, device_id={"cell": cell_peer(j)}, device_id_type=MESH))

    loads = [
        pltpu.make_async_copy(order, order_in, load.at[0]),
        pltpu.make_async_copy(gs, gs_in, load.at[1]),
        pltpu.make_async_copy(gr, gr_in, load.at[2]),
        pltpu.make_async_copy(ps, indices.at[s, 0], load.at[3]),
        pltpu.make_async_copy(pr, indices.at[s, 1], load.at[4]),
        pltpu.make_async_copy(
            models.at[pl.ds(pl.multiple_of(s * own, own), own), :], models_in, load.at[5]),
        pltpu.make_async_copy(noise, noise_in, load.at[6]),
    ]
    for copy in loads:
        copy.start()
    for copy in loads[:5]:
        copy.wait()
    rows = lax.broadcasted_iota(jnp.int32, (cells, cells), 0)
    select = jnp.where(rows == order_in[...], 1.0, 0.0).astype(BF16)
    raw = jnp.concatenate([gs_in[...].astype(F32), gr_in[...].astype(F32)], axis=0).astype(BF16)
    fields[c, s] = jnp.dot(raw, select, preferred_element_type=F32).astype(BF16)

    pl.semaphore_wait(barrier, n_s + n_c - 2)

    done = []
    count = [0]

    def send_block(t, g, ds, dc):
        at = count[0]
        count[0] += 1
        copy = remote(fields.at[t, g], fields.at[t, g], f_ssem.at[at], f_rsem.at[t, g], ds, dc)
        copy.start()
        done.append(copy.wait_send)

    def got_block(t, g):
        remote(fields.at[t, g], fields.at[t, g], f_ssem.at[0], f_rsem.at[t, g], 0, 1).wait_recv()

    def index_copy(j, slot):
        return remote(indices.at[slot], indices.at[slot], i_ssem.at[0, j], i_rsem.at[0, j], j, 0)

    def noise_copy(j):
        return remote(
            nz_send.at[src_peer(j)], nz_recv.at[s], i_ssem.at[1, j], i_rsem.at[1, j], j, 0)

    def noise_got(j):
        g = src_peer(j)
        remote(nz_send.at[g], nz_recv.at[g], i_ssem.at[1, j], i_rsem.at[1, j], j, 0).wait_recv()

    def model_copy(j):
        return remote(md_send.at[cell_peer(j)], md_recv.at[c], m_ssem.at[j], m_rsem.at[j], 0, j)

    def model_got(j):
        t = cell_peer(j)
        remote(md_send.at[t], md_recv.at[t], m_ssem.at[j], m_rsem.at[j], 0, j).wait_recv()

    steps = range(2, n_c, 2)
    across = n_s - 1
    near = range(1, across)
    send_block(c, s, across, 0)
    for d in steps:
        send_block(c, s, 0, d)
    for j in near:
        send_block(c, s, j, 0)
    send_block(c, s, 0, 1)
    each(n_s, lambda j: index_copy(j, s).start())

    for copy in loads[5:]:
        copy.wait()
    wide = 2 * mine
    q = lax.broadcasted_iota(jnp.int32, (n_c * wide, own), 0)
    m = lax.broadcasted_iota(jnp.int32, (n_c * wide, own), 1)
    spread_rows = jnp.where((q // wide) * mine + q % mine == m, 1.0, 0.0).astype(BF16)
    placed = jnp.dot(spread_rows, models_in[...], preferred_element_type=F32)
    low = lax.broadcasted_iota(jnp.int32, (n_c * wide, half), 0) % wide < mine
    placed = jnp.where(low, placed[:, :half], placed[:, half:])
    md_send[...] = placed.astype(BF16).reshape(n_c, wide, half)
    md_recv[c] = md_send[c]
    each(n_c, lambda j: model_copy(j).start())
    q = lax.broadcasted_iota(jnp.int32, (n_s * wide, models.shape[0]), 0)
    m = lax.broadcasted_iota(jnp.int32, (n_s * wide, models.shape[0]), 1)
    columns = jnp.where(
        ((q // wide) * own + c * mine + q % wide == m) & (q % wide < mine), 1.0, 0.0).astype(BF16)
    nz = lax.dot_general(columns, noise_in[...], NT, preferred_element_type=F32)
    nz_send[...] = nz.astype(BF16).reshape(n_s, wide, pairs)
    nz_recv[s] = nz_send[s]
    each(n_s, lambda j: noise_copy(j).start())

    g = src_peer(across)
    got_block(c, g)
    for d in steps:
        send_block(c, g, 0, d)
    send_block(c, g, 0, 1)
    for d in steps:
        t = cell_peer(d)
        got_block(t, s)
        for j in near:
            send_block(t, s, j, 0)
        send_block(t, s, 0, 1)

    each(n_s, lambda j: index_copy(j, src_peer(j)).wait_recv())
    row = lax.broadcasted_iota(jnp.int32, (2 * receivers, pairs), 0)
    row = jnp.where(row < receivers, row, row - receivers)
    source = lax.broadcasted_iota(jnp.int32, (s_dev, pairs), 0)
    for g in range(n_s):
        mask[g] = jnp.where(source == indices[g, 0], 1.0, 0.0)
        onehot[g] = jnp.where(row == indices[g, 1], 1.0, 0.0).astype(BF16)
    each(n_c, model_got)

    def unpack(t):
        block = fields[t].astype(F32)
        gs_all[t] = block[:, :s_dev].reshape(sources, cells)
        part = block[:, s_dev:].reshape(receivers, cells).astype(BF16)
        gr_all[t] = jnp.concatenate([part, part], axis=0)

    def forward(t, lines):
        base = gs_all[t]
        left = jnp.concatenate([(base * line).astype(BF16) for line in lines], axis=0)
        return lax.dot_general(left, gr_all[t], NT, preferred_element_type=F32)

    data = [None]

    def first(d):
        t = cell_peer(d)
        unpack(t)
        line = md_recv[t].astype(F32)
        lines = [
            jnp.concatenate([line[j : j + 1], line[mine + j : mine + j + 1]], axis=1)
            for j in range(mine)
        ]
        part = forward(t, lines)
        data[0] = part if data[0] is None else data[0] + part

    def own_core(d):
        t = cell_peer(d)
        for j in near if d == 0 else range(1, n_s):
            g = src_peer(j)
            got_block(t, g)
            send_block(t, g, 0, 1)
        first(d)

    def other_core(d):
        t = cell_peer(d + 1)
        for j in range(n_s):
            got_block(t, src_peer(j))
        first(d + 1)

    own_core(0)
    for d in steps:
        own_core(d)
        other_core(d - 2)
    other_core(n_c - 2)

    def to_pairs(value):
        mixed = split_pair(value * scale, receivers).reshape(mine, n_s, s_dev, 2 * receivers)
        out = []
        for g in range(n_s):
            left = mixed[:, g].reshape(mine * s_dev, 2 * receivers).astype(BF16)
            at_pairs = jnp.dot(left, onehot[g], preferred_element_type=F32)
            out.append(at_pairs.reshape(mine, s_dev, pairs) * mask[g][None])
        return out

    def from_pairs(values):
        out = [
            lax.dot_general(
                values[g].reshape(mine * s_dev, pairs).astype(BF16), onehot[g], NT,
                preferred_element_type=F32).reshape(mine, 1, s_dev, 2 * receivers)
            for g in range(n_s)
        ]
        whole = jnp.concatenate(out, axis=1).reshape(mine * sources, 2 * receivers)
        return split_pair(whole * scale, receivers).astype(BF16)

    def pair_sum(values):
        total = values[0]
        for value in values[1:]:
            total = total + value
        return jnp.sum(jnp.sum(total, axis=2, keepdims=True), axis=1, keepdims=True)

    def x_copy(step, j):
        return remote(
            x_send.at[step, cell_peer(j)], x_recv.at[step, c],
            x_ssem.at[step, j], x_rsem.at[step, j], 0, j)

    def x_got(step, j):
        t = cell_peer(j)
        remote(
            x_send.at[step, t], x_recv.at[step, t],
            x_ssem.at[step, j], x_rsem.at[step, j], 0, j).wait_recv()

    each(n_s, noise_got)
    first_data = to_pairs(data[0])
    res = []
    for g in range(n_s):
        line = nz_recv[g].astype(F32)
        lines = jnp.concatenate([line[j : j + 1][None] for j in range(mine)], axis=0)
        res.append(-(first_data[g] + lines * mask[g][None]))

    place = lax.broadcasted_iota(jnp.int32, (wide, half), 0)
    farthest = [d + k for d in range(n_c - 2, -1, -2) for k in (1, 0)]
    alphas = []
    for step in range(HSTEPS):
        delta = jnp.sqrt(pair_sum([value * value for value in res]) / pairs_all + 1e-06)
        weight = [delta / jnp.maximum(jnp.abs(value), delta) for value in res]
        back = from_pairs([w * value for w, value in zip(weight, res)])
        numer = None
        data = None
        for d in farthest:
            t = cell_peer(d)
            fan = jnp.dot(back, gr_all[t], preferred_element_type=F32)
            grad = jnp.sum(
                fan.reshape(mine, sources, cells) * gs_all[t][None], axis=1, keepdims=True)
            square = grad * grad
            numer = square if numer is None else numer + square
            low = grad.astype(BF16).astype(F32)
            part = forward(t, [low[j] for j in range(mine)])
            data = part if data is None else data + part
            packed = jnp.zeros((wide, half), F32)
            for j in range(mine):
                packed = jnp.where(place == j, low[j][:, :half], packed)
                packed = jnp.where(place == mine + j, low[j][:, half:], packed)
            if d == 0:
                x_recv[step, t] = packed.astype(BF16)
            else:
                x_send[step, t] = packed.astype(BF16)
                x_copy(step, d).start()
        image = to_pairs(data)
        curvature = pair_sum([w * value * value for w, value in zip(weight, image)])
        alpha = jnp.sum(numer, axis=2, keepdims=True) / (curvature + 1e-06)
        res = [value - alpha * other for value, other in zip(res, image)]
        alphas.append(alpha)

    odd = c % 2
    two = 2 * (pairs // n_c)
    place = lax.broadcasted_iota(jnp.int32, (wide, pairs), 0)
    lane = lax.broadcasted_iota(jnp.int32, (wide, pairs), 1) % two < two // 2
    marks = jnp.zeros((wide, pairs), F32)
    for j in range(mine):
        marks = jnp.where(
            place == (1 - odd) * mine + j, jnp.where(lane, alphas[0][j], alphas[1][j]), marks)
    for g in range(n_s):
        lines = jnp.sum(res[g], axis=1, keepdims=True)
        note = marks
        for j in range(mine):
            note = jnp.where(place == odd * mine + j, lines[j], note)
        for h in range(n_c // 2):
            fin_send[g, h] = note[:, h * two : (h + 1) * two]

    for b in farthest:
        for a in range(n_s - 1, -1, -1):
            if a + b:
                remote(
                    fin_send.at[src_peer(a), cell_peer(b) // 2], fin_recv.at[s * n_c + c],
                    fin_ssem.at[0], fin_rsem.at[0], a, b).start()
    fin_recv[s * n_c + c] = fin_send[s, c // 2]

    for step in range(HSTEPS):
        each(n_c, lambda j, step=step: x_got(step, j))
    got = x_recv[...].astype(F32).reshape(HSTEPS * n_c // 2, 2, wide, half)
    first_of, second_of = got[:, 0], got[:, 1]

    def turned(value):
        return jnp.concatenate([value[:, mine:], value[:, :mine]], axis=1)

    top = lax.broadcasted_iota(jnp.int32, first_of.shape, 1) < mine
    lower = jnp.where(top, first_of, turned(second_of)).reshape(HSTEPS * own, half)
    upper = jnp.where(top, turned(first_of), second_of).reshape(HSTEPS * own, half)
    grads = jnp.concatenate([lower, upper], axis=1)

    for wait in done:
        wait()
    each(n_s, lambda j: index_copy(j, s).wait_send())
    each(n_c, lambda j: model_copy(j).wait_send())
    each(n_s, lambda j: noise_copy(j).wait_send())
    for step in range(HSTEPS):
        each(n_c, lambda j, step=step: x_copy(step, j).wait_send())

    rest = fin_recv.at[pl.ds(0, n_s * n_c - 1)]
    fin_all = remote(rest, rest, fin_ssem.at[0], fin_rsem.at[0], 0, 1)
    fin_all.wait_recv()
    notes = fin_recv[pl.ds(s * n_c, n_c)].reshape(n_c // 2, 2, wide, two)
    top = lax.broadcasted_iota(jnp.int32, (n_c // 2, wide, two), 1) < mine
    factor = turned(jnp.where(top, notes[:, 1], notes[:, 0])).reshape(own, two)
    rec_out[...] = -(
        factor[:, :1] * grads[:own] + factor[:, two // 2 : two // 2 + 1] * grads[own:])
    notes = fin_recv[...].reshape(n_s * n_c // 2, 2, wide, two)
    top = lax.broadcasted_iota(jnp.int32, (n_s * n_c // 2, wide, two), 1) < mine
    lines = jnp.where(top, notes[:, 0], notes[:, 1]).reshape(n_s * own, two).T
    res_out[...] = jnp.where(odd == 0, lines[: two // 2], lines[two // 2 :])
    fin_all.wait_send()


def gathered_call(n_s, n_c, *arrays):
    gs, gr, ps, _, order, models, noise = arrays
    s_dev, cells = gs.shape
    r_dev = gr.shape[0]
    pairs = ps.shape[1]
    models_count = models.shape[0]
    own = models_count // n_s
    wide = 2 * (own // n_c)
    share = pairs // n_c
    dma = pltpu.SemaphoreType.DMA
    return pl.pallas_call(
        functools.partial(gathered_body, n_s, n_c),
        out_shape=(
            pltpu.VMEM((own, cells), F32),
            pltpu.VMEM((share, models_count), F32),
        ),
        in_specs=[pl.BlockSpec(memory_space=pltpu.HBM)] * 7,
        out_specs=[pl.BlockSpec(memory_space=pltpu.VMEM)] * 2,
        scratch_shapes=[
            pltpu.VMEM((s_dev, cells), BF16),
            pltpu.VMEM((r_dev, cells), BF16),
            pltpu.VMEM((1, cells), jnp.int32),
            pltpu.VMEM((own, cells), BF16),
            pltpu.VMEM((pairs, models_count), BF16),
            pltpu.VMEM((n_c, n_s, s_dev + r_dev, cells), BF16),
            pltpu.VMEM((n_s, 2, 1, pairs), jnp.int32),
            pltpu.VMEM((n_s, wide, pairs), BF16),
            pltpu.VMEM((n_s, wide, pairs), BF16),
            pltpu.VMEM((n_c, wide, cells // 2), BF16),
            pltpu.VMEM((n_c, wide, cells // 2), BF16),
            pltpu.VMEM((n_c, n_s * s_dev, cells), F32),
            pltpu.VMEM((n_c, 2 * n_s * r_dev, cells), BF16),
            pltpu.VMEM((n_s, s_dev, pairs), F32),
            pltpu.VMEM((n_s, 2 * n_s * r_dev, pairs), BF16),
            pltpu.VMEM((HSTEPS, n_c, wide, cells // 2), BF16),
            pltpu.VMEM((HSTEPS, n_c, wide, cells // 2), BF16),
            pltpu.VMEM((n_s, n_c // 2, wide, 2 * share), F32),
            pltpu.VMEM((n_s * n_c, wide, 2 * share), F32),
            dma((7,)), dma((n_s * n_c,)), dma((n_c, n_s)),
            dma((2, n_s)), dma((2, n_s)),
            dma((n_c,)), dma((n_c,)),
            dma((HSTEPS, n_c)), dma((HSTEPS, n_c)),
            dma((1,)), dma((1,)),
        ],
        compiler_params=pltpu.CompilerParams(
            collective_id=0, has_side_effects=True, vmem_limit_bytes=60 * 1024 * 1024
        ),
    )(*arrays)


def fits_gathered(n_s, n_c, s_dev, r_dev, cells, pairs, models_count):
    return (
        n_c & (n_c - 1) == 0 and n_s == 4
        and models_count == 4 * n_s * n_c
        and s_dev == 8 and r_dev % 8 == 0 and 2 * n_s * r_dev == 128
        and pairs == 64 * n_c and cells % 256 == 0
    )


def shards(
    green_source, green_receiver, pair_source, pair_receiver, cell_order, test_models, data_noise
):
    n_s = lax.axis_size("src")
    n_c = lax.axis_size("cell")
    s_dev, cells = green_source.shape
    r_dev = green_receiver.shape[0]
    group_pairs = pair_source.shape[0]
    models_count = test_models.shape[0]
    own = models_count // n_s
    share = group_pairs // n_c
    chunk = share * n_s
    pairs_all = group_pairs * n_s
    arrays = (
        green_source, green_receiver, pair_source[None, :], pair_receiver[None, :],
        cell_order, test_models, data_noise,
    )
    if fits_gathered(n_s, n_c, s_dev, r_dev, cells, group_pairs, models_count):
        return gathered_call(n_s, n_c, *arrays)
    dma = pltpu.SemaphoreType.DMA
    return pl.pallas_call(
        functools.partial(kernel_body, n_s, n_c),
        out_shape=(
            pltpu.VMEM((own, cells), F32),
            pltpu.VMEM((share, models_count), F32),
        ),
        in_specs=[pl.BlockSpec(memory_space=pltpu.HBM)] * 7,
        out_specs=[pl.BlockSpec(memory_space=pltpu.VMEM)] * 2,
        scratch_shapes=[
            pltpu.VMEM((s_dev, cells), BF16),
            pltpu.VMEM((r_dev, cells), BF16),
            pltpu.VMEM((1, cells), jnp.int32),
            pltpu.VMEM((own, cells), BF16),
            pltpu.VMEM((share, models_count), BF16),
            pltpu.VMEM((n_s, s_dev + r_dev, cells), BF16),
            pltpu.VMEM((n_s, 2, 1, group_pairs), jnp.int32),
            pltpu.VMEM((n_s, own, share), BF16),
            pltpu.VMEM((n_s, own, share), BF16),
            pltpu.VMEM((pairs_all, n_s * (s_dev + r_dev)), BF16),
            pltpu.VMEM((pairs_all, cells), BF16),
            pltpu.VMEM((HSTEPS + 1, n_c, own, chunk), BF16),
            pltpu.VMEM((HSTEPS + 1, n_c, own, chunk), BF16),
            pltpu.VMEM((HSTEPS, n_c, own, chunk), BF16),
            pltpu.VMEM((HSTEPS, 8, own), F32),
            pltpu.VMEM((HSTEPS, n_c, 8, own), F32),
            pltpu.VMEM((n_s, own, share), F32),
            pltpu.VMEM((n_s, own, share), F32),
            pltpu.VMEM((own, pairs_all), BF16),
            pltpu.VMEM((n_c, own, chunk), F32),
            pltpu.VMEM((HSTEPS, own, cells), F32),
            dma((7,)), dma((3, n_s)), dma((3, n_s)),
            dma((HSTEPS + 1, n_c)), dma((HSTEPS + 1, n_c)),
            dma((HSTEPS, n_c)), dma((HSTEPS, n_c)),
            dma((HSTEPS, n_c)), dma((HSTEPS, n_c)),
            dma((n_s,)), dma((n_s,)),
        ],
        compiler_params=pltpu.CompilerParams(
            collective_id=0, has_side_effects=True, vmem_limit_bytes=60 * 1024 * 1024
        ),
    )(*arrays)


def solution(mesh):
    return jax.shard_map(
        shards,
        mesh=mesh,
        in_specs=(
            P("src", "cell"),
            P("src", "cell"),
            P("src"),
            P("src"),
            P("cell", None),
            P(None, "cell"),
            P("src", None),
        ),
        out_specs=(P("src", "cell"), P(("src", "cell"), None)),
        check_vma=False,
    )
```

```python
import functools
import math

import jax
import jax.numpy as jnp
from jax import lax
from jax.experimental import pallas as pl
from jax.experimental.pallas import tpu as pltpu
from jax.sharding import PartitionSpec as P

HSTEPS = 2
MESH = pl.DeviceIdType.MESH
F32 = jnp.float32
BF16 = jnp.bfloat16
NT = (((1,), (1,)), ((), ()))


def each(count, body):
    if count <= 8:
        for i in range(count - 1, 0, -1):
            body(i)
    else:

        def step(i, carry):
            body(count - i)
            return carry

        lax.fori_loop(1, count, step, 0)


def kernel_body(
    n_s, n_c,
    gs, gr, ps, pr, order, models, noise,
    rec_out, res_out,
    gs_in, gr_in, order_in, models_in, noise_in,
    fields, indices, nz_send, nz_recv,
    picks, oper, rs_send, rs_recv, ag, stat_send, stat_recv,
    fin_send, fin_recv, wlow, res, grads,
    load, in_send, in_recv, rs_ssem, rs_rsem, ag_ssem, ag_rsem, st_ssem, st_rsem, fin_ssem, fin_rsem,
):
    s = lax.axis_index("src")
    c = lax.axis_index("cell")
    group_pairs = ps.shape[1]
    cells = gs.shape[1]
    models_count = models.shape[0]
    own = models_count // n_s
    share = group_pairs // n_c
    chunk = share * n_s
    pairs_all = group_pairs * n_s
    s_dev = gs.shape[0]
    r_dev = gr.shape[0]
    scale = 1.0 / math.sqrt(cells * n_c)

    def src_peer(j):
        return jnp.bitwise_xor(s, j)

    def cell_peer(j):
        return jnp.bitwise_xor(c, j)

    def to_src(src_ref, dst_ref, ssem, rsem, peer):
        return pltpu.make_async_remote_copy(
            src_ref=src_ref, dst_ref=dst_ref, send_sem=ssem, recv_sem=rsem,
            device_id={"src": peer}, device_id_type=MESH,
        )

    def to_cell(src_ref, dst_ref, ssem, rsem, peer):
        return pltpu.make_async_remote_copy(
            src_ref=src_ref, dst_ref=dst_ref, send_sem=ssem, recv_sem=rsem,
            device_id={"cell": peer}, device_id_type=MESH,
        )

    barrier = pltpu.get_barrier_semaphore()
    each(n_s, lambda j: pl.semaphore_signal(
        barrier, inc=1, device_id={"src": src_peer(j)}, device_id_type=MESH))
    each(n_c, lambda j: pl.semaphore_signal(
        barrier, inc=1, device_id={"cell": cell_peer(j)}, device_id_type=MESH))

    loads = [
        pltpu.make_async_copy(order, order_in, load.at[0]),
        pltpu.make_async_copy(gs, gs_in, load.at[1]),
        pltpu.make_async_copy(gr, gr_in, load.at[2]),
        pltpu.make_async_copy(ps, indices.at[s, 0], load.at[3]),
        pltpu.make_async_copy(pr, indices.at[s, 1], load.at[4]),
        pltpu.make_async_copy(
            noise.at[pl.ds(pl.multiple_of(c * share, share), share), :], noise_in, load.at[5]),
        pltpu.make_async_copy(
            models.at[pl.ds(pl.multiple_of(s * own, own), own), :], models_in, load.at[6]),
    ]
    for copy in loads:
        copy.start()
    for copy in loads:
        copy.wait()
    rows = lax.broadcasted_iota(jnp.int32, (cells, cells), 0)
    select = jnp.where(rows == order_in[...], 1.0, 0.0).astype(BF16)
    raw = jnp.concatenate([gs_in[...].astype(F32), gr_in[...].astype(F32)], axis=0).astype(BF16)
    fields[s] = jnp.dot(raw, select, preferred_element_type=F32).astype(BF16)
    nz_send[...] = noise_in[...].astype(F32).T.reshape(n_s, own, share).astype(BF16)
    nz_recv[s] = nz_send[s]

    pl.semaphore_wait(barrier, n_s + n_c - 2)

    def in_copies(j, slot, which=(0, 1, 2)):
        peer = src_peer(j)
        makers = [
            lambda: to_src(fields.at[slot], fields.at[slot], in_send.at[0, j], in_recv.at[0, j], peer),
            lambda: to_src(indices.at[slot], indices.at[slot], in_send.at[1, j], in_recv.at[1, j], peer),
            lambda: to_src(nz_send.at[peer], nz_recv.at[slot], in_send.at[2, j], in_recv.at[2, j], peer),
        ]
        return [makers[n]() for n in which]

    each(n_s, lambda j: in_copies(j, s, (1,))[0].start())
    each(n_s, lambda j: in_copies(j, s, (0,))[0].start())
    each(n_s, lambda j: in_copies(j, s, (2,))[0].start())

    dev_rows = s_dev + r_dev
    field_rows = n_s * dev_rows
    row = lax.broadcasted_iota(jnp.int32, (field_rows, 1), 0)
    group = jnp.zeros((field_rows, 1), jnp.int32)
    for k in range(1, n_s):
        group = group + jnp.where(row >= k * dev_rows, 1, 0)
    within = row - group * dev_rows
    is_source = within < s_dev
    source_id = jnp.where(is_source, group * s_dev + within, -1)
    receiver_id = jnp.where(is_source, -1, group * r_dev + within - s_dev)

    each(n_s, lambda j: in_copies(j, src_peer(j), (1,))[0].wait_recv())

    for k in range(n_s):
        hit = (source_id == indices[k, 0] + k * s_dev) | (receiver_id == indices[k, 1])
        pick = jnp.where(hit, 1.0, 0.0).T.astype(BF16)
        for t in range(n_c):
            at = t * chunk + k * share
            picks[at : at + share, :] = pick[t * share : (t + 1) * share]
    each(n_s, lambda j: in_copies(j, src_peer(j), (0,))[0].wait_recv())
    every = fields[...].astype(F32).reshape(field_rows, cells)
    source_cols = jnp.where(is_source, every, 0.0).astype(BF16)
    receiver_cols = jnp.where(is_source, 0.0, every).astype(BF16)

    def build(k):
        at = pl.multiple_of(k * chunk, chunk)
        pick = picks[pl.ds(at, chunk), :]
        block = (
            jnp.dot(pick, source_cols, preferred_element_type=F32)
            * jnp.dot(pick, receiver_cols, preferred_element_type=F32)
        ).astype(BF16)
        oper[pl.ds(at, chunk), :] = block
        return block

    def rs_copy(phase, j, target):
        return to_cell(
            rs_send.at[phase, target], rs_recv.at[phase, j],
            rs_ssem.at[phase, j], rs_rsem.at[phase, j], target,
        )

    def forward(phase, low, after_sends):
        def part(k):
            at = pl.multiple_of(k * chunk, chunk)
            block = build(k) if phase == 0 else oper[pl.ds(at, chunk), :]
            return lax.dot_general(low, block, NT, preferred_element_type=F32)

        def one(j):
            target = cell_peer(j)
            rs_send[phase, target] = part(target).astype(BF16)
            rs_copy(phase, j, target).start()

        each(n_c, one)
        after_sends()
        rs_total = part(c)
        each(n_c, lambda j: rs_copy(phase, j, cell_peer(j)).wait_recv())
        for j in range(1, n_c):
            rs_total = rs_total + rs_recv[phase, j].astype(F32)
        return rs_total * scale

    def ag_copy(phase, j, slot):
        return to_cell(
            ag.at[phase, slot], ag.at[phase, slot],
            ag_ssem.at[phase, j], ag_rsem.at[phase, j], cell_peer(j),
        )

    def gather(phase, value):
        ag[phase, c] = value.astype(BF16)
        each(n_c, lambda j: ag_copy(phase, j, c).start())
        each(n_c, lambda j: ag_copy(phase, j, cell_peer(j)).wait_recv())
        return ag[phase].astype(F32)

    def stat_copy(step, j):
        return to_cell(
            stat_send.at[step], stat_recv.at[step, j],
            st_ssem.at[step, j], st_rsem.at[step, j], cell_peer(j),
        )

    diagonal = lax.broadcasted_iota(jnp.int32, (own, own), 0) == lax.broadcasted_iota(
        jnp.int32, (own, own), 1
    )

    def to_row(column):
        return jnp.sum(jnp.where(diagonal, column, 0.0), axis=0, keepdims=True)

    def to_column(row):
        return jnp.sum(jnp.where(diagonal, row, 0.0), axis=1, keepdims=True)

    def stat_start(step, first, second):
        top = lax.broadcasted_iota(jnp.int32, (8, own), 0) == 0
        stat_send[step] = jnp.where(top, to_row(first), to_row(second))
        each(n_c, lambda j: stat_copy(step, j).start())

    def stat_total(step):
        each(n_c, lambda j: stat_copy(step, j).wait_recv())
        total = stat_send[step]
        for j in range(1, n_c):
            total = total + stat_recv[step, j]
        return to_column(total[0:1]), to_column(total[1:2])

    own_models = models_in[...]
    first_data = forward(0, own_models, lambda: None)
    each(n_s, lambda j: in_copies(j, src_peer(j), (2,))[0].wait_recv())
    own_noise = jnp.concatenate([nz_recv[k].astype(F32) for k in range(n_s)], axis=1)
    chunk_res = -(first_data + own_noise)
    res[...] = gather(0, chunk_res)

    def pair_sum(values):
        return jnp.sum(jnp.sum(values, axis=0), axis=1, keepdims=True)

    alphas = []
    for step in range(HSTEPS):
        last = step == HSTEPS - 1
        full = res[...]
        spread = pair_sum(full * full)
        delta = jnp.sqrt(spread / pairs_all + 1e-06)
        weight = delta[None] / jnp.maximum(jnp.abs(full), delta[None])
        weighted = weight * full
        for k in range(n_c):
            wlow[:, k * chunk : (k + 1) * chunk] = weighted[k].astype(BF16)
        grad = jnp.dot(wlow[...], oper[...], preferred_element_type=F32) * scale
        after = []

        def send_numer():
            grads[step] = grad
            numer_own = jnp.sum(grad * grad, axis=1, keepdims=True)
            after.append(numer_own)
            if last:
                after.append(delta / jnp.maximum(jnp.abs(chunk_res), delta))
            else:
                stat_start(step, numer_own, numer_own)

        image = forward(step + 1, grad.astype(BF16), send_numer)
        if last:
            curve_own = jnp.sum(after[1] * image * image, axis=1, keepdims=True)
            stat_start(step, after[0], curve_own)
            numer, curvature = stat_total(step)
            alpha = numer / (curvature + 1e-06)
        else:
            images = gather(step + 1, image)
            numer, _ = stat_total(step)
            curvature = pair_sum(weight * images * images)
            alpha = numer / (curvature + 1e-06)
            res[...] = full - alpha[None] * images
        chunk_res = chunk_res - alpha * image
        alphas.append(alpha)

    for k in range(n_s):
        fin_send[k] = chunk_res[:, k * share : (k + 1) * share]

    def fin_copy(j, slot):
        return to_src(
            fin_send.at[src_peer(j)], fin_recv.at[slot], fin_ssem.at[j], fin_rsem.at[j], src_peer(j)
        )

    each(n_s, lambda j: fin_copy(j, s).start())
    fin_recv[s] = fin_send[s]
    total_rec = -(alphas[0] * grads[0])
    for step in range(1, HSTEPS):
        total_rec = total_rec - alphas[step] * grads[step]
    rec_out[...] = total_rec

    def in_done(j):
        for copy in in_copies(j, s):
            copy.wait_send()

    each(n_s, in_done)
    for phase in range(HSTEPS + 1):
        each(n_c, lambda j, phase=phase: rs_copy(phase, j, cell_peer(j)).wait_send())
    for phase in range(HSTEPS):
        each(n_c, lambda j, phase=phase: ag_copy(phase, j, c).wait_send())
        each(n_c, lambda j, phase=phase: stat_copy(phase, j).wait_send())
    each(n_s, lambda j: fin_copy(j, src_peer(j)).wait_recv())
    res_out[...] = fin_recv[...].reshape(models_count, share).T
    each(n_s, lambda j: fin_copy(j, s).wait_send())


def split_pair(value, lanes):
    high = value.astype(BF16).astype(F32)
    lane = lax.broadcasted_iota(jnp.int32, value.shape, 1)
    return jnp.where(lane < lanes, high, value - high)


def gathered_body(
    n_s, n_c,
    gs, gr, ps, pr, order, models, noise,
    rec_out, res_out,
    gs_in, gr_in, order_in, models_in, noise_in,
    fields, indices, nz_send, nz_recv, md_send, md_recv,
    gs_all, gr_all, mask, onehot,
    x_send, x_recv, fin_send, fin_recv,
    load, f_ssem, f_rsem, i_ssem, i_rsem, m_ssem, m_rsem, x_ssem, x_rsem, fin_ssem, fin_rsem,
):
    s = lax.axis_index("src")
    c = lax.axis_index("cell")
    pairs = ps.shape[1]
    cells = gs.shape[1]
    s_dev = gs.shape[0]
    r_dev = gr.shape[0]
    own = models.shape[0] // n_s
    mine = own // n_c
    half = cells // 2
    sources = n_s * s_dev
    receivers = n_s * r_dev
    pairs_all = pairs * n_s
    scale = 1.0 / math.sqrt(cells * n_c)

    def src_peer(j):
        return jnp.bitwise_xor(s, j)

    def cell_peer(j):
        return jnp.bitwise_xor(c, j)

    def remote(src_ref, dst_ref, ssem, rsem, ds, dc):
        return pltpu.make_async_remote_copy(
            src_ref=src_ref, dst_ref=dst_ref, send_sem=ssem, recv_sem=rsem,
            device_id={"src": src_peer(ds), "cell": cell_peer(dc)}, device_id_type=MESH,
        )

    barrier = pltpu.get_barrier_semaphore()
    each(n_s, lambda j: pl.semaphore_signal(
        barrier, inc=1, device_id={"src": src_peer(j)}, device_id_type=MESH))
    each(n_c, lambda j: pl.semaphore_signal(
        barrier, inc=1, device_id={"cell": cell_peer(j)}, device_id_type=MESH))

    loads = [
        pltpu.make_async_copy(order, order_in, load.at[0]),
        pltpu.make_async_copy(gs, gs_in, load.at[1]),
        pltpu.make_async_copy(gr, gr_in, load.at[2]),
        pltpu.make_async_copy(ps, indices.at[s, 0], load.at[3]),
        pltpu.make_async_copy(pr, indices.at[s, 1], load.at[4]),
        pltpu.make_async_copy(
            models.at[pl.ds(pl.multiple_of(s * own, own), own), :], models_in, load.at[5]),
        pltpu.make_async_copy(noise, noise_in, load.at[6]),
    ]
    for copy in loads:
        copy.start()
    for copy in loads[:5]:
        copy.wait()
    rows = lax.broadcasted_iota(jnp.int32, (cells, cells), 0)
    select = jnp.where(rows == order_in[...], 1.0, 0.0).astype(BF16)
    raw = jnp.concatenate([gs_in[...].astype(F32), gr_in[...].astype(F32)], axis=0).astype(BF16)
    fields[c, s] = jnp.dot(raw, select, preferred_element_type=F32).astype(BF16)

    for copy in loads[5:]:
        copy.wait()
    wide = 2 * mine
    q = lax.broadcasted_iota(jnp.int32, (n_c * wide, own), 0)
    m = lax.broadcasted_iota(jnp.int32, (n_c * wide, own), 1)
    spread_rows = jnp.where((q % mine) * n_c + q // wide == m, 1.0, 0.0).astype(BF16)
    placed = jnp.dot(spread_rows, models_in[...], preferred_element_type=F32)
    low = lax.broadcasted_iota(jnp.int32, (n_c * wide, half), 0) % wide < mine
    placed = jnp.where(low, placed[:, :half], placed[:, half:])
    md_send[...] = placed.astype(BF16).reshape(n_c, wide, half)
    md_recv[c] = md_send[c]
    q = lax.broadcasted_iota(jnp.int32, (n_s * wide, models.shape[0]), 0)
    m = lax.broadcasted_iota(jnp.int32, (n_s * wide, models.shape[0]), 1)
    columns = jnp.where(
        ((q // wide) * own + (q % wide) * n_c + c == m) & (q % wide < mine), 1.0, 0.0).astype(BF16)
    nz = lax.dot_general(columns, noise_in[...], NT, preferred_element_type=F32)
    nz_send[...] = nz.astype(BF16).reshape(n_s, wide, pairs)
    nz_recv[s] = nz_send[s]

    pl.semaphore_wait(barrier, n_s + n_c - 2)

    done = []
    count = [0]

    def send_block(t, g, ds, dc):
        at = count[0]
        count[0] += 1
        copy = remote(fields.at[t, g], fields.at[t, g], f_ssem.at[at], f_rsem.at[t, g], ds, dc)
        copy.start()
        done.append(copy.wait_send)

    def got_block(t, g):
        remote(fields.at[t, g], fields.at[t, g], f_ssem.at[0], f_rsem.at[t, g], 0, 1).wait_recv()

    def index_copy(j, slot):
        return remote(indices.at[slot], indices.at[slot], i_ssem.at[0, j], i_rsem.at[0, j], j, 0)

    def noise_copy(j):
        return remote(
            nz_send.at[src_peer(j)], nz_recv.at[s], i_ssem.at[1, j], i_rsem.at[1, j], j, 0)

    def noise_got(j):
        g = src_peer(j)
        remote(nz_send.at[g], nz_recv.at[g], i_ssem.at[1, j], i_rsem.at[1, j], j, 0).wait_recv()

    def model_copy(j):
        return remote(md_send.at[cell_peer(j)], md_recv.at[c], m_ssem.at[j], m_rsem.at[j], 0, j)

    def model_got(j):
        t = cell_peer(j)
        remote(md_send.at[t], md_recv.at[t], m_ssem.at[j], m_rsem.at[j], 0, j).wait_recv()

    steps = range(2, n_c, 2)
    across = n_s - 1
    near = range(1, across)
    send_block(c, s, across, 0)
    for d in steps:
        send_block(c, s, 0, d)
    for j in near:
        send_block(c, s, j, 0)
    send_block(c, s, 0, 1)
    each(n_s, lambda j: index_copy(j, s).start())

    each(n_c, lambda j: model_copy(j).start())
    each(n_s, lambda j: noise_copy(j).start())

    g = src_peer(across)
    got_block(c, g)
    for d in steps:
        send_block(c, g, 0, d)
    send_block(c, g, 0, 1)
    for d in steps:
        t = cell_peer(d)
        got_block(t, s)
        for j in near:
            send_block(t, s, j, 0)
        send_block(t, s, 0, 1)

    each(n_s, lambda j: index_copy(j, src_peer(j)).wait_recv())
    row = lax.broadcasted_iota(jnp.int32, (2 * receivers, pairs), 0)
    row = jnp.where(row < receivers, row, row - receivers)
    source = lax.broadcasted_iota(jnp.int32, (s_dev, pairs), 0)
    for g in range(n_s):
        mask[g] = jnp.where(source == indices[g, 0], 1.0, 0.0)
        onehot[g] = jnp.where(row == indices[g, 1], 1.0, 0.0).astype(BF16)

    def unpack(t):
        block = fields[t].astype(F32)
        gs_all[t] = block[:, :s_dev].reshape(sources, cells)
        part = block[:, s_dev:].reshape(receivers, cells).astype(BF16)
        gr_all[t] = jnp.concatenate([part, part], axis=0)

    def forward(t, lines):
        base = gs_all[t]
        left = jnp.concatenate([(base * line).astype(BF16) for line in lines], axis=0)
        return lax.dot_general(left, gr_all[t], NT, preferred_element_type=F32)

    data = [None]

    def first(d):
        t = cell_peer(d)
        unpack(t)
        if d:
            model_got(d)
        line = md_recv[t].astype(F32)
        lines = [
            jnp.concatenate([line[j : j + 1], line[mine + j : mine + j + 1]], axis=1)
            for j in range(mine)
        ]
        part = forward(t, lines)
        data[0] = part if data[0] is None else data[0] + part

    def own_core(d):
        t = cell_peer(d)
        for j in near if d == 0 else range(1, n_s):
            g = src_peer(j)
            got_block(t, g)
            send_block(t, g, 0, 1)
        first(d)

    def other_core(d):
        t = cell_peer(d + 1)
        for j in range(n_s):
            got_block(t, src_peer(j))
        first(d + 1)

    own_core(0)
    for d in steps:
        own_core(d)
        other_core(d - 2)
    other_core(n_c - 2)

    def to_pairs(value):
        mixed = split_pair(value * scale, receivers).reshape(mine, n_s, s_dev, 2 * receivers)
        out = []
        for g in range(n_s):
            left = mixed[:, g].reshape(mine * s_dev, 2 * receivers).astype(BF16)
            at_pairs = jnp.dot(left, onehot[g], preferred_element_type=F32)
            out.append(at_pairs.reshape(mine, s_dev, pairs) * mask[g][None])
        return out

    def from_pairs(values):
        out = [
            lax.dot_general(
                values[g].reshape(mine * s_dev, pairs).astype(BF16), onehot[g], NT,
                preferred_element_type=F32).reshape(mine, 1, s_dev, 2 * receivers)
            for g in range(n_s)
        ]
        whole = jnp.concatenate(out, axis=1).reshape(mine * sources, 2 * receivers)
        return split_pair(whole * scale, receivers).astype(BF16)

    def pair_sum(values):
        total = values[0]
        for value in values[1:]:
            total = total + value
        return jnp.sum(jnp.sum(total, axis=2, keepdims=True), axis=1, keepdims=True)

    def x_copy(step, j):
        return remote(
            x_send.at[step, cell_peer(j)], x_recv.at[step, c],
            x_ssem.at[step, j], x_rsem.at[step, j], 0, j)

    def x_got(step, j):
        t = cell_peer(j)
        remote(
            x_send.at[step, t], x_recv.at[step, t],
            x_ssem.at[step, j], x_rsem.at[step, j], 0, j).wait_recv()

    each(n_s, noise_got)
    first_data = to_pairs(data[0])
    res = []
    for g in range(n_s):
        line = nz_recv[g].astype(F32)
        lines = jnp.concatenate([line[j : j + 1][None] for j in range(mine)], axis=0)
        res.append(-(first_data[g] + lines * mask[g][None]))

    place = lax.broadcasted_iota(jnp.int32, (wide, half), 0)
    farthest = [d + k for d in range(n_c - 2, -1, -2) for k in (1, 0)]
    alphas = []
    for step in range(HSTEPS):
        delta = jnp.sqrt(pair_sum([value * value for value in res]) / pairs_all + 1e-06)
        weight = [delta / jnp.maximum(jnp.abs(value), delta) for value in res]
        back = from_pairs([w * value for w, value in zip(weight, res)])
        numer = None
        data = None
        for d in farthest:
            t = cell_peer(d)
            fan = jnp.dot(back, gr_all[t], preferred_element_type=F32)
            grad = jnp.sum(
                fan.reshape(mine, sources, cells) * gs_all[t][None], axis=1, keepdims=True)
            square = grad * grad
            numer = square if numer is None else numer + square
            low = grad.astype(BF16).astype(F32)
            part = forward(t, [low[j] for j in range(mine)])
            data = part if data is None else data + part
            packed = jnp.zeros((wide, half), F32)
            for j in range(mine):
                packed = jnp.where(place == j, low[j][:, :half], packed)
                packed = jnp.where(place == mine + j, low[j][:, half:], packed)
            x_send[step, t] = packed.astype(BF16)
        x_recv[step, c] = x_send[step, c]
        image = to_pairs(data)
        curvature = pair_sum([w * value * value for w, value in zip(weight, image)])
        alpha = jnp.sum(numer, axis=2, keepdims=True) / (curvature + 1e-06)
        res = [value - alpha * other for value, other in zip(res, image)]
        alphas.append(alpha)
        if step < HSTEPS - 1:
            for d in farthest:
                if d:
                    x_copy(step, d).start()

    odd = c % 2
    two = 2 * (pairs // n_c)
    room = two // (2 * mine)
    lane = lax.broadcasted_iota(jnp.int32, (1, two), 1)
    marks = jnp.zeros((1, two), F32)
    for j in range(mine):
        for step in range(HSTEPS):
            marks = jnp.where(lane // room == 2 * j + step, alphas[step][j], marks)
    for g in range(n_s):
        lines = jnp.sum(res[g], axis=1, keepdims=True)
        for h in range(n_c // 2):
            fin_send[g, h] = jnp.concatenate(
                [lines[j][:, h * two : (h + 1) * two] for j in range(mine)] + [marks], axis=1)

    others = n_s * n_c

    def fin_start(i, carry):
        a, b = (others - i) // n_c, (others - i) % n_c
        remote(
            fin_send.at[src_peer(a), cell_peer(b) // 2], fin_recv.at[s * n_c + c],
            fin_ssem.at[0], fin_rsem.at[0], a, b).start()
        return carry

    lax.fori_loop(1, others, fin_start, 0)
    for d in farthest:
        if d:
            x_copy(HSTEPS - 1, d).start()
    fin_recv[s * n_c + c] = fin_send[s, c // 2]

    m = lax.broadcasted_iota(jnp.int32, (own, n_c * wide), 0)
    q = lax.broadcasted_iota(jnp.int32, (own, n_c * wide), 1)
    at = (m % n_c) * wide + m // n_c
    rows_of = [jnp.where(q == at + k * mine, 1.0, 0.0).astype(BF16) for k in (0, 1)]
    grads = []
    for step in range(HSTEPS):
        for j in range(n_c - 1, 0, -1):
            x_got(step, j)
        blocks = x_recv[step].astype(F32).reshape(n_c * wide, half).astype(BF16)
        grads.append(jnp.concatenate(
            [jnp.dot(pick, blocks, preferred_element_type=F32) for pick in rows_of], axis=1))

    for wait in done:
        wait()
    each(n_s, lambda j: index_copy(j, s).wait_send())
    each(n_c, lambda j: model_copy(j).wait_send())
    each(n_s, lambda j: noise_copy(j).wait_send())
    for step in range(HSTEPS):
        each(n_c, lambda j, step=step: x_copy(step, j).wait_send())

    rest = fin_recv.at[pl.ds(0, n_s * n_c - 1)]
    fin_all = remote(rest, rest, fin_ssem.at[0], fin_rsem.at[0], 0, 1)
    fin_all.wait_recv()
    notes = fin_recv[pl.ds(s * n_c, n_c), 0, mine * two :]
    for j in range(mine):
        at = pl.ds(j * n_c, n_c)
        here = slice(j * n_c, (j + 1) * n_c)
        first_of, second_of = (
            notes[:, (2 * j + step) * room : (2 * j + step) * room + 1] for step in range(HSTEPS))
        rec_out[at, :] = -(first_of * grads[0][here] + second_of * grads[1][here])
    lines = jnp.concatenate(
        [
            fin_recv[:, 0, j * two : (j + 1) * two].reshape(n_s, 1, n_c, two)
            for j in range(mine)
        ], axis=1).reshape(n_s * own, two).T
    res_out[...] = jnp.where(odd == 0, lines[: two // 2], lines[two // 2 :])
    fin_all.wait_send()


def gathered_call(n_s, n_c, *arrays):
    gs, gr, ps, _, order, models, noise = arrays
    s_dev, cells = gs.shape
    r_dev = gr.shape[0]
    pairs = ps.shape[1]
    models_count = models.shape[0]
    own = models_count // n_s
    wide = 2 * (own // n_c)
    share = pairs // n_c
    dma = pltpu.SemaphoreType.DMA
    return pl.pallas_call(
        functools.partial(gathered_body, n_s, n_c),
        out_shape=(
            pltpu.VMEM((own, cells), F32),
            pltpu.VMEM((share, models_count), F32),
        ),
        in_specs=[pl.BlockSpec(memory_space=pltpu.HBM)] * 7,
        out_specs=[pl.BlockSpec(memory_space=pltpu.VMEM)] * 2,
        scratch_shapes=[
            pltpu.VMEM((s_dev, cells), BF16),
            pltpu.VMEM((r_dev, cells), BF16),
            pltpu.VMEM((1, cells), jnp.int32),
            pltpu.VMEM((own, cells), BF16),
            pltpu.VMEM((pairs, models_count), BF16),
            pltpu.VMEM((n_c, n_s, s_dev + r_dev, cells), BF16),
            pltpu.VMEM((n_s, 2, 1, pairs), jnp.int32),
            pltpu.VMEM((n_s, wide, pairs), BF16),
            pltpu.VMEM((n_s, wide, pairs), BF16),
            pltpu.VMEM((n_c, wide, cells // 2), BF16),
            pltpu.VMEM((n_c, wide, cells // 2), BF16),
            pltpu.VMEM((n_c, n_s * s_dev, cells), F32),
            pltpu.VMEM((n_c, 2 * n_s * r_dev, cells), BF16),
            pltpu.VMEM((n_s, s_dev, pairs), F32),
            pltpu.VMEM((n_s, 2 * n_s * r_dev, pairs), BF16),
            pltpu.VMEM((HSTEPS, n_c, wide, cells // 2), BF16),
            pltpu.VMEM((HSTEPS, n_c, wide, cells // 2), BF16),
            pltpu.VMEM((n_s, n_c // 2, 1, (wide // 2 + 1) * 2 * share), F32),
            pltpu.VMEM((n_s * n_c, 1, (wide // 2 + 1) * 2 * share), F32),
            dma((7,)), dma((n_s * n_c,)), dma((n_c, n_s)),
            dma((2, n_s)), dma((2, n_s)),
            dma((n_c,)), dma((n_c,)),
            dma((HSTEPS, n_c)), dma((HSTEPS, n_c)),
            dma((1,)), dma((1,)),
        ],
        compiler_params=pltpu.CompilerParams(
            collective_id=0, has_side_effects=True, vmem_limit_bytes=60 * 1024 * 1024
        ),
    )(*arrays)


def fits_gathered(n_s, n_c, s_dev, r_dev, cells, pairs, models_count):
    return (
        n_c & (n_c - 1) == 0 and n_s == 4
        and models_count == 4 * n_s * n_c
        and s_dev == 8 and r_dev % 8 == 0 and 2 * n_s * r_dev == 128
        and pairs == 64 * n_c and cells % 256 == 0
    )


def shards(
    green_source, green_receiver, pair_source, pair_receiver, cell_order, test_models, data_noise
):
    n_s = lax.axis_size("src")
    n_c = lax.axis_size("cell")
    s_dev, cells = green_source.shape
    r_dev = green_receiver.shape[0]
    group_pairs = pair_source.shape[0]
    models_count = test_models.shape[0]
    own = models_count // n_s
    share = group_pairs // n_c
    chunk = share * n_s
    pairs_all = group_pairs * n_s
    arrays = (
        green_source, green_receiver, pair_source[None, :], pair_receiver[None, :],
        cell_order, test_models, data_noise,
    )
    if fits_gathered(n_s, n_c, s_dev, r_dev, cells, group_pairs, models_count):
        return gathered_call(n_s, n_c, *arrays)
    dma = pltpu.SemaphoreType.DMA
    return pl.pallas_call(
        functools.partial(kernel_body, n_s, n_c),
        out_shape=(
            pltpu.VMEM((own, cells), F32),
            pltpu.VMEM((share, models_count), F32),
        ),
        in_specs=[pl.BlockSpec(memory_space=pltpu.HBM)] * 7,
        out_specs=[pl.BlockSpec(memory_space=pltpu.VMEM)] * 2,
        scratch_shapes=[
            pltpu.VMEM((s_dev, cells), BF16),
            pltpu.VMEM((r_dev, cells), BF16),
            pltpu.VMEM((1, cells), jnp.int32),
            pltpu.VMEM((own, cells), BF16),
            pltpu.VMEM((share, models_count), BF16),
            pltpu.VMEM((n_s, s_dev + r_dev, cells), BF16),
            pltpu.VMEM((n_s, 2, 1, group_pairs), jnp.int32),
            pltpu.VMEM((n_s, own, share), BF16),
            pltpu.VMEM((n_s, own, share), BF16),
            pltpu.VMEM((pairs_all, n_s * (s_dev + r_dev)), BF16),
            pltpu.VMEM((pairs_all, cells), BF16),
            pltpu.VMEM((HSTEPS + 1, n_c, own, chunk), BF16),
            pltpu.VMEM((HSTEPS + 1, n_c, own, chunk), BF16),
            pltpu.VMEM((HSTEPS, n_c, own, chunk), BF16),
            pltpu.VMEM((HSTEPS, 8, own), F32),
            pltpu.VMEM((HSTEPS, n_c, 8, own), F32),
            pltpu.VMEM((n_s, own, share), F32),
            pltpu.VMEM((n_s, own, share), F32),
            pltpu.VMEM((own, pairs_all), BF16),
            pltpu.VMEM((n_c, own, chunk), F32),
            pltpu.VMEM((HSTEPS, own, cells), F32),
            dma((7,)), dma((3, n_s)), dma((3, n_s)),
            dma((HSTEPS + 1, n_c)), dma((HSTEPS + 1, n_c)),
            dma((HSTEPS, n_c)), dma((HSTEPS, n_c)),
            dma((HSTEPS, n_c)), dma((HSTEPS, n_c)),
            dma((n_s,)), dma((n_s,)),
        ],
        compiler_params=pltpu.CompilerParams(
            collective_id=0, has_side_effects=True, vmem_limit_bytes=60 * 1024 * 1024
        ),
    )(*arrays)


def solution(mesh):
    return jax.shard_map(
        shards,
        mesh=mesh,
        in_specs=(
            P("src", "cell"),
            P("src", "cell"),
            P("src"),
            P("src"),
            P("cell", None),
            P(None, "cell"),
            P("src", None),
        ),
        out_specs=(P("src", "cell"), P(("src", "cell"), None)),
        check_vma=False,
    )
```

```python
import functools
import math

import jax
import jax.numpy as jnp
from jax import lax
from jax.experimental import pallas as pl
from jax.experimental.pallas import tpu as pltpu
from jax.sharding import PartitionSpec as P

HSTEPS = 2
MESH = pl.DeviceIdType.MESH
F32 = jnp.float32
BF16 = jnp.bfloat16
NT = (((1,), (1,)), ((), ()))


def each(count, body):
    if count <= 8:
        for i in range(count - 1, 0, -1):
            body(i)
    else:

        def step(i, carry):
            body(count - i)
            return carry

        lax.fori_loop(1, count, step, 0)


def kernel_body(
    n_s, n_c,
    gs, gr, ps, pr, order, models, noise,
    rec_out, res_out,
    gs_in, gr_in, order_in, models_in, noise_in,
    fields, indices, nz_send, nz_recv,
    picks, oper, rs_send, rs_recv, ag, stat_send, stat_recv,
    fin_send, fin_recv, wlow, res, grads,
    load, in_send, in_recv, rs_ssem, rs_rsem, ag_ssem, ag_rsem, st_ssem, st_rsem, fin_ssem, fin_rsem,
):
    s = lax.axis_index("src")
    c = lax.axis_index("cell")
    group_pairs = ps.shape[1]
    cells = gs.shape[1]
    models_count = models.shape[0]
    own = models_count // n_s
    share = group_pairs // n_c
    chunk = share * n_s
    pairs_all = group_pairs * n_s
    s_dev = gs.shape[0]
    r_dev = gr.shape[0]
    scale = 1.0 / math.sqrt(cells * n_c)

    def src_peer(j):
        return jnp.bitwise_xor(s, j)

    def cell_peer(j):
        return jnp.bitwise_xor(c, j)

    def to_src(src_ref, dst_ref, ssem, rsem, peer):
        return pltpu.make_async_remote_copy(
            src_ref=src_ref, dst_ref=dst_ref, send_sem=ssem, recv_sem=rsem,
            device_id={"src": peer}, device_id_type=MESH,
        )

    def to_cell(src_ref, dst_ref, ssem, rsem, peer):
        return pltpu.make_async_remote_copy(
            src_ref=src_ref, dst_ref=dst_ref, send_sem=ssem, recv_sem=rsem,
            device_id={"cell": peer}, device_id_type=MESH,
        )

    barrier = pltpu.get_barrier_semaphore()
    each(n_s, lambda j: pl.semaphore_signal(
        barrier, inc=1, device_id={"src": src_peer(j)}, device_id_type=MESH))
    each(n_c, lambda j: pl.semaphore_signal(
        barrier, inc=1, device_id={"cell": cell_peer(j)}, device_id_type=MESH))

    loads = [
        pltpu.make_async_copy(order, order_in, load.at[0]),
        pltpu.make_async_copy(gs, gs_in, load.at[1]),
        pltpu.make_async_copy(gr, gr_in, load.at[2]),
        pltpu.make_async_copy(ps, indices.at[s, 0], load.at[3]),
        pltpu.make_async_copy(pr, indices.at[s, 1], load.at[4]),
        pltpu.make_async_copy(
            noise.at[pl.ds(pl.multiple_of(c * share, share), share), :], noise_in, load.at[5]),
        pltpu.make_async_copy(
            models.at[pl.ds(pl.multiple_of(s * own, own), own), :], models_in, load.at[6]),
    ]
    for copy in loads:
        copy.start()
    for copy in loads:
        copy.wait()
    rows = lax.broadcasted_iota(jnp.int32, (cells, cells), 0)
    select = jnp.where(rows == order_in[...], 1.0, 0.0).astype(BF16)
    raw = jnp.concatenate([gs_in[...].astype(F32), gr_in[...].astype(F32)], axis=0).astype(BF16)
    fields[s] = jnp.dot(raw, select, preferred_element_type=F32).astype(BF16)
    nz_send[...] = noise_in[...].astype(F32).T.reshape(n_s, own, share).astype(BF16)
    nz_recv[s] = nz_send[s]

    pl.semaphore_wait(barrier, n_s + n_c - 2)

    def in_copies(j, slot, which=(0, 1, 2)):
        peer = src_peer(j)
        makers = [
            lambda: to_src(fields.at[slot], fields.at[slot], in_send.at[0, j], in_recv.at[0, j], peer),
            lambda: to_src(indices.at[slot], indices.at[slot], in_send.at[1, j], in_recv.at[1, j], peer),
            lambda: to_src(nz_send.at[peer], nz_recv.at[slot], in_send.at[2, j], in_recv.at[2, j], peer),
        ]
        return [makers[n]() for n in which]

    each(n_s, lambda j: in_copies(j, s, (1,))[0].start())
    each(n_s, lambda j: in_copies(j, s, (0,))[0].start())
    each(n_s, lambda j: in_copies(j, s, (2,))[0].start())

    dev_rows = s_dev + r_dev
    field_rows = n_s * dev_rows
    row = lax.broadcasted_iota(jnp.int32, (field_rows, 1), 0)
    group = jnp.zeros((field_rows, 1), jnp.int32)
    for k in range(1, n_s):
        group = group + jnp.where(row >= k * dev_rows, 1, 0)
    within = row - group * dev_rows
    is_source = within < s_dev
    source_id = jnp.where(is_source, group * s_dev + within, -1)
    receiver_id = jnp.where(is_source, -1, group * r_dev + within - s_dev)

    each(n_s, lambda j: in_copies(j, src_peer(j), (1,))[0].wait_recv())

    for k in range(n_s):
        hit = (source_id == indices[k, 0] + k * s_dev) | (receiver_id == indices[k, 1])
        pick = jnp.where(hit, 1.0, 0.0).T.astype(BF16)
        for t in range(n_c):
            at = t * chunk + k * share
            picks[at : at + share, :] = pick[t * share : (t + 1) * share]
    each(n_s, lambda j: in_copies(j, src_peer(j), (0,))[0].wait_recv())
    every = fields[...].astype(F32).reshape(field_rows, cells)
    source_cols = jnp.where(is_source, every, 0.0).astype(BF16)
    receiver_cols = jnp.where(is_source, 0.0, every).astype(BF16)

    def build(k):
        at = pl.multiple_of(k * chunk, chunk)
        pick = picks[pl.ds(at, chunk), :]
        block = (
            jnp.dot(pick, source_cols, preferred_element_type=F32)
            * jnp.dot(pick, receiver_cols, preferred_element_type=F32)
        ).astype(BF16)
        oper[pl.ds(at, chunk), :] = block
        return block

    def rs_copy(phase, j, target):
        return to_cell(
            rs_send.at[phase, target], rs_recv.at[phase, j],
            rs_ssem.at[phase, j], rs_rsem.at[phase, j], target,
        )

    def forward(phase, low, after_sends):
        def part(k):
            at = pl.multiple_of(k * chunk, chunk)
            block = build(k) if phase == 0 else oper[pl.ds(at, chunk), :]
            return lax.dot_general(low, block, NT, preferred_element_type=F32)

        def one(j):
            target = cell_peer(j)
            rs_send[phase, target] = part(target).astype(BF16)
            rs_copy(phase, j, target).start()

        each(n_c, one)
        after_sends()
        rs_total = part(c)
        each(n_c, lambda j: rs_copy(phase, j, cell_peer(j)).wait_recv())
        for j in range(1, n_c):
            rs_total = rs_total + rs_recv[phase, j].astype(F32)
        return rs_total * scale

    def ag_copy(phase, j, slot):
        return to_cell(
            ag.at[phase, slot], ag.at[phase, slot],
            ag_ssem.at[phase, j], ag_rsem.at[phase, j], cell_peer(j),
        )

    def gather(phase, value):
        ag[phase, c] = value.astype(BF16)
        each(n_c, lambda j: ag_copy(phase, j, c).start())
        each(n_c, lambda j: ag_copy(phase, j, cell_peer(j)).wait_recv())
        return ag[phase].astype(F32)

    def stat_copy(step, j):
        return to_cell(
            stat_send.at[step], stat_recv.at[step, j],
            st_ssem.at[step, j], st_rsem.at[step, j], cell_peer(j),
        )

    diagonal = lax.broadcasted_iota(jnp.int32, (own, own), 0) == lax.broadcasted_iota(
        jnp.int32, (own, own), 1
    )

    def to_row(column):
        return jnp.sum(jnp.where(diagonal, column, 0.0), axis=0, keepdims=True)

    def to_column(row):
        return jnp.sum(jnp.where(diagonal, row, 0.0), axis=1, keepdims=True)

    def stat_start(step, first, second):
        top = lax.broadcasted_iota(jnp.int32, (8, own), 0) == 0
        stat_send[step] = jnp.where(top, to_row(first), to_row(second))
        each(n_c, lambda j: stat_copy(step, j).start())

    def stat_total(step):
        each(n_c, lambda j: stat_copy(step, j).wait_recv())
        total = stat_send[step]
        for j in range(1, n_c):
            total = total + stat_recv[step, j]
        return to_column(total[0:1]), to_column(total[1:2])

    own_models = models_in[...]
    first_data = forward(0, own_models, lambda: None)
    each(n_s, lambda j: in_copies(j, src_peer(j), (2,))[0].wait_recv())
    own_noise = jnp.concatenate([nz_recv[k].astype(F32) for k in range(n_s)], axis=1)
    chunk_res = -(first_data + own_noise)
    res[...] = gather(0, chunk_res)

    def pair_sum(values):
        return jnp.sum(jnp.sum(values, axis=0), axis=1, keepdims=True)

    alphas = []
    for step in range(HSTEPS):
        last = step == HSTEPS - 1
        full = res[...]
        spread = pair_sum(full * full)
        delta = jnp.sqrt(spread / pairs_all + 1e-06)
        weight = delta[None] / jnp.maximum(jnp.abs(full), delta[None])
        weighted = weight * full
        for k in range(n_c):
            wlow[:, k * chunk : (k + 1) * chunk] = weighted[k].astype(BF16)
        grad = jnp.dot(wlow[...], oper[...], preferred_element_type=F32) * scale
        after = []

        def send_numer():
            grads[step] = grad
            numer_own = jnp.sum(grad * grad, axis=1, keepdims=True)
            after.append(numer_own)
            if last:
                after.append(delta / jnp.maximum(jnp.abs(chunk_res), delta))
            else:
                stat_start(step, numer_own, numer_own)

        image = forward(step + 1, grad.astype(BF16), send_numer)
        if last:
            curve_own = jnp.sum(after[1] * image * image, axis=1, keepdims=True)
            stat_start(step, after[0], curve_own)
            numer, curvature = stat_total(step)
            alpha = numer / (curvature + 1e-06)
        else:
            images = gather(step + 1, image)
            numer, _ = stat_total(step)
            curvature = pair_sum(weight * images * images)
            alpha = numer / (curvature + 1e-06)
            res[...] = full - alpha[None] * images
        chunk_res = chunk_res - alpha * image
        alphas.append(alpha)

    for k in range(n_s):
        fin_send[k] = chunk_res[:, k * share : (k + 1) * share]

    def fin_copy(j, slot):
        return to_src(
            fin_send.at[src_peer(j)], fin_recv.at[slot], fin_ssem.at[j], fin_rsem.at[j], src_peer(j)
        )

    each(n_s, lambda j: fin_copy(j, s).start())
    fin_recv[s] = fin_send[s]
    total_rec = -(alphas[0] * grads[0])
    for step in range(1, HSTEPS):
        total_rec = total_rec - alphas[step] * grads[step]
    rec_out[...] = total_rec

    def in_done(j):
        for copy in in_copies(j, s):
            copy.wait_send()

    each(n_s, in_done)
    for phase in range(HSTEPS + 1):
        each(n_c, lambda j, phase=phase: rs_copy(phase, j, cell_peer(j)).wait_send())
    for phase in range(HSTEPS):
        each(n_c, lambda j, phase=phase: ag_copy(phase, j, c).wait_send())
        each(n_c, lambda j, phase=phase: stat_copy(phase, j).wait_send())
    each(n_s, lambda j: fin_copy(j, src_peer(j)).wait_recv())
    res_out[...] = fin_recv[...].reshape(models_count, share).T
    each(n_s, lambda j: fin_copy(j, s).wait_send())


def split_pair(value, lanes):
    high = value.astype(BF16).astype(F32)
    lane = lax.broadcasted_iota(jnp.int32, value.shape, 1)
    return jnp.where(lane < lanes, high, value - high)


def gathered_body(
    n_s, n_c,
    gs, gr, ps, pr, order, models, noise,
    out,
    gs_in, gr_in, order_in, models_in, noise_in,
    fields, indices, nz_send, nz_recv, md_send, md_recv,
    gs_all, gr_all, mask, onehot, pair_rows,
    noise_masked, x_send, x_recv, fin_send, fin_recv,
    load, f_ssem, f_rsem, i_ssem, i_rsem, m_ssem, m_rsem, x_ssem, x_rsem, fin_ssem, fin_rsem,
):
    s = lax.axis_index("src")
    c = lax.axis_index("cell")
    pairs = ps.shape[1]
    cells = gs.shape[1]
    s_dev = gs.shape[0]
    r_dev = gr.shape[0]
    own = models.shape[0] // n_s
    mine = own // n_c
    half = cells // 2
    sources = n_s * s_dev
    receivers = n_s * r_dev
    pairs_all = pairs * n_s
    scale = 1.0 / math.sqrt(cells * n_c)

    def src_peer(j):
        return jnp.bitwise_xor(s, j)

    def cell_peer(j):
        return jnp.bitwise_xor(c, j)

    def remote(src_ref, dst_ref, ssem, rsem, ds, dc):
        return pltpu.make_async_remote_copy(
            src_ref=src_ref, dst_ref=dst_ref, send_sem=ssem, recv_sem=rsem,
            device_id={"src": src_peer(ds), "cell": cell_peer(dc)}, device_id_type=MESH,
        )

    barrier = pltpu.get_barrier_semaphore()
    each(n_s, lambda j: pl.semaphore_signal(
        barrier, inc=1, device_id={"src": src_peer(j)}, device_id_type=MESH))
    each(n_c, lambda j: pl.semaphore_signal(
        barrier, inc=1, device_id={"cell": cell_peer(j)}, device_id_type=MESH))

    loads = [
        pltpu.make_async_copy(order, order_in, load.at[0]),
        pltpu.make_async_copy(gs, gs_in, load.at[1]),
        pltpu.make_async_copy(gr, gr_in, load.at[2]),
        pltpu.make_async_copy(ps, indices.at[s, 0], load.at[3]),
        pltpu.make_async_copy(pr, indices.at[s, 1], load.at[4]),
        pltpu.make_async_copy(
            models.at[pl.ds(pl.multiple_of(s * own, own), own), :], models_in, load.at[5]),
        pltpu.make_async_copy(noise, noise_in, load.at[6]),
    ]
    for copy in loads:
        copy.start()
    for copy in loads[:5]:
        copy.wait()
    rows = lax.broadcasted_iota(jnp.int32, (cells, cells), 0)
    select = jnp.where(rows == order_in[...], 1.0, 0.0).astype(BF16)
    raw = jnp.concatenate([gs_in[...].astype(F32), gr_in[...].astype(F32)], axis=0).astype(BF16)
    fields[c, s] = jnp.dot(raw, select, preferred_element_type=F32).astype(BF16)

    for copy in loads[5:]:
        copy.wait()
    wide = 2 * mine
    q = lax.broadcasted_iota(jnp.int32, (n_c * wide, own), 0)
    m = lax.broadcasted_iota(jnp.int32, (n_c * wide, own), 1)
    spread_rows = jnp.where((q % mine) * n_c + q // wide == m, 1.0, 0.0).astype(BF16)
    placed = jnp.dot(spread_rows, models_in[...], preferred_element_type=F32)
    low = lax.broadcasted_iota(jnp.int32, (n_c * wide, half), 0) % wide < mine
    placed = jnp.where(low, placed[:, :half], placed[:, half:])
    md_send[...] = placed.astype(BF16).reshape(n_c, wide, half)
    md_recv[c] = md_send[c]
    q = lax.broadcasted_iota(jnp.int32, (n_s * wide, models.shape[0]), 0)
    m = lax.broadcasted_iota(jnp.int32, (n_s * wide, models.shape[0]), 1)
    columns = jnp.where(
        ((q // wide) * own + (q % wide) * n_c + c == m) & (q % wide < mine), 1.0, 0.0).astype(BF16)
    nz = lax.dot_general(columns, noise_in[...], NT, preferred_element_type=F32)
    nz_send[...] = nz.astype(BF16).reshape(n_s, wide, pairs)
    nz_recv[s] = nz_send[s]

    pl.semaphore_wait(barrier, n_s + n_c - 2)

    done = []
    count = [0]

    def send_block(t, g, ds, dc):
        at = count[0]
        count[0] += 1
        copy = remote(fields.at[t, g], fields.at[t, g], f_ssem.at[at], f_rsem.at[t, g], ds, dc)
        copy.start()
        done.append(copy.wait_send)

    def got_block(t, g):
        remote(fields.at[t, g], fields.at[t, g], f_ssem.at[0], f_rsem.at[t, g], 0, 1).wait_recv()

    def index_copy(j, slot):
        return remote(indices.at[slot], indices.at[slot], i_ssem.at[0, j], i_rsem.at[0, j], j, 0)

    def noise_copy(j):
        return remote(
            nz_send.at[src_peer(j)], nz_recv.at[s], i_ssem.at[1, j], i_rsem.at[1, j], j, 0)

    def noise_got(j):
        g = src_peer(j)
        remote(nz_send.at[g], nz_recv.at[g], i_ssem.at[1, j], i_rsem.at[1, j], j, 0).wait_recv()

    def model_copy(j):
        return remote(md_send.at[cell_peer(j)], md_recv.at[c], m_ssem.at[j], m_rsem.at[j], 0, j)

    def model_got(j):
        t = cell_peer(j)
        remote(md_send.at[t], md_recv.at[t], m_ssem.at[j], m_rsem.at[j], 0, j).wait_recv()

    steps = range(2, n_c, 2)
    across = n_s - 1
    near = range(1, across)
    send_block(c, s, across, 0)
    for d in steps:
        send_block(c, s, 0, d)
    for j in near:
        send_block(c, s, j, 0)
    send_block(c, s, 0, 1)
    each(n_s, lambda j: index_copy(j, s).start())

    each(n_c, lambda j: model_copy(j).start())
    each(n_s, lambda j: noise_copy(j).start())

    g = src_peer(across)
    got_block(c, g)
    for d in steps:
        send_block(c, g, 0, d)
    send_block(c, g, 0, 1)
    for d in steps:
        t = cell_peer(d)
        got_block(t, s)
        for j in near:
            send_block(t, s, j, 0)
        send_block(t, s, 0, 1)

    each(n_s, lambda j: index_copy(j, src_peer(j)).wait_recv())
    row = lax.broadcasted_iota(jnp.int32, (2 * receivers, pairs), 0)
    row = jnp.where(row < receivers, row, row - receivers)
    source = lax.broadcasted_iota(jnp.int32, (s_dev, pairs), 0)
    for g in range(n_s):
        mask[g] = jnp.where(source == indices[g, 0], 1.0, 0.0)
        hit = jnp.where(row == indices[g, 1], 1.0, 0.0)
        onehot[g] = hit.astype(BF16)
        pair_rows[g] = hit.T.astype(BF16)

    def unpack(t):
        block = fields[t].astype(F32)
        gs_all[t] = block[:, :s_dev].reshape(sources, cells)
        part = block[:, s_dev:].reshape(receivers, cells).astype(BF16)
        gr_all[t] = jnp.concatenate([part, part], axis=0)

    def forward(t, lines):
        base = gs_all[t]
        left = jnp.concatenate([(base * line).astype(BF16) for line in lines], axis=0)
        return lax.dot_general(left, gr_all[t], NT, preferred_element_type=F32)

    data = [None]

    def first(d):
        t = cell_peer(d)
        unpack(t)
        if d:
            model_got(d)
        line = md_recv[t].astype(F32)
        lines = [
            jnp.concatenate([line[j : j + 1], line[mine + j : mine + j + 1]], axis=1)
            for j in range(mine)
        ]
        part = forward(t, lines)
        data[0] = part if data[0] is None else data[0] + part

    def own_core(d):
        t = cell_peer(d)
        for j in near if d == 0 else range(1, n_s):
            g = src_peer(j)
            got_block(t, g)
            send_block(t, g, 0, 1)
        first(d)

    def other_core(d):
        t = cell_peer(d + 1)
        for j in range(n_s):
            got_block(t, src_peer(j))
        first(d + 1)

    own_core(0)
    each(n_s, noise_got)
    for g in range(n_s):
        line = nz_recv[g].astype(F32)
        for j in range(mine):
            noise_masked[g, j * s_dev : (j + 1) * s_dev] = line[j : j + 1] * mask[g]
    for d in steps:
        own_core(d)
        other_core(d - 2)
    other_core(n_c - 2)

    def to_pairs(value):
        mixed = split_pair(value * scale, receivers).reshape(mine, n_s, s_dev, 2 * receivers)
        out = []
        for g in range(n_s):
            left = mixed[:, g].reshape(mine * s_dev, 2 * receivers).astype(BF16)
            at_pairs = jnp.dot(left, onehot[g], preferred_element_type=F32)
            out.append(at_pairs.reshape(mine, s_dev, pairs) * mask[g][None])
        return out

    def from_pairs(values):
        out = [
            jnp.dot(
                values[g].reshape(mine * s_dev, pairs).astype(BF16), pair_rows[g],
                preferred_element_type=F32).reshape(mine, 1, s_dev, 2 * receivers)
            for g in range(n_s)
        ]
        whole = jnp.concatenate(out, axis=1).reshape(mine * sources, 2 * receivers)
        return split_pair(whole * scale, receivers).astype(BF16)

    def pair_sum(values):
        total = values[0]
        for value in values[1:]:
            total = total + value
        return jnp.sum(jnp.sum(total, axis=2, keepdims=True), axis=1, keepdims=True)

    def x_copy(step, j):
        return remote(
            x_send.at[step, cell_peer(j)], x_recv.at[step, c],
            x_ssem.at[step, j], x_rsem.at[step, j], 0, j)

    def x_got(step, j):
        t = cell_peer(j)
        remote(
            x_send.at[step, t], x_recv.at[step, t],
            x_ssem.at[step, j], x_rsem.at[step, j], 0, j).wait_recv()

    first_data = to_pairs(data[0])
    res = [-(value + noise_masked[g].reshape(mine, s_dev, pairs)) for g, value in enumerate(first_data)]

    place = lax.broadcasted_iota(jnp.int32, (wide, half), 0)
    farthest = [d + k for d in range(n_c - 2, -1, -2) for k in (1, 0)]
    alphas = []
    for step in range(HSTEPS):
        delta = jnp.sqrt(pair_sum([value * value for value in res]) / pairs_all + 1e-06)
        weight = [delta / jnp.maximum(jnp.abs(value), delta) for value in res]
        back = from_pairs([w * value for w, value in zip(weight, res)])
        numer = None
        data = None
        for d in farthest:
            t = cell_peer(d)
            fan = jnp.dot(back, gr_all[t], preferred_element_type=F32)
            grad = jnp.sum(
                fan.reshape(mine, sources, cells) * gs_all[t][None], axis=1, keepdims=True)
            square = grad * grad
            numer = square if numer is None else numer + square
            low = grad.astype(BF16).astype(F32)
            part = forward(t, [low[j] for j in range(mine)])
            data = part if data is None else data + part
            packed = jnp.zeros((wide, half), F32)
            for j in range(mine):
                packed = jnp.where(place == j, low[j][:, :half], packed)
                packed = jnp.where(place == mine + j, low[j][:, half:], packed)
            x_send[step, t] = packed.astype(BF16)
        x_recv[step, c] = x_send[step, c]
        image = to_pairs(data)
        curvature = pair_sum([w * value * value for w, value in zip(weight, image)])
        alpha = jnp.sum(numer, axis=2, keepdims=True) / (curvature + 1e-06)
        res = [value - alpha * other for value, other in zip(res, image)]
        alphas.append(alpha)
        if step < HSTEPS - 1:
            for d in farthest:
                if d:
                    x_copy(step, d).start()

    odd = c % 2
    two = 2 * (pairs // n_c)
    room = two // (2 * mine)
    lane = lax.broadcasted_iota(jnp.int32, (1, two), 1)
    marks = jnp.zeros((1, two), F32)
    for j in range(mine):
        for step in range(HSTEPS):
            marks = jnp.where(lane // room == 2 * j + step, alphas[step][j], marks)
    for g in range(n_s):
        lines = jnp.sum(res[g], axis=1, keepdims=True)
        for h in range(n_c // 2):
            fin_send[g, h] = jnp.concatenate(
                [lines[j][:, h * two : (h + 1) * two] for j in range(mine)] + [marks], axis=1)

    others = n_s * n_c

    def fin_start(i, carry):
        a, b = (others - i) // n_c, (others - i) % n_c
        remote(
            fin_send.at[src_peer(a), cell_peer(b) // 2], fin_recv.at[s * n_c + c],
            fin_ssem.at[0], fin_rsem.at[0], a, b).start()
        return carry

    lax.fori_loop(1, others, fin_start, 0)
    for d in farthest:
        if d:
            x_copy(HSTEPS - 1, d).start()
    fin_recv[s * n_c + c] = fin_send[s, c // 2]

    m = lax.broadcasted_iota(jnp.int32, (own, n_c * wide), 0)
    q = lax.broadcasted_iota(jnp.int32, (own, n_c * wide), 1)
    at = (m % n_c) * wide + m // n_c
    rows_of = [jnp.where(q == at + k * mine, 1.0, 0.0).astype(BF16) for k in (0, 1)]
    grads = []
    for step in range(HSTEPS):
        for j in range(n_c - 1, 0, -1):
            x_got(step, j)
        blocks = x_recv[step].astype(F32).reshape(n_c * wide, half).astype(BF16)
        grads.append(jnp.concatenate(
            [jnp.dot(pick, blocks, preferred_element_type=F32) for pick in rows_of], axis=1))

    for wait in done:
        wait()
    each(n_s, lambda j: index_copy(j, s).wait_send())
    each(n_c, lambda j: model_copy(j).wait_send())
    each(n_s, lambda j: noise_copy(j).wait_send())
    for step in range(HSTEPS):
        each(n_c, lambda j, step=step: x_copy(step, j).wait_send())

    rest = fin_recv.at[pl.ds(0, n_s * n_c - 1)]
    fin_all = remote(rest, rest, fin_ssem.at[0], fin_rsem.at[0], 0, 1)
    fin_all.wait_recv()
    notes = fin_recv[pl.ds(s * n_c, n_c), 0, mine * two :]
    for j in range(mine):
        at = pl.ds(j * n_c, n_c)
        here = slice(j * n_c, (j + 1) * n_c)
        first_of, second_of = (
            notes[:, (2 * j + step) * room : (2 * j + step) * room + 1] for step in range(HSTEPS))
        out[at, :] = -(first_of * grads[0][here] + second_of * grads[1][here])
    lines = jnp.concatenate(
        [
            fin_recv[:, 0, j * two : (j + 1) * two].reshape(n_s, 1, n_c, two)
            for j in range(mine)
        ], axis=1).reshape(n_s * own, two).T
    lines = jnp.where(odd == 0, lines[: two // 2], lines[two // 2 :])
    tall = out.shape[0] - own
    for k in range(lines.shape[0] // tall):
        out[own:, k * lines.shape[1] : (k + 1) * lines.shape[1]] = lines[k * tall : (k + 1) * tall]
    fin_all.wait_send()


def gathered_call(n_s, n_c, *arrays):
    gs, gr, ps, _, order, models, noise = arrays
    s_dev, cells = gs.shape
    r_dev = gr.shape[0]
    pairs = ps.shape[1]
    models_count = models.shape[0]
    own = models_count // n_s
    wide = 2 * (own // n_c)
    share = pairs // n_c
    dma = pltpu.SemaphoreType.DMA
    tall = share * models_count // cells
    out = pl.pallas_call(
        functools.partial(gathered_body, n_s, n_c),
        out_shape=pltpu.VMEM((own + tall, cells), F32),
        in_specs=[pl.BlockSpec(memory_space=pltpu.HBM)] * 7,
        out_specs=pl.BlockSpec(memory_space=pltpu.VMEM),
        scratch_shapes=[
            pltpu.VMEM((s_dev, cells), BF16),
            pltpu.VMEM((r_dev, cells), BF16),
            pltpu.VMEM((1, cells), jnp.int32),
            pltpu.VMEM((own, cells), BF16),
            pltpu.VMEM((pairs, models_count), BF16),
            pltpu.VMEM((n_c, n_s, s_dev + r_dev, cells), BF16),
            pltpu.VMEM((n_s, 2, 1, pairs), jnp.int32),
            pltpu.VMEM((n_s, wide, pairs), BF16),
            pltpu.VMEM((n_s, wide, pairs), BF16),
            pltpu.VMEM((n_c, wide, cells // 2), BF16),
            pltpu.VMEM((n_c, wide, cells // 2), BF16),
            pltpu.VMEM((n_c, n_s * s_dev, cells), F32),
            pltpu.VMEM((n_c, 2 * n_s * r_dev, cells), BF16),
            pltpu.VMEM((n_s, s_dev, pairs), F32),
            pltpu.VMEM((n_s, 2 * n_s * r_dev, pairs), BF16),
            pltpu.VMEM((n_s, pairs, 2 * n_s * r_dev), BF16),
            pltpu.VMEM((n_s, wide // 2 * s_dev, pairs), F32),
            pltpu.VMEM((HSTEPS, n_c, wide, cells // 2), BF16),
            pltpu.VMEM((HSTEPS, n_c, wide, cells // 2), BF16),
            pltpu.VMEM((n_s, n_c // 2, 1, (wide // 2 + 1) * 2 * share), F32),
            pltpu.VMEM((n_s * n_c, 1, (wide // 2 + 1) * 2 * share), F32),
            dma((7,)), dma((n_s * n_c,)), dma((n_c, n_s)),
            dma((2, n_s)), dma((2, n_s)),
            dma((n_c,)), dma((n_c,)),
            dma((HSTEPS, n_c)), dma((HSTEPS, n_c)),
            dma((1,)), dma((1,)),
        ],
        compiler_params=pltpu.CompilerParams(
            collective_id=0, has_side_effects=True, vmem_limit_bytes=60 * 1024 * 1024
        ),
    )(*arrays)
    pieces = [
        out[own:, k * models_count : (k + 1) * models_count] for k in range(cells // models_count)
    ]
    return out[:own], jnp.concatenate(pieces, axis=0)


def fits_gathered(n_s, n_c, s_dev, r_dev, cells, pairs, models_count):
    return (
        n_c & (n_c - 1) == 0 and n_s == 4
        and models_count == 4 * n_s * n_c
        and s_dev == 8 and r_dev % 8 == 0 and 2 * n_s * r_dev == 128
        and pairs == 64 * n_c and cells % 256 == 0
        and cells % models_count == 0 and 64 * models_count == 8 * cells
    )


def shards(
    green_source, green_receiver, pair_source, pair_receiver, cell_order, test_models, data_noise
):
    n_s = lax.axis_size("src")
    n_c = lax.axis_size("cell")
    s_dev, cells = green_source.shape
    r_dev = green_receiver.shape[0]
    group_pairs = pair_source.shape[0]
    models_count = test_models.shape[0]
    own = models_count // n_s
    share = group_pairs // n_c
    chunk = share * n_s
    pairs_all = group_pairs * n_s
    arrays = (
        green_source, green_receiver, pair_source[None, :], pair_receiver[None, :],
        cell_order, test_models, data_noise,
    )
    if fits_gathered(n_s, n_c, s_dev, r_dev, cells, group_pairs, models_count):
        return gathered_call(n_s, n_c, *arrays)
    dma = pltpu.SemaphoreType.DMA
    return pl.pallas_call(
        functools.partial(kernel_body, n_s, n_c),
        out_shape=(
            pltpu.VMEM((own, cells), F32),
            pltpu.VMEM((share, models_count), F32),
        ),
        in_specs=[pl.BlockSpec(memory_space=pltpu.HBM)] * 7,
        out_specs=[pl.BlockSpec(memory_space=pltpu.VMEM)] * 2,
        scratch_shapes=[
            pltpu.VMEM((s_dev, cells), BF16),
            pltpu.VMEM((r_dev, cells), BF16),
            pltpu.VMEM((1, cells), jnp.int32),
            pltpu.VMEM((own, cells), BF16),
            pltpu.VMEM((share, models_count), BF16),
            pltpu.VMEM((n_s, s_dev + r_dev, cells), BF16),
            pltpu.VMEM((n_s, 2, 1, group_pairs), jnp.int32),
            pltpu.VMEM((n_s, own, share), BF16),
            pltpu.VMEM((n_s, own, share), BF16),
            pltpu.VMEM((pairs_all, n_s * (s_dev + r_dev)), BF16),
            pltpu.VMEM((pairs_all, cells), BF16),
            pltpu.VMEM((HSTEPS + 1, n_c, own, chunk), BF16),
            pltpu.VMEM((HSTEPS + 1, n_c, own, chunk), BF16),
            pltpu.VMEM((HSTEPS, n_c, own, chunk), BF16),
            pltpu.VMEM((HSTEPS, 8, own), F32),
            pltpu.VMEM((HSTEPS, n_c, 8, own), F32),
            pltpu.VMEM((n_s, own, share), F32),
            pltpu.VMEM((n_s, own, share), F32),
            pltpu.VMEM((own, pairs_all), BF16),
            pltpu.VMEM((n_c, own, chunk), F32),
            pltpu.VMEM((HSTEPS, own, cells), F32),
            dma((7,)), dma((3, n_s)), dma((3, n_s)),
            dma((HSTEPS + 1, n_c)), dma((HSTEPS + 1, n_c)),
            dma((HSTEPS, n_c)), dma((HSTEPS, n_c)),
            dma((HSTEPS, n_c)), dma((HSTEPS, n_c)),
            dma((n_s,)), dma((n_s,)),
        ],
        compiler_params=pltpu.CompilerParams(
            collective_id=0, has_side_effects=True, vmem_limit_bytes=60 * 1024 * 1024
        ),
    )(*arrays)


def solution(mesh):
    return jax.shard_map(
        shards,
        mesh=mesh,
        in_specs=(
            P("src", "cell"),
            P("src", "cell"),
            P("src"),
            P("src"),
            P("cell", None),
            P(None, "cell"),
            P("src", None),
        ),
        out_specs=(P("src", "cell"), P(("src", "cell"), None)),
        check_vma=False,
    )
```

```python
import functools
import math

import jax
import jax.numpy as jnp
from jax import lax
from jax.experimental import pallas as pl
from jax.experimental.pallas import tpu as pltpu
from jax.sharding import PartitionSpec as P

HSTEPS = 2
MESH = pl.DeviceIdType.MESH
F32 = jnp.float32
BF16 = jnp.bfloat16
NT = (((1,), (1,)), ((), ()))


def each(count, body):
    if count <= 8:
        for i in range(count - 1, 0, -1):
            body(i)
    else:

        def step(i, carry):
            body(count - i)
            return carry

        lax.fori_loop(1, count, step, 0)


def kernel_body(
    n_s, n_c,
    gs, gr, ps, pr, order, models, noise,
    rec_out, res_out,
    gs_in, gr_in, order_in, models_in, noise_in,
    fields, indices, nz_send, nz_recv,
    picks, oper, rs_send, rs_recv, ag, stat_send, stat_recv,
    fin_send, fin_recv, wlow, res, grads,
    load, in_send, in_recv, rs_ssem, rs_rsem, ag_ssem, ag_rsem, st_ssem, st_rsem, fin_ssem, fin_rsem,
):
    s = lax.axis_index("src")
    c = lax.axis_index("cell")
    group_pairs = ps.shape[1]
    cells = gs.shape[1]
    models_count = models.shape[0]
    own = models_count // n_s
    share = group_pairs // n_c
    chunk = share * n_s
    pairs_all = group_pairs * n_s
    s_dev = gs.shape[0]
    r_dev = gr.shape[0]
    scale = 1.0 / math.sqrt(cells * n_c)

    def src_peer(j):
        return jnp.bitwise_xor(s, j)

    def cell_peer(j):
        return jnp.bitwise_xor(c, j)

    def to_src(src_ref, dst_ref, ssem, rsem, peer):
        return pltpu.make_async_remote_copy(
            src_ref=src_ref, dst_ref=dst_ref, send_sem=ssem, recv_sem=rsem,
            device_id={"src": peer}, device_id_type=MESH,
        )

    def to_cell(src_ref, dst_ref, ssem, rsem, peer):
        return pltpu.make_async_remote_copy(
            src_ref=src_ref, dst_ref=dst_ref, send_sem=ssem, recv_sem=rsem,
            device_id={"cell": peer}, device_id_type=MESH,
        )

    barrier = pltpu.get_barrier_semaphore()
    each(n_s, lambda j: pl.semaphore_signal(
        barrier, inc=1, device_id={"src": src_peer(j)}, device_id_type=MESH))
    each(n_c, lambda j: pl.semaphore_signal(
        barrier, inc=1, device_id={"cell": cell_peer(j)}, device_id_type=MESH))

    loads = [
        pltpu.make_async_copy(order, order_in, load.at[0]),
        pltpu.make_async_copy(gs, gs_in, load.at[1]),
        pltpu.make_async_copy(gr, gr_in, load.at[2]),
        pltpu.make_async_copy(ps, indices.at[s, 0], load.at[3]),
        pltpu.make_async_copy(pr, indices.at[s, 1], load.at[4]),
        pltpu.make_async_copy(
            noise.at[pl.ds(pl.multiple_of(c * share, share), share), :], noise_in, load.at[5]),
        pltpu.make_async_copy(
            models.at[pl.ds(pl.multiple_of(s * own, own), own), :], models_in, load.at[6]),
    ]
    for copy in loads:
        copy.start()
    for copy in loads:
        copy.wait()
    rows = lax.broadcasted_iota(jnp.int32, (cells, cells), 0)
    select = jnp.where(rows == order_in[...], 1.0, 0.0).astype(BF16)
    raw = jnp.concatenate([gs_in[...].astype(F32), gr_in[...].astype(F32)], axis=0).astype(BF16)
    fields[s] = jnp.dot(raw, select, preferred_element_type=F32).astype(BF16)
    nz_send[...] = noise_in[...].astype(F32).T.reshape(n_s, own, share).astype(BF16)
    nz_recv[s] = nz_send[s]

    pl.semaphore_wait(barrier, n_s + n_c - 2)

    def in_copies(j, slot, which=(0, 1, 2)):
        peer = src_peer(j)
        makers = [
            lambda: to_src(fields.at[slot], fields.at[slot], in_send.at[0, j], in_recv.at[0, j], peer),
            lambda: to_src(indices.at[slot], indices.at[slot], in_send.at[1, j], in_recv.at[1, j], peer),
            lambda: to_src(nz_send.at[peer], nz_recv.at[slot], in_send.at[2, j], in_recv.at[2, j], peer),
        ]
        return [makers[n]() for n in which]

    each(n_s, lambda j: in_copies(j, s, (1,))[0].start())
    each(n_s, lambda j: in_copies(j, s, (0,))[0].start())
    each(n_s, lambda j: in_copies(j, s, (2,))[0].start())

    dev_rows = s_dev + r_dev
    field_rows = n_s * dev_rows
    row = lax.broadcasted_iota(jnp.int32, (field_rows, 1), 0)
    group = jnp.zeros((field_rows, 1), jnp.int32)
    for k in range(1, n_s):
        group = group + jnp.where(row >= k * dev_rows, 1, 0)
    within = row - group * dev_rows
    is_source = within < s_dev
    source_id = jnp.where(is_source, group * s_dev + within, -1)
    receiver_id = jnp.where(is_source, -1, group * r_dev + within - s_dev)

    each(n_s, lambda j: in_copies(j, src_peer(j), (1,))[0].wait_recv())

    for k in range(n_s):
        hit = (source_id == indices[k, 0] + k * s_dev) | (receiver_id == indices[k, 1])
        pick = jnp.where(hit, 1.0, 0.0).T.astype(BF16)
        for t in range(n_c):
            at = t * chunk + k * share
            picks[at : at + share, :] = pick[t * share : (t + 1) * share]
    each(n_s, lambda j: in_copies(j, src_peer(j), (0,))[0].wait_recv())
    every = fields[...].astype(F32).reshape(field_rows, cells)
    source_cols = jnp.where(is_source, every, 0.0).astype(BF16)
    receiver_cols = jnp.where(is_source, 0.0, every).astype(BF16)

    def build(k):
        at = pl.multiple_of(k * chunk, chunk)
        pick = picks[pl.ds(at, chunk), :]
        block = (
            jnp.dot(pick, source_cols, preferred_element_type=F32)
            * jnp.dot(pick, receiver_cols, preferred_element_type=F32)
        ).astype(BF16)
        oper[pl.ds(at, chunk), :] = block
        return block

    def rs_copy(phase, j, target):
        return to_cell(
            rs_send.at[phase, target], rs_recv.at[phase, j],
            rs_ssem.at[phase, j], rs_rsem.at[phase, j], target,
        )

    def forward(phase, low, after_sends):
        def part(k):
            at = pl.multiple_of(k * chunk, chunk)
            block = build(k) if phase == 0 else oper[pl.ds(at, chunk), :]
            return lax.dot_general(low, block, NT, preferred_element_type=F32)

        def one(j):
            target = cell_peer(j)
            rs_send[phase, target] = part(target).astype(BF16)
            rs_copy(phase, j, target).start()

        each(n_c, one)
        after_sends()
        rs_total = part(c)
        each(n_c, lambda j: rs_copy(phase, j, cell_peer(j)).wait_recv())
        for j in range(1, n_c):
            rs_total = rs_total + rs_recv[phase, j].astype(F32)
        return rs_total * scale

    def ag_copy(phase, j, slot):
        return to_cell(
            ag.at[phase, slot], ag.at[phase, slot],
            ag_ssem.at[phase, j], ag_rsem.at[phase, j], cell_peer(j),
        )

    def gather(phase, value):
        ag[phase, c] = value.astype(BF16)
        each(n_c, lambda j: ag_copy(phase, j, c).start())
        each(n_c, lambda j: ag_copy(phase, j, cell_peer(j)).wait_recv())
        return ag[phase].astype(F32)

    def stat_copy(step, j):
        return to_cell(
            stat_send.at[step], stat_recv.at[step, j],
            st_ssem.at[step, j], st_rsem.at[step, j], cell_peer(j),
        )

    diagonal = lax.broadcasted_iota(jnp.int32, (own, own), 0) == lax.broadcasted_iota(
        jnp.int32, (own, own), 1
    )

    def to_row(column):
        return jnp.sum(jnp.where(diagonal, column, 0.0), axis=0, keepdims=True)

    def to_column(row):
        return jnp.sum(jnp.where(diagonal, row, 0.0), axis=1, keepdims=True)

    def stat_start(step, first, second):
        top = lax.broadcasted_iota(jnp.int32, (8, own), 0) == 0
        stat_send[step] = jnp.where(top, to_row(first), to_row(second))
        each(n_c, lambda j: stat_copy(step, j).start())

    def stat_total(step):
        each(n_c, lambda j: stat_copy(step, j).wait_recv())
        total = stat_send[step]
        for j in range(1, n_c):
            total = total + stat_recv[step, j]
        return to_column(total[0:1]), to_column(total[1:2])

    own_models = models_in[...]
    first_data = forward(0, own_models, lambda: None)
    each(n_s, lambda j: in_copies(j, src_peer(j), (2,))[0].wait_recv())
    own_noise = jnp.concatenate([nz_recv[k].astype(F32) for k in range(n_s)], axis=1)
    chunk_res = -(first_data + own_noise)
    res[...] = gather(0, chunk_res)

    def pair_sum(values):
        return jnp.sum(jnp.sum(values, axis=0), axis=1, keepdims=True)

    alphas = []
    for step in range(HSTEPS):
        last = step == HSTEPS - 1
        full = res[...]
        spread = pair_sum(full * full)
        delta = jnp.sqrt(spread / pairs_all + 1e-06)
        weight = delta[None] / jnp.maximum(jnp.abs(full), delta[None])
        weighted = weight * full
        for k in range(n_c):
            wlow[:, k * chunk : (k + 1) * chunk] = weighted[k].astype(BF16)
        grad = jnp.dot(wlow[...], oper[...], preferred_element_type=F32) * scale
        after = []

        def send_numer():
            grads[step] = grad
            numer_own = jnp.sum(grad * grad, axis=1, keepdims=True)
            after.append(numer_own)
            if last:
                after.append(delta / jnp.maximum(jnp.abs(chunk_res), delta))
            else:
                stat_start(step, numer_own, numer_own)

        image = forward(step + 1, grad.astype(BF16), send_numer)
        if last:
            curve_own = jnp.sum(after[1] * image * image, axis=1, keepdims=True)
            stat_start(step, after[0], curve_own)
            numer, curvature = stat_total(step)
            alpha = numer / (curvature + 1e-06)
        else:
            images = gather(step + 1, image)
            numer, _ = stat_total(step)
            curvature = pair_sum(weight * images * images)
            alpha = numer / (curvature + 1e-06)
            res[...] = full - alpha[None] * images
        chunk_res = chunk_res - alpha * image
        alphas.append(alpha)

    for k in range(n_s):
        fin_send[k] = chunk_res[:, k * share : (k + 1) * share]

    def fin_copy(j, slot):
        return to_src(
            fin_send.at[src_peer(j)], fin_recv.at[slot], fin_ssem.at[j], fin_rsem.at[j], src_peer(j)
        )

    each(n_s, lambda j: fin_copy(j, s).start())
    fin_recv[s] = fin_send[s]
    total_rec = -(alphas[0] * grads[0])
    for step in range(1, HSTEPS):
        total_rec = total_rec - alphas[step] * grads[step]
    rec_out[...] = total_rec

    def in_done(j):
        for copy in in_copies(j, s):
            copy.wait_send()

    each(n_s, in_done)
    for phase in range(HSTEPS + 1):
        each(n_c, lambda j, phase=phase: rs_copy(phase, j, cell_peer(j)).wait_send())
    for phase in range(HSTEPS):
        each(n_c, lambda j, phase=phase: ag_copy(phase, j, c).wait_send())
        each(n_c, lambda j, phase=phase: stat_copy(phase, j).wait_send())
    each(n_s, lambda j: fin_copy(j, src_peer(j)).wait_recv())
    res_out[...] = fin_recv[...].reshape(models_count, share).T
    each(n_s, lambda j: fin_copy(j, s).wait_send())


def split_pair(value, lanes):
    high = value.astype(BF16).astype(F32)
    lane = lax.broadcasted_iota(jnp.int32, value.shape, 1)
    return jnp.where(lane < lanes, high, value - high)


def gathered_body(
    n_s, n_c,
    gs, gr, ps, pr, order, models, noise,
    out,
    gs_in, gr_in, order_in, models_in, noise_in,
    fields, indices, nz_send, nz_recv, md_send, md_recv,
    gs_all, gr_all, mask, onehot, pair_rows,
    noise_masked, x_send, x_recv, fin_send, fin_recv,
    load, f_ssem, f_rsem, i_ssem, i_rsem, m_ssem, m_rsem, x_ssem, x_rsem, fin_ssem, fin_rsem,
):
    s = lax.axis_index("src")
    c = lax.axis_index("cell")
    pairs = ps.shape[1]
    cells = gs.shape[1]
    s_dev = gs.shape[0]
    r_dev = gr.shape[0]
    own = models.shape[0] // n_s
    mine = own // n_c
    half = cells // 2
    sources = n_s * s_dev
    receivers = n_s * r_dev
    pairs_all = pairs * n_s
    scale = 1.0 / math.sqrt(cells * n_c)

    def src_peer(j):
        return jnp.bitwise_xor(s, j)

    def cell_peer(j):
        return jnp.bitwise_xor(c, j)

    def remote(src_ref, dst_ref, ssem, rsem, ds, dc):
        return pltpu.make_async_remote_copy(
            src_ref=src_ref, dst_ref=dst_ref, send_sem=ssem, recv_sem=rsem,
            device_id={"src": src_peer(ds), "cell": cell_peer(dc)}, device_id_type=MESH,
        )

    barrier = pltpu.get_barrier_semaphore()
    each(n_c, lambda j: pl.semaphore_signal(
        barrier, inc=1, device_id={"cell": cell_peer(j)}, device_id_type=MESH))
    each(n_s, lambda j: pl.semaphore_signal(
        barrier, inc=1, device_id={"src": src_peer(j)}, device_id_type=MESH))

    loads = [
        pltpu.make_async_copy(order, order_in, load.at[0]),
        pltpu.make_async_copy(gs, gs_in, load.at[1]),
        pltpu.make_async_copy(gr, gr_in, load.at[2]),
        pltpu.make_async_copy(ps, indices.at[s, 0], load.at[3]),
        pltpu.make_async_copy(pr, indices.at[s, 1], load.at[4]),
        pltpu.make_async_copy(
            models.at[pl.ds(pl.multiple_of(s * own, own), own), :], models_in, load.at[5]),
        pltpu.make_async_copy(noise, noise_in, load.at[6]),
    ]
    for copy in loads:
        copy.start()
    for copy in loads[:5]:
        copy.wait()
    rows = lax.broadcasted_iota(jnp.int32, (cells, cells), 0)
    select = jnp.where(rows == order_in[...], 1.0, 0.0).astype(BF16)
    raw = jnp.concatenate([gs_in[...].astype(F32), gr_in[...].astype(F32)], axis=0).astype(BF16)
    fields[c, s] = jnp.dot(raw, select, preferred_element_type=F32).astype(BF16)

    for copy in loads[5:]:
        copy.wait()
    wide = 2 * mine
    q = lax.broadcasted_iota(jnp.int32, (n_c * wide, own), 0)
    m = lax.broadcasted_iota(jnp.int32, (n_c * wide, own), 1)
    spread_rows = jnp.where((q % mine) * n_c + q // wide == m, 1.0, 0.0).astype(BF16)
    placed = jnp.dot(spread_rows, models_in[...], preferred_element_type=F32)
    low = lax.broadcasted_iota(jnp.int32, (n_c * wide, half), 0) % wide < mine
    placed = jnp.where(low, placed[:, :half], placed[:, half:])
    md_send[...] = placed.astype(BF16).reshape(n_c, wide, half)
    md_recv[c] = md_send[c]
    q = lax.broadcasted_iota(jnp.int32, (n_s * wide, models.shape[0]), 0)
    m = lax.broadcasted_iota(jnp.int32, (n_s * wide, models.shape[0]), 1)
    columns = jnp.where(
        ((q // wide) * own + (q % wide) * n_c + c == m) & (q % wide < mine), 1.0, 0.0).astype(BF16)
    nz = lax.dot_general(columns, noise_in[...], NT, preferred_element_type=F32)
    nz_send[...] = nz.astype(BF16).reshape(n_s, wide, pairs)
    nz_recv[s] = nz_send[s]

    pl.semaphore_wait(barrier, n_s + n_c - 2)

    done = []
    count = [0]

    def send_block(t, g, ds, dc):
        at = count[0]
        count[0] += 1
        copy = remote(fields.at[t, g], fields.at[t, g], f_ssem.at[at], f_rsem.at[t, g], ds, dc)
        copy.start()
        done.append(copy.wait_send)

    def got_block(t, g):
        remote(fields.at[t, g], fields.at[t, g], f_ssem.at[0], f_rsem.at[t, g], 0, 1).wait_recv()

    def index_copy(j, slot):
        return remote(indices.at[slot], indices.at[slot], i_ssem.at[0, j], i_rsem.at[0, j], j, 0)

    def noise_copy(j):
        return remote(
            nz_send.at[src_peer(j)], nz_recv.at[s], i_ssem.at[1, j], i_rsem.at[1, j], j, 0)

    def noise_got(j):
        g = src_peer(j)
        remote(nz_send.at[g], nz_recv.at[g], i_ssem.at[1, j], i_rsem.at[1, j], j, 0).wait_recv()

    def model_copy(j):
        return remote(md_send.at[cell_peer(j)], md_recv.at[c], m_ssem.at[j], m_rsem.at[j], 0, j)

    def model_got(j):
        t = cell_peer(j)
        remote(md_send.at[t], md_recv.at[t], m_ssem.at[j], m_rsem.at[j], 0, j).wait_recv()

    steps = range(2, n_c, 2)
    across = n_s - 1
    near = range(1, across)
    send_block(c, s, across, 0)
    for d in steps:
        send_block(c, s, 0, d)
    for j in near:
        send_block(c, s, j, 0)
    send_block(c, s, 0, 1)
    each(n_s, lambda j: index_copy(j, s).start())

    each(n_c, lambda j: model_copy(j).start())
    each(n_s, lambda j: noise_copy(j).start())

    g = src_peer(across)
    got_block(c, g)
    for d in steps:
        send_block(c, g, 0, d)
    send_block(c, g, 0, 1)
    for d in steps:
        t = cell_peer(d)
        got_block(t, s)
        for j in near:
            send_block(t, s, j, 0)
        send_block(t, s, 0, 1)

    each(n_s, lambda j: index_copy(j, src_peer(j)).wait_recv())
    row = lax.broadcasted_iota(jnp.int32, (2 * receivers, pairs), 0)
    row = jnp.where(row < receivers, row, row - receivers)
    source = lax.broadcasted_iota(jnp.int32, (s_dev, pairs), 0)
    for g in range(n_s):
        mask[g] = jnp.where(source == indices[g, 0], 1.0, 0.0)
        hit = jnp.where(row == indices[g, 1], 1.0, 0.0)
        onehot[g] = hit.astype(BF16)
        pair_rows[g] = hit.T.astype(BF16)

    def unpack(t):
        block = fields[t].astype(F32)
        gs_all[t] = block[:, :s_dev].reshape(sources, cells)
        part = block[:, s_dev:].reshape(receivers, cells).astype(BF16)
        gr_all[t] = jnp.concatenate([part, part], axis=0)

    def forward(t, lines):
        base = gs_all[t]
        left = jnp.concatenate([(base * line).astype(BF16) for line in lines], axis=0)
        return lax.dot_general(left, gr_all[t], NT, preferred_element_type=F32)

    data = [None]

    def first(d):
        t = cell_peer(d)
        unpack(t)
        if d:
            model_got(d)
        line = md_recv[t].astype(F32)
        lines = [
            jnp.concatenate([line[j : j + 1], line[mine + j : mine + j + 1]], axis=1)
            for j in range(mine)
        ]
        part = forward(t, lines)
        data[0] = part if data[0] is None else data[0] + part

    def own_core(d):
        t = cell_peer(d)
        for j in near if d == 0 else range(1, n_s):
            g = src_peer(j)
            got_block(t, g)
            send_block(t, g, 0, 1)
        first(d)

    def other_core(d):
        t = cell_peer(d + 1)
        for j in range(n_s):
            got_block(t, src_peer(j))
        first(d + 1)

    own_core(0)
    each(n_s, noise_got)
    for g in range(n_s):
        line = nz_recv[g].astype(F32)
        for j in range(mine):
            noise_masked[g, j * s_dev : (j + 1) * s_dev] = line[j : j + 1] * mask[g]
    for d in steps:
        own_core(d)
        other_core(d - 2)
    other_core(n_c - 2)

    def to_pairs(value):
        mixed = split_pair(value * scale, receivers).reshape(mine, n_s, s_dev, 2 * receivers)
        out = []
        for g in range(n_s):
            left = mixed[:, g].reshape(mine * s_dev, 2 * receivers).astype(BF16)
            at_pairs = jnp.dot(left, onehot[g], preferred_element_type=F32)
            out.append(at_pairs.reshape(mine, s_dev, pairs) * mask[g][None])
        return out

    def from_pairs(values):
        out = [
            jnp.dot(
                values[g].reshape(mine * s_dev, pairs).astype(BF16), pair_rows[g],
                preferred_element_type=F32).reshape(mine, 1, s_dev, 2 * receivers)
            for g in range(n_s)
        ]
        whole = jnp.concatenate(out, axis=1).reshape(mine * sources, 2 * receivers)
        return split_pair(whole * scale, receivers).astype(BF16)

    def pair_sum(values):
        total = values[0]
        for value in values[1:]:
            total = total + value
        return jnp.sum(jnp.sum(total, axis=2, keepdims=True), axis=1, keepdims=True)

    def x_copy(step, j):
        return remote(
            x_send.at[step, cell_peer(j)], x_recv.at[step, c],
            x_ssem.at[step, j], x_rsem.at[step, j], 0, j)

    def x_got(step, j):
        t = cell_peer(j)
        remote(
            x_send.at[step, t], x_recv.at[step, t],
            x_ssem.at[step, j], x_rsem.at[step, j], 0, j).wait_recv()

    first_data = to_pairs(data[0])
    res = [-(value + noise_masked[g].reshape(mine, s_dev, pairs)) for g, value in enumerate(first_data)]

    place = lax.broadcasted_iota(jnp.int32, (wide, half), 0)
    farthest = [d + k for d in range(n_c - 2, -1, -2) for k in (1, 0)]
    alphas = []
    for step in range(HSTEPS):
        delta = jnp.sqrt(pair_sum([value * value for value in res]) / pairs_all + 1e-06)
        weight = [delta / jnp.maximum(jnp.abs(value), delta) for value in res]
        back = from_pairs([w * value for w, value in zip(weight, res)])
        numer = None
        data = None
        for d in farthest:
            t = cell_peer(d)
            fan = jnp.dot(back, gr_all[t], preferred_element_type=F32)
            grad = jnp.sum(
                fan.reshape(mine, sources, cells) * gs_all[t][None], axis=1, keepdims=True)
            square = grad * grad
            numer = square if numer is None else numer + square
            low = grad.astype(BF16).astype(F32)
            part = forward(t, [low[j] for j in range(mine)])
            data = part if data is None else data + part
            packed = jnp.zeros((wide, half), F32)
            for j in range(mine):
                packed = jnp.where(place == j, low[j][:, :half], packed)
                packed = jnp.where(place == mine + j, low[j][:, half:], packed)
            x_send[step, t] = packed.astype(BF16)
        x_recv[step, c] = x_send[step, c]
        image = to_pairs(data)
        curvature = pair_sum([w * value * value for w, value in zip(weight, image)])
        alpha = jnp.sum(numer, axis=2, keepdims=True) / (curvature + 1e-06)
        res = [value - alpha * other for value, other in zip(res, image)]
        alphas.append(alpha)
        if step < HSTEPS - 1:
            for d in farthest:
                if d:
                    x_copy(step, d).start()

    odd = c % 2
    two = 2 * (pairs // n_c)
    room = two // (2 * mine)
    lane = lax.broadcasted_iota(jnp.int32, (1, two), 1)
    marks = jnp.zeros((1, two), F32)
    for j in range(mine):
        for step in range(HSTEPS):
            marks = jnp.where(lane // room == 2 * j + step, alphas[step][j], marks)
    for g in range(n_s):
        lines = jnp.sum(res[g], axis=1, keepdims=True)
        for h in range(n_c // 2):
            fin_send[g, h] = jnp.concatenate(
                [lines[j][:, h * two : (h + 1) * two] for j in range(mine)] + [marks], axis=1)

    others = n_s * n_c

    def fin_start(i, carry):
        a, b = (others - i) // n_c, (others - i) % n_c
        remote(
            fin_send.at[src_peer(a), cell_peer(b) // 2], fin_recv.at[s * n_c + c],
            fin_ssem.at[0], fin_rsem.at[0], a, b).start()
        return carry

    lax.fori_loop(1, n_c * (n_s - 1) + 1, fin_start, 0)
    for d in farthest:
        if d:
            x_copy(HSTEPS - 1, d).start()
    lax.fori_loop(n_c * (n_s - 1) + 1, others, fin_start, 0)
    fin_recv[s * n_c + c] = fin_send[s, c // 2]

    m = lax.broadcasted_iota(jnp.int32, (own, n_c * wide), 0)
    q = lax.broadcasted_iota(jnp.int32, (own, n_c * wide), 1)
    at = (m % n_c) * wide + m // n_c
    rows_of = [jnp.where(q == at + k * mine, 1.0, 0.0).astype(BF16) for k in (0, 1)]
    grads = []
    for step in range(HSTEPS):
        for j in range(n_c - 1, 0, -1):
            x_got(step, j)
        blocks = x_recv[step].astype(F32).reshape(n_c * wide, half).astype(BF16)
        grads.append(jnp.concatenate(
            [jnp.dot(pick, blocks, preferred_element_type=F32) for pick in rows_of], axis=1))

    for wait in done:
        wait()
    each(n_s, lambda j: index_copy(j, s).wait_send())
    each(n_c, lambda j: model_copy(j).wait_send())
    each(n_s, lambda j: noise_copy(j).wait_send())
    for step in range(HSTEPS):
        each(n_c, lambda j, step=step: x_copy(step, j).wait_send())

    rest = fin_recv.at[pl.ds(0, n_s * n_c - 1)]
    fin_all = remote(rest, rest, fin_ssem.at[0], fin_rsem.at[0], 0, 1)
    fin_all.wait_recv()
    notes = fin_recv[pl.ds(s * n_c, n_c), 0, mine * two :]
    for j in range(mine):
        at = pl.ds(j * n_c, n_c)
        here = slice(j * n_c, (j + 1) * n_c)
        first_of, second_of = (
            notes[:, (2 * j + step) * room : (2 * j + step) * room + 1] for step in range(HSTEPS))
        out[at, :] = -(first_of * grads[0][here] + second_of * grads[1][here])
    lines = jnp.concatenate(
        [
            fin_recv[:, 0, j * two : (j + 1) * two].reshape(n_s, 1, n_c, two)
            for j in range(mine)
        ], axis=1).reshape(n_s * own, two).T
    lines = jnp.where(odd == 0, lines[: two // 2], lines[two // 2 :])
    tall = out.shape[0] - own
    for k in range(lines.shape[0] // tall):
        out[own:, k * lines.shape[1] : (k + 1) * lines.shape[1]] = lines[k * tall : (k + 1) * tall]
    fin_all.wait_send()


def gathered_call(n_s, n_c, *arrays):
    gs, gr, ps, _, order, models, noise = arrays
    s_dev, cells = gs.shape
    r_dev = gr.shape[0]
    pairs = ps.shape[1]
    models_count = models.shape[0]
    own = models_count // n_s
    wide = 2 * (own // n_c)
    share = pairs // n_c
    dma = pltpu.SemaphoreType.DMA
    tall = share * models_count // cells
    out = pl.pallas_call(
        functools.partial(gathered_body, n_s, n_c),
        out_shape=pltpu.VMEM((own + tall, cells), F32),
        in_specs=[pl.BlockSpec(memory_space=pltpu.HBM)] * 7,
        out_specs=pl.BlockSpec(memory_space=pltpu.VMEM),
        scratch_shapes=[
            pltpu.VMEM((s_dev, cells), BF16),
            pltpu.VMEM((r_dev, cells), BF16),
            pltpu.VMEM((1, cells), jnp.int32),
            pltpu.VMEM((own, cells), BF16),
            pltpu.VMEM((pairs, models_count), BF16),
            pltpu.VMEM((n_c, n_s, s_dev + r_dev, cells), BF16),
            pltpu.VMEM((n_s, 2, 1, pairs), jnp.int32),
            pltpu.VMEM((n_s, wide, pairs), BF16),
            pltpu.VMEM((n_s, wide, pairs), BF16),
            pltpu.VMEM((n_c, wide, cells // 2), BF16),
            pltpu.VMEM((n_c, wide, cells // 2), BF16),
            pltpu.VMEM((n_c, n_s * s_dev, cells), F32),
            pltpu.VMEM((n_c, 2 * n_s * r_dev, cells), BF16),
            pltpu.VMEM((n_s, s_dev, pairs), F32),
            pltpu.VMEM((n_s, 2 * n_s * r_dev, pairs), BF16),
            pltpu.VMEM((n_s, pairs, 2 * n_s * r_dev), BF16),
            pltpu.VMEM((n_s, wide // 2 * s_dev, pairs), F32),
            pltpu.VMEM((HSTEPS, n_c, wide, cells // 2), BF16),
            pltpu.VMEM((HSTEPS, n_c, wide, cells // 2), BF16),
            pltpu.VMEM((n_s, n_c // 2, 1, (wide // 2 + 1) * 2 * share), F32),
            pltpu.VMEM((n_s * n_c, 1, (wide // 2 + 1) * 2 * share), F32),
            dma((7,)), dma((n_s * n_c,)), dma((n_c, n_s)),
            dma((2, n_s)), dma((2, n_s)),
            dma((n_c,)), dma((n_c,)),
            dma((HSTEPS, n_c)), dma((HSTEPS, n_c)),
            dma((1,)), dma((1,)),
        ],
        compiler_params=pltpu.CompilerParams(
            collective_id=0, has_side_effects=True, vmem_limit_bytes=60 * 1024 * 1024
        ),
    )(*arrays)
    pieces = [
        out[own:, k * models_count : (k + 1) * models_count] for k in range(cells // models_count)
    ]
    return out[:own], jnp.concatenate(pieces, axis=0)


def fits_gathered(n_s, n_c, s_dev, r_dev, cells, pairs, models_count):
    return (
        n_c & (n_c - 1) == 0 and n_s == 4
        and models_count == 4 * n_s * n_c
        and s_dev == 8 and r_dev % 8 == 0 and 2 * n_s * r_dev == 128
        and pairs == 64 * n_c and cells % 256 == 0
        and cells % models_count == 0 and 64 * models_count == 8 * cells
    )


def shards(
    green_source, green_receiver, pair_source, pair_receiver, cell_order, test_models, data_noise
):
    n_s = lax.axis_size("src")
    n_c = lax.axis_size("cell")
    s_dev, cells = green_source.shape
    r_dev = green_receiver.shape[0]
    group_pairs = pair_source.shape[0]
    models_count = test_models.shape[0]
    own = models_count // n_s
    share = group_pairs // n_c
    chunk = share * n_s
    pairs_all = group_pairs * n_s
    arrays = (
        green_source, green_receiver, pair_source[None, :], pair_receiver[None, :],
        cell_order, test_models, data_noise,
    )
    if fits_gathered(n_s, n_c, s_dev, r_dev, cells, group_pairs, models_count):
        return gathered_call(n_s, n_c, *arrays)
    dma = pltpu.SemaphoreType.DMA
    return pl.pallas_call(
        functools.partial(kernel_body, n_s, n_c),
        out_shape=(
            pltpu.VMEM((own, cells), F32),
            pltpu.VMEM((share, models_count), F32),
        ),
        in_specs=[pl.BlockSpec(memory_space=pltpu.HBM)] * 7,
        out_specs=[pl.BlockSpec(memory_space=pltpu.VMEM)] * 2,
        scratch_shapes=[
            pltpu.VMEM((s_dev, cells), BF16),
            pltpu.VMEM((r_dev, cells), BF16),
            pltpu.VMEM((1, cells), jnp.int32),
            pltpu.VMEM((own, cells), BF16),
            pltpu.VMEM((share, models_count), BF16),
            pltpu.VMEM((n_s, s_dev + r_dev, cells), BF16),
            pltpu.VMEM((n_s, 2, 1, group_pairs), jnp.int32),
            pltpu.VMEM((n_s, own, share), BF16),
            pltpu.VMEM((n_s, own, share), BF16),
            pltpu.VMEM((pairs_all, n_s * (s_dev + r_dev)), BF16),
            pltpu.VMEM((pairs_all, cells), BF16),
            pltpu.VMEM((HSTEPS + 1, n_c, own, chunk), BF16),
            pltpu.VMEM((HSTEPS + 1, n_c, own, chunk), BF16),
            pltpu.VMEM((HSTEPS, n_c, own, chunk), BF16),
            pltpu.VMEM((HSTEPS, 8, own), F32),
            pltpu.VMEM((HSTEPS, n_c, 8, own), F32),
            pltpu.VMEM((n_s, own, share), F32),
            pltpu.VMEM((n_s, own, share), F32),
            pltpu.VMEM((own, pairs_all), BF16),
            pltpu.VMEM((n_c, own, chunk), F32),
            pltpu.VMEM((HSTEPS, own, cells), F32),
            dma((7,)), dma((3, n_s)), dma((3, n_s)),
            dma((HSTEPS + 1, n_c)), dma((HSTEPS + 1, n_c)),
            dma((HSTEPS, n_c)), dma((HSTEPS, n_c)),
            dma((HSTEPS, n_c)), dma((HSTEPS, n_c)),
            dma((n_s,)), dma((n_s,)),
        ],
        compiler_params=pltpu.CompilerParams(
            collective_id=0, has_side_effects=True, vmem_limit_bytes=60 * 1024 * 1024
        ),
    )(*arrays)


def solution(mesh):
    return jax.shard_map(
        shards,
        mesh=mesh,
        in_specs=(
            P("src", "cell"),
            P("src", "cell"),
            P("src"),
            P("src"),
            P("cell", None),
            P(None, "cell"),
            P("src", None),
        ),
        out_specs=(P("src", "cell"), P(("src", "cell"), None)),
        check_vma=False,
    )
```

```python
import functools
import math

import jax
import jax.numpy as jnp
from jax import lax
from jax.experimental import pallas as pl
from jax.experimental.pallas import tpu as pltpu
from jax.sharding import PartitionSpec as P

HSTEPS = 2
MESH = pl.DeviceIdType.MESH
F32 = jnp.float32
BF16 = jnp.bfloat16
NT = (((1,), (1,)), ((), ()))


def each(count, body):
    if count <= 8:
        for i in range(count - 1, 0, -1):
            body(i)
    else:

        def step(i, carry):
            body(count - i)
            return carry

        lax.fori_loop(1, count, step, 0)


def kernel_body(
    n_s, n_c,
    gs, gr, ps, pr, order, models, noise,
    rec_out, res_out,
    gs_in, gr_in, order_in, models_in, noise_in,
    fields, indices, nz_send, nz_recv,
    picks, oper, rs_send, rs_recv, ag, stat_send, stat_recv,
    fin_send, fin_recv, wlow, res, grads,
    load, in_send, in_recv, rs_ssem, rs_rsem, ag_ssem, ag_rsem, st_ssem, st_rsem, fin_ssem, fin_rsem,
):
    s = lax.axis_index("src")
    c = lax.axis_index("cell")
    group_pairs = ps.shape[1]
    cells = gs.shape[1]
    models_count = models.shape[0]
    own = models_count // n_s
    share = group_pairs // n_c
    chunk = share * n_s
    pairs_all = group_pairs * n_s
    s_dev = gs.shape[0]
    r_dev = gr.shape[0]
    scale = 1.0 / math.sqrt(cells * n_c)

    def src_peer(j):
        return jnp.bitwise_xor(s, j)

    def cell_peer(j):
        return jnp.bitwise_xor(c, j)

    def to_src(src_ref, dst_ref, ssem, rsem, peer):
        return pltpu.make_async_remote_copy(
            src_ref=src_ref, dst_ref=dst_ref, send_sem=ssem, recv_sem=rsem,
            device_id={"src": peer}, device_id_type=MESH,
        )

    def to_cell(src_ref, dst_ref, ssem, rsem, peer):
        return pltpu.make_async_remote_copy(
            src_ref=src_ref, dst_ref=dst_ref, send_sem=ssem, recv_sem=rsem,
            device_id={"cell": peer}, device_id_type=MESH,
        )

    barrier = pltpu.get_barrier_semaphore()
    each(n_s, lambda j: pl.semaphore_signal(
        barrier, inc=1, device_id={"src": src_peer(j)}, device_id_type=MESH))
    each(n_c, lambda j: pl.semaphore_signal(
        barrier, inc=1, device_id={"cell": cell_peer(j)}, device_id_type=MESH))

    loads = [
        pltpu.make_async_copy(order, order_in, load.at[0]),
        pltpu.make_async_copy(gs, gs_in, load.at[1]),
        pltpu.make_async_copy(gr, gr_in, load.at[2]),
        pltpu.make_async_copy(ps, indices.at[s, 0], load.at[3]),
        pltpu.make_async_copy(pr, indices.at[s, 1], load.at[4]),
        pltpu.make_async_copy(
            noise.at[pl.ds(pl.multiple_of(c * share, share), share), :], noise_in, load.at[5]),
        pltpu.make_async_copy(
            models.at[pl.ds(pl.multiple_of(s * own, own), own), :], models_in, load.at[6]),
    ]
    for copy in loads:
        copy.start()
    for copy in loads:
        copy.wait()
    rows = lax.broadcasted_iota(jnp.int32, (cells, cells), 0)
    select = jnp.where(rows == order_in[...], 1.0, 0.0).astype(BF16)
    raw = jnp.concatenate([gs_in[...].astype(F32), gr_in[...].astype(F32)], axis=0).astype(BF16)
    fields[s] = jnp.dot(raw, select, preferred_element_type=F32).astype(BF16)
    nz_send[...] = noise_in[...].astype(F32).T.reshape(n_s, own, share).astype(BF16)
    nz_recv[s] = nz_send[s]

    pl.semaphore_wait(barrier, n_s + n_c - 2)

    def in_copies(j, slot, which=(0, 1, 2)):
        peer = src_peer(j)
        makers = [
            lambda: to_src(fields.at[slot], fields.at[slot], in_send.at[0, j], in_recv.at[0, j], peer),
            lambda: to_src(indices.at[slot], indices.at[slot], in_send.at[1, j], in_recv.at[1, j], peer),
            lambda: to_src(nz_send.at[peer], nz_recv.at[slot], in_send.at[2, j], in_recv.at[2, j], peer),
        ]
        return [makers[n]() for n in which]

    each(n_s, lambda j: in_copies(j, s, (1,))[0].start())
    each(n_s, lambda j: in_copies(j, s, (0,))[0].start())
    each(n_s, lambda j: in_copies(j, s, (2,))[0].start())

    dev_rows = s_dev + r_dev
    field_rows = n_s * dev_rows
    row = lax.broadcasted_iota(jnp.int32, (field_rows, 1), 0)
    group = jnp.zeros((field_rows, 1), jnp.int32)
    for k in range(1, n_s):
        group = group + jnp.where(row >= k * dev_rows, 1, 0)
    within = row - group * dev_rows
    is_source = within < s_dev
    source_id = jnp.where(is_source, group * s_dev + within, -1)
    receiver_id = jnp.where(is_source, -1, group * r_dev + within - s_dev)

    each(n_s, lambda j: in_copies(j, src_peer(j), (1,))[0].wait_recv())

    for k in range(n_s):
        hit = (source_id == indices[k, 0] + k * s_dev) | (receiver_id == indices[k, 1])
        pick = jnp.where(hit, 1.0, 0.0).T.astype(BF16)
        for t in range(n_c):
            at = t * chunk + k * share
            picks[at : at + share, :] = pick[t * share : (t + 1) * share]
    each(n_s, lambda j: in_copies(j, src_peer(j), (0,))[0].wait_recv())
    every = fields[...].astype(F32).reshape(field_rows, cells)
    source_cols = jnp.where(is_source, every, 0.0).astype(BF16)
    receiver_cols = jnp.where(is_source, 0.0, every).astype(BF16)

    def build(k):
        at = pl.multiple_of(k * chunk, chunk)
        pick = picks[pl.ds(at, chunk), :]
        block = (
            jnp.dot(pick, source_cols, preferred_element_type=F32)
            * jnp.dot(pick, receiver_cols, preferred_element_type=F32)
        ).astype(BF16)
        oper[pl.ds(at, chunk), :] = block
        return block

    def rs_copy(phase, j, target):
        return to_cell(
            rs_send.at[phase, target], rs_recv.at[phase, j],
            rs_ssem.at[phase, j], rs_rsem.at[phase, j], target,
        )

    def forward(phase, low, after_sends):
        def part(k):
            at = pl.multiple_of(k * chunk, chunk)
            block = build(k) if phase == 0 else oper[pl.ds(at, chunk), :]
            return lax.dot_general(low, block, NT, preferred_element_type=F32)

        def one(j):
            target = cell_peer(j)
            rs_send[phase, target] = part(target).astype(BF16)
            rs_copy(phase, j, target).start()

        each(n_c, one)
        after_sends()
        rs_total = part(c)
        each(n_c, lambda j: rs_copy(phase, j, cell_peer(j)).wait_recv())
        for j in range(1, n_c):
            rs_total = rs_total + rs_recv[phase, j].astype(F32)
        return rs_total * scale

    def ag_copy(phase, j, slot):
        return to_cell(
            ag.at[phase, slot], ag.at[phase, slot],
            ag_ssem.at[phase, j], ag_rsem.at[phase, j], cell_peer(j),
        )

    def gather(phase, value):
        ag[phase, c] = value.astype(BF16)
        each(n_c, lambda j: ag_copy(phase, j, c).start())
        each(n_c, lambda j: ag_copy(phase, j, cell_peer(j)).wait_recv())
        return ag[phase].astype(F32)

    def stat_copy(step, j):
        return to_cell(
            stat_send.at[step], stat_recv.at[step, j],
            st_ssem.at[step, j], st_rsem.at[step, j], cell_peer(j),
        )

    diagonal = lax.broadcasted_iota(jnp.int32, (own, own), 0) == lax.broadcasted_iota(
        jnp.int32, (own, own), 1
    )

    def to_row(column):
        return jnp.sum(jnp.where(diagonal, column, 0.0), axis=0, keepdims=True)

    def to_column(row):
        return jnp.sum(jnp.where(diagonal, row, 0.0), axis=1, keepdims=True)

    def stat_start(step, first, second):
        top = lax.broadcasted_iota(jnp.int32, (8, own), 0) == 0
        stat_send[step] = jnp.where(top, to_row(first), to_row(second))
        each(n_c, lambda j: stat_copy(step, j).start())

    def stat_total(step):
        each(n_c, lambda j: stat_copy(step, j).wait_recv())
        total = stat_send[step]
        for j in range(1, n_c):
            total = total + stat_recv[step, j]
        return to_column(total[0:1]), to_column(total[1:2])

    own_models = models_in[...]
    first_data = forward(0, own_models, lambda: None)
    each(n_s, lambda j: in_copies(j, src_peer(j), (2,))[0].wait_recv())
    own_noise = jnp.concatenate([nz_recv[k].astype(F32) for k in range(n_s)], axis=1)
    chunk_res = -(first_data + own_noise)
    res[...] = gather(0, chunk_res)

    def pair_sum(values):
        return jnp.sum(jnp.sum(values, axis=0), axis=1, keepdims=True)

    alphas = []
    for step in range(HSTEPS):
        last = step == HSTEPS - 1
        full = res[...]
        spread = pair_sum(full * full)
        delta = jnp.sqrt(spread / pairs_all + 1e-06)
        weight = delta[None] / jnp.maximum(jnp.abs(full), delta[None])
        weighted = weight * full
        for k in range(n_c):
            wlow[:, k * chunk : (k + 1) * chunk] = weighted[k].astype(BF16)
        grad = jnp.dot(wlow[...], oper[...], preferred_element_type=F32) * scale
        after = []

        def send_numer():
            grads[step] = grad
            numer_own = jnp.sum(grad * grad, axis=1, keepdims=True)
            after.append(numer_own)
            if last:
                after.append(delta / jnp.maximum(jnp.abs(chunk_res), delta))
            else:
                stat_start(step, numer_own, numer_own)

        image = forward(step + 1, grad.astype(BF16), send_numer)
        if last:
            curve_own = jnp.sum(after[1] * image * image, axis=1, keepdims=True)
            stat_start(step, after[0], curve_own)
            numer, curvature = stat_total(step)
            alpha = numer / (curvature + 1e-06)
        else:
            images = gather(step + 1, image)
            numer, _ = stat_total(step)
            curvature = pair_sum(weight * images * images)
            alpha = numer / (curvature + 1e-06)
            res[...] = full - alpha[None] * images
        chunk_res = chunk_res - alpha * image
        alphas.append(alpha)

    for k in range(n_s):
        fin_send[k] = chunk_res[:, k * share : (k + 1) * share]

    def fin_copy(j, slot):
        return to_src(
            fin_send.at[src_peer(j)], fin_recv.at[slot], fin_ssem.at[j], fin_rsem.at[j], src_peer(j)
        )

    each(n_s, lambda j: fin_copy(j, s).start())
    fin_recv[s] = fin_send[s]
    total_rec = -(alphas[0] * grads[0])
    for step in range(1, HSTEPS):
        total_rec = total_rec - alphas[step] * grads[step]
    rec_out[...] = total_rec

    def in_done(j):
        for copy in in_copies(j, s):
            copy.wait_send()

    each(n_s, in_done)
    for phase in range(HSTEPS + 1):
        each(n_c, lambda j, phase=phase: rs_copy(phase, j, cell_peer(j)).wait_send())
    for phase in range(HSTEPS):
        each(n_c, lambda j, phase=phase: ag_copy(phase, j, c).wait_send())
        each(n_c, lambda j, phase=phase: stat_copy(phase, j).wait_send())
    each(n_s, lambda j: fin_copy(j, src_peer(j)).wait_recv())
    res_out[...] = fin_recv[...].reshape(models_count, share).T
    each(n_s, lambda j: fin_copy(j, s).wait_send())


def split_pair(value, lanes):
    high = value.astype(BF16).astype(F32)
    lane = lax.broadcasted_iota(jnp.int32, value.shape, 1)
    return jnp.where(lane < lanes, high, value - high)


def gathered_body(
    n_s, n_c,
    gs, gr, ps, pr, order, models, noise,
    out,
    gs_in, gr_in, order_in, models_in, noise_in,
    fields, indices, nz_send, nz_recv, md_send, md_recv,
    gs_all, gs_low, gr_all, mask, onehot, pair_rows,
    noise_masked, x_send, x_recv, fin_send, fin_recv,
    load, f_ssem, f_rsem, i_ssem, i_rsem, m_ssem, m_rsem, x_ssem, x_rsem, fin_ssem, fin_rsem,
):
    s = lax.axis_index("src")
    c = lax.axis_index("cell")
    pairs = ps.shape[1]
    cells = gs.shape[1]
    s_dev = gs.shape[0]
    r_dev = gr.shape[0]
    own = models.shape[0] // n_s
    mine = own // n_c
    half = cells // 2
    sources = n_s * s_dev
    receivers = n_s * r_dev
    pairs_all = pairs * n_s
    scale = 1.0 / math.sqrt(cells * n_c)

    def src_peer(j):
        return jnp.bitwise_xor(s, j)

    def cell_peer(j):
        return jnp.bitwise_xor(c, j)

    def remote(src_ref, dst_ref, ssem, rsem, ds, dc):
        return pltpu.make_async_remote_copy(
            src_ref=src_ref, dst_ref=dst_ref, send_sem=ssem, recv_sem=rsem,
            device_id={"src": src_peer(ds), "cell": cell_peer(dc)}, device_id_type=MESH,
        )

    barrier = pltpu.get_barrier_semaphore()
    each(n_c, lambda j: pl.semaphore_signal(
        barrier, inc=1, device_id={"cell": cell_peer(j)}, device_id_type=MESH))
    each(n_s, lambda j: pl.semaphore_signal(
        barrier, inc=1, device_id={"src": src_peer(j)}, device_id_type=MESH))

    loads = [
        pltpu.make_async_copy(order, order_in, load.at[0]),
        pltpu.make_async_copy(gs, gs_in, load.at[1]),
        pltpu.make_async_copy(gr, gr_in, load.at[2]),
        pltpu.make_async_copy(ps, indices.at[s, 0], load.at[3]),
        pltpu.make_async_copy(pr, indices.at[s, 1], load.at[4]),
        pltpu.make_async_copy(
            models.at[pl.ds(pl.multiple_of(s * own, own), own), :], models_in, load.at[5]),
        pltpu.make_async_copy(noise, noise_in, load.at[6]),
    ]
    for copy in loads:
        copy.start()
    for copy in loads[:5]:
        copy.wait()
    rows = lax.broadcasted_iota(jnp.int32, (cells, cells), 0)
    select = jnp.where(rows == order_in[...], 1.0, 0.0).astype(BF16)
    raw = jnp.concatenate([gs_in[...].astype(F32), gr_in[...].astype(F32)], axis=0).astype(BF16)
    fields[c, s] = jnp.dot(raw, select, preferred_element_type=F32).astype(BF16)

    for copy in loads[5:]:
        copy.wait()
    wide = 2 * mine
    q = lax.broadcasted_iota(jnp.int32, (n_c * wide, own), 0)
    m = lax.broadcasted_iota(jnp.int32, (n_c * wide, own), 1)
    spread_rows = jnp.where((q % mine) * n_c + q // wide == m, 1.0, 0.0).astype(BF16)
    placed = jnp.dot(spread_rows, models_in[...], preferred_element_type=F32)
    low = lax.broadcasted_iota(jnp.int32, (n_c * wide, half), 0) % wide < mine
    placed = jnp.where(low, placed[:, :half], placed[:, half:])
    md_send[...] = placed.astype(BF16).reshape(n_c, wide, half)
    md_recv[c] = md_send[c]
    q = lax.broadcasted_iota(jnp.int32, (n_s * wide, models.shape[0]), 0)
    m = lax.broadcasted_iota(jnp.int32, (n_s * wide, models.shape[0]), 1)
    columns = jnp.where(
        ((q // wide) * own + (q % wide) * n_c + c == m) & (q % wide < mine), 1.0, 0.0).astype(BF16)
    nz = lax.dot_general(columns, noise_in[...], NT, preferred_element_type=F32)
    nz_send[...] = nz.astype(BF16).reshape(n_s, wide, pairs)
    nz_recv[s] = nz_send[s]

    pl.semaphore_wait(barrier, n_s + n_c - 2)

    done = []
    count = [0]

    def send_block(t, g, ds, dc):
        at = count[0]
        count[0] += 1
        copy = remote(fields.at[t, g], fields.at[t, g], f_ssem.at[at], f_rsem.at[t, g], ds, dc)
        copy.start()
        done.append(copy.wait_send)

    def got_block(t, g):
        remote(fields.at[t, g], fields.at[t, g], f_ssem.at[0], f_rsem.at[t, g], 0, 1).wait_recv()

    def index_copy(j, slot):
        return remote(indices.at[slot], indices.at[slot], i_ssem.at[0, j], i_rsem.at[0, j], j, 0)

    def noise_copy(j):
        return remote(
            nz_send.at[src_peer(j)], nz_recv.at[s], i_ssem.at[1, j], i_rsem.at[1, j], j, 0)

    def noise_got(j):
        g = src_peer(j)
        remote(nz_send.at[g], nz_recv.at[g], i_ssem.at[1, j], i_rsem.at[1, j], j, 0).wait_recv()

    def model_copy(j):
        return remote(md_send.at[cell_peer(j)], md_recv.at[c], m_ssem.at[j], m_rsem.at[j], 0, j)

    def model_got(j):
        t = cell_peer(j)
        remote(md_send.at[t], md_recv.at[t], m_ssem.at[j], m_rsem.at[j], 0, j).wait_recv()

    steps = range(2, n_c, 2)
    across = n_s - 1
    near = range(1, across)
    send_block(c, s, across, 0)
    for d in steps:
        send_block(c, s, 0, d)
    for j in near:
        send_block(c, s, j, 0)
    send_block(c, s, 0, 1)
    each(n_s, lambda j: index_copy(j, s).start())

    each(n_c, lambda j: model_copy(j).start())
    each(n_s, lambda j: noise_copy(j).start())

    g = src_peer(across)
    got_block(c, g)
    for d in steps:
        send_block(c, g, 0, d)
    send_block(c, g, 0, 1)
    for d in steps:
        t = cell_peer(d)
        got_block(t, s)
        for j in near:
            send_block(t, s, j, 0)
        send_block(t, s, 0, 1)

    each(n_s, lambda j: index_copy(j, src_peer(j)).wait_recv())
    row = lax.broadcasted_iota(jnp.int32, (2 * receivers, pairs), 0)
    row = jnp.where(row < receivers, row, row - receivers)
    source = lax.broadcasted_iota(jnp.int32, (s_dev, pairs), 0)
    for g in range(n_s):
        mask[g] = jnp.where(source == indices[g, 0], 1.0, 0.0)
        hit = jnp.where(row == indices[g, 1], 1.0, 0.0)
        onehot[g] = hit.astype(BF16)
        pair_rows[g] = hit.T.astype(BF16)

    def unpack(t):
        block = fields[t].astype(F32)
        gs_all[t] = block[:, :s_dev].reshape(sources, cells)
        gs_low[t] = block[:, :s_dev].reshape(sources, cells).astype(BF16)
        part = block[:, s_dev:].reshape(receivers, cells).astype(BF16)
        gr_all[t] = jnp.concatenate([part, part], axis=0)

    def forward(t, lines):
        base = gs_low[t]
        left = jnp.concatenate([base * line.astype(BF16) for line in lines], axis=0)
        return lax.dot_general(left, gr_all[t], NT, preferred_element_type=F32)

    data = [None]

    def first(d):
        t = cell_peer(d)
        unpack(t)
        if d:
            model_got(d)
        line = md_recv[t].astype(F32)
        lines = [
            jnp.concatenate([line[j : j + 1], line[mine + j : mine + j + 1]], axis=1)
            for j in range(mine)
        ]
        part = forward(t, lines)
        data[0] = part if data[0] is None else data[0] + part

    def own_core(d):
        t = cell_peer(d)
        for j in near if d == 0 else range(1, n_s):
            g = src_peer(j)
            got_block(t, g)
            send_block(t, g, 0, 1)
        first(d)

    def other_core(d):
        t = cell_peer(d + 1)
        for j in range(n_s):
            got_block(t, src_peer(j))
        first(d + 1)

    own_core(0)
    each(n_s, noise_got)
    for g in range(n_s):
        line = nz_recv[g].astype(F32)
        for j in range(mine):
            noise_masked[g, j * s_dev : (j + 1) * s_dev] = line[j : j + 1] * mask[g]
    for d in steps:
        own_core(d)
        other_core(d - 2)
    other_core(n_c - 2)

    def to_pairs(value):
        mixed = split_pair(value * scale, receivers).reshape(mine, n_s, s_dev, 2 * receivers)
        out = []
        for g in range(n_s):
            left = mixed[:, g].reshape(mine * s_dev, 2 * receivers).astype(BF16)
            at_pairs = jnp.dot(left, onehot[g], preferred_element_type=F32)
            out.append(at_pairs.reshape(mine, s_dev, pairs) * mask[g][None])
        return out

    def from_pairs(values):
        out = [
            jnp.dot(
                values[g].reshape(mine * s_dev, pairs).astype(BF16), pair_rows[g],
                preferred_element_type=F32).reshape(mine, 1, s_dev, 2 * receivers)
            for g in range(n_s)
        ]
        whole = jnp.concatenate(out, axis=1).reshape(mine * sources, 2 * receivers)
        return split_pair(whole * scale, receivers).astype(BF16)

    def pair_sum(values):
        total = values[0]
        for value in values[1:]:
            total = total + value
        return jnp.sum(jnp.sum(total, axis=1, keepdims=True), axis=2, keepdims=True)

    def x_copy(step, j):
        return remote(
            x_send.at[step, cell_peer(j)], x_recv.at[step, c],
            x_ssem.at[step, j], x_rsem.at[step, j], 0, j)

    def x_got(step, j):
        t = cell_peer(j)
        remote(
            x_send.at[step, t], x_recv.at[step, t],
            x_ssem.at[step, j], x_rsem.at[step, j], 0, j).wait_recv()

    first_data = to_pairs(data[0])
    res = [-(value + noise_masked[g].reshape(mine, s_dev, pairs)) for g, value in enumerate(first_data)]

    place = lax.broadcasted_iota(jnp.int32, (wide, half), 0)
    farthest = [d + k for d in range(n_c - 2, -1, -2) for k in (1, 0)]
    alphas = []
    for step in range(HSTEPS):
        delta = jnp.sqrt(pair_sum([value * value for value in res]) / pairs_all + 1e-06)
        weight = [delta / jnp.maximum(jnp.abs(value), delta) for value in res]
        back = from_pairs([w * value for w, value in zip(weight, res)])
        numer = None
        data = None
        for d in farthest:
            t = cell_peer(d)
            fan = jnp.dot(back, gr_all[t], preferred_element_type=F32)
            grad = jnp.sum(
                fan.reshape(mine, sources, cells) * gs_all[t][None], axis=1, keepdims=True)
            square = grad * grad
            numer = square if numer is None else numer + square
            low = grad.astype(BF16).astype(F32)
            part = forward(t, [low[j] for j in range(mine)])
            data = part if data is None else data + part
            packed = jnp.zeros((wide, half), F32)
            for j in range(mine):
                packed = jnp.where(place == j, low[j][:, :half], packed)
                packed = jnp.where(place == mine + j, low[j][:, half:], packed)
            x_send[step, t] = packed.astype(BF16)
        x_recv[step, c] = x_send[step, c]
        image = to_pairs(data)
        curvature = pair_sum([w * value * value for w, value in zip(weight, image)])
        alpha = jnp.sum(numer, axis=2, keepdims=True) / (curvature + 1e-06)
        res = [value - alpha * other for value, other in zip(res, image)]
        alphas.append(alpha)
        if step < HSTEPS - 1:
            for d in farthest:
                if d:
                    x_copy(step, d).start()

    odd = c % 2
    two = 2 * (pairs // n_c)
    room = two // (2 * mine)
    lane = lax.broadcasted_iota(jnp.int32, (1, two), 1)
    marks = jnp.zeros((1, two), F32)
    for j in range(mine):
        for step in range(HSTEPS):
            marks = jnp.where(lane // room == 2 * j + step, alphas[step][j], marks)
    for g in range(n_s):
        lines = jnp.sum(res[g], axis=1, keepdims=True)
        for h in range(n_c // 2):
            fin_send[g, h] = jnp.concatenate(
                [lines[j][:, h * two : (h + 1) * two] for j in range(mine)] + [marks], axis=1)

    others = n_s * n_c

    def fin_start(i, carry):
        a, b = (others - i) // n_c, (others - i) % n_c
        remote(
            fin_send.at[src_peer(a), cell_peer(b) // 2], fin_recv.at[s * n_c + c],
            fin_ssem.at[0], fin_rsem.at[0], a, b).start()
        return carry

    lax.fori_loop(1, n_c * (n_s - 1) + 1, fin_start, 0)
    for d in farthest:
        if d:
            x_copy(HSTEPS - 1, d).start()
    lax.fori_loop(n_c * (n_s - 1) + 1, others, fin_start, 0)
    fin_recv[s * n_c + c] = fin_send[s, c // 2]

    m = lax.broadcasted_iota(jnp.int32, (own, n_c * wide), 0)
    q = lax.broadcasted_iota(jnp.int32, (own, n_c * wide), 1)
    at = (m % n_c) * wide + m // n_c
    rows_of = [jnp.where(q == at + k * mine, 1.0, 0.0).astype(BF16) for k in (0, 1)]
    grads = []
    for step in range(HSTEPS):
        for j in range(n_c - 1, 0, -1):
            x_got(step, j)
        blocks = x_recv[step].astype(F32).reshape(n_c * wide, half).astype(BF16)
        grads.append(jnp.concatenate(
            [jnp.dot(pick, blocks, preferred_element_type=F32) for pick in rows_of], axis=1))

    for wait in done:
        wait()
    each(n_s, lambda j: index_copy(j, s).wait_send())
    each(n_c, lambda j: model_copy(j).wait_send())
    each(n_s, lambda j: noise_copy(j).wait_send())
    for step in range(HSTEPS):
        each(n_c, lambda j, step=step: x_copy(step, j).wait_send())

    rest = fin_recv.at[pl.ds(0, n_s * n_c - 1)]
    fin_all = remote(rest, rest, fin_ssem.at[0], fin_rsem.at[0], 0, 1)
    fin_all.wait_recv()
    notes = fin_recv[pl.ds(s * n_c, n_c), 0, mine * two :]
    for j in range(mine):
        at = pl.ds(j * n_c, n_c)
        here = slice(j * n_c, (j + 1) * n_c)
        first_of, second_of = (
            notes[:, (2 * j + step) * room : (2 * j + step) * room + 1] for step in range(HSTEPS))
        out[at, :] = -(first_of * grads[0][here] + second_of * grads[1][here])
    lines = jnp.concatenate(
        [
            fin_recv[:, 0, j * two : (j + 1) * two].reshape(n_s, 1, n_c, two)
            for j in range(mine)
        ], axis=1).reshape(n_s * own, two).T
    lines = jnp.where(odd == 0, lines[: two // 2], lines[two // 2 :])
    tall = out.shape[0] - own
    for k in range(lines.shape[0] // tall):
        out[own:, k * lines.shape[1] : (k + 1) * lines.shape[1]] = lines[k * tall : (k + 1) * tall]
    fin_all.wait_send()


def gathered_call(n_s, n_c, *arrays):
    gs, gr, ps, _, order, models, noise = arrays
    s_dev, cells = gs.shape
    r_dev = gr.shape[0]
    pairs = ps.shape[1]
    models_count = models.shape[0]
    own = models_count // n_s
    wide = 2 * (own // n_c)
    share = pairs // n_c
    dma = pltpu.SemaphoreType.DMA
    tall = share * models_count // cells
    out = pl.pallas_call(
        functools.partial(gathered_body, n_s, n_c),
        out_shape=pltpu.VMEM((own + tall, cells), F32),
        in_specs=[pl.BlockSpec(memory_space=pltpu.HBM)] * 7,
        out_specs=pl.BlockSpec(memory_space=pltpu.VMEM),
        scratch_shapes=[
            pltpu.VMEM((s_dev, cells), BF16),
            pltpu.VMEM((r_dev, cells), BF16),
            pltpu.VMEM((1, cells), jnp.int32),
            pltpu.VMEM((own, cells), BF16),
            pltpu.VMEM((pairs, models_count), BF16),
            pltpu.VMEM((n_c, n_s, s_dev + r_dev, cells), BF16),
            pltpu.VMEM((n_s, 2, 1, pairs), jnp.int32),
            pltpu.VMEM((n_s, wide, pairs), BF16),
            pltpu.VMEM((n_s, wide, pairs), BF16),
            pltpu.VMEM((n_c, wide, cells // 2), BF16),
            pltpu.VMEM((n_c, wide, cells // 2), BF16),
            pltpu.VMEM((n_c, n_s * s_dev, cells), F32),
            pltpu.VMEM((n_c, n_s * s_dev, cells), BF16),
            pltpu.VMEM((n_c, 2 * n_s * r_dev, cells), BF16),
            pltpu.VMEM((n_s, s_dev, pairs), F32),
            pltpu.VMEM((n_s, 2 * n_s * r_dev, pairs), BF16),
            pltpu.VMEM((n_s, pairs, 2 * n_s * r_dev), BF16),
            pltpu.VMEM((n_s, wide // 2 * s_dev, pairs), F32),
            pltpu.VMEM((HSTEPS, n_c, wide, cells // 2), BF16),
            pltpu.VMEM((HSTEPS, n_c, wide, cells // 2), BF16),
            pltpu.VMEM((n_s, n_c // 2, 1, (wide // 2 + 1) * 2 * share), F32),
            pltpu.VMEM((n_s * n_c, 1, (wide // 2 + 1) * 2 * share), F32),
            dma((7,)), dma((n_s * n_c,)), dma((n_c, n_s)),
            dma((2, n_s)), dma((2, n_s)),
            dma((n_c,)), dma((n_c,)),
            dma((HSTEPS, n_c)), dma((HSTEPS, n_c)),
            dma((1,)), dma((1,)),
        ],
        compiler_params=pltpu.CompilerParams(
            collective_id=0, has_side_effects=True, vmem_limit_bytes=60 * 1024 * 1024
        ),
    )(*arrays)
    pieces = [
        out[own:, k * models_count : (k + 1) * models_count] for k in range(cells // models_count)
    ]
    return out[:own], jnp.concatenate(pieces, axis=0)


def fits_gathered(n_s, n_c, s_dev, r_dev, cells, pairs, models_count):
    return (
        n_c & (n_c - 1) == 0 and n_s == 4
        and models_count == 4 * n_s * n_c
        and s_dev == 8 and r_dev % 8 == 0 and 2 * n_s * r_dev == 128
        and pairs == 64 * n_c and cells % 256 == 0
        and cells % models_count == 0 and 64 * models_count == 8 * cells
    )


def shards(
    green_source, green_receiver, pair_source, pair_receiver, cell_order, test_models, data_noise
):
    n_s = lax.axis_size("src")
    n_c = lax.axis_size("cell")
    s_dev, cells = green_source.shape
    r_dev = green_receiver.shape[0]
    group_pairs = pair_source.shape[0]
    models_count = test_models.shape[0]
    own = models_count // n_s
    share = group_pairs // n_c
    chunk = share * n_s
    pairs_all = group_pairs * n_s
    arrays = (
        green_source, green_receiver, pair_source[None, :], pair_receiver[None, :],
        cell_order, test_models, data_noise,
    )
    if fits_gathered(n_s, n_c, s_dev, r_dev, cells, group_pairs, models_count):
        return gathered_call(n_s, n_c, *arrays)
    dma = pltpu.SemaphoreType.DMA
    return pl.pallas_call(
        functools.partial(kernel_body, n_s, n_c),
        out_shape=(
            pltpu.VMEM((own, cells), F32),
            pltpu.VMEM((share, models_count), F32),
        ),
        in_specs=[pl.BlockSpec(memory_space=pltpu.HBM)] * 7,
        out_specs=[pl.BlockSpec(memory_space=pltpu.VMEM)] * 2,
        scratch_shapes=[
            pltpu.VMEM((s_dev, cells), BF16),
            pltpu.VMEM((r_dev, cells), BF16),
            pltpu.VMEM((1, cells), jnp.int32),
            pltpu.VMEM((own, cells), BF16),
            pltpu.VMEM((share, models_count), BF16),
            pltpu.VMEM((n_s, s_dev + r_dev, cells), BF16),
            pltpu.VMEM((n_s, 2, 1, group_pairs), jnp.int32),
            pltpu.VMEM((n_s, own, share), BF16),
            pltpu.VMEM((n_s, own, share), BF16),
            pltpu.VMEM((pairs_all, n_s * (s_dev + r_dev)), BF16),
            pltpu.VMEM((pairs_all, cells), BF16),
            pltpu.VMEM((HSTEPS + 1, n_c, own, chunk), BF16),
            pltpu.VMEM((HSTEPS + 1, n_c, own, chunk), BF16),
            pltpu.VMEM((HSTEPS, n_c, own, chunk), BF16),
            pltpu.VMEM((HSTEPS, 8, own), F32),
            pltpu.VMEM((HSTEPS, n_c, 8, own), F32),
            pltpu.VMEM((n_s, own, share), F32),
            pltpu.VMEM((n_s, own, share), F32),
            pltpu.VMEM((own, pairs_all), BF16),
            pltpu.VMEM((n_c, own, chunk), F32),
            pltpu.VMEM((HSTEPS, own, cells), F32),
            dma((7,)), dma((3, n_s)), dma((3, n_s)),
            dma((HSTEPS + 1, n_c)), dma((HSTEPS + 1, n_c)),
            dma((HSTEPS, n_c)), dma((HSTEPS, n_c)),
            dma((HSTEPS, n_c)), dma((HSTEPS, n_c)),
            dma((n_s,)), dma((n_s,)),
        ],
        compiler_params=pltpu.CompilerParams(
            collective_id=0, has_side_effects=True, vmem_limit_bytes=60 * 1024 * 1024
        ),
    )(*arrays)


def solution(mesh):
    return jax.shard_map(
        shards,
        mesh=mesh,
        in_specs=(
            P("src", "cell"),
            P("src", "cell"),
            P("src"),
            P("src"),
            P("cell", None),
            P(None, "cell"),
            P("src", None),
        ),
        out_specs=(P("src", "cell"), P(("src", "cell"), None)),
        check_vma=False,
    )
```

```python
import functools
import math

import jax
import jax.numpy as jnp
from jax import lax
from jax.experimental import pallas as pl
from jax.experimental.pallas import tpu as pltpu
from jax.sharding import PartitionSpec as P

HSTEPS = 2
MESH = pl.DeviceIdType.MESH
F32 = jnp.float32
BF16 = jnp.bfloat16
NT = (((1,), (1,)), ((), ()))


def each(count, body):
    if count <= 8:
        for i in range(count - 1, 0, -1):
            body(i)
    else:

        def step(i, carry):
            body(count - i)
            return carry

        lax.fori_loop(1, count, step, 0)


def kernel_body(
    n_s, n_c,
    gs, gr, ps, pr, order, models, noise,
    rec_out, res_out,
    gs_in, gr_in, order_in, models_in, noise_in,
    fields, indices, nz_send, nz_recv,
    picks, oper, rs_send, rs_recv, ag, stat_send, stat_recv,
    fin_send, fin_recv, wlow, res, grads,
    load, in_send, in_recv, rs_ssem, rs_rsem, ag_ssem, ag_rsem, st_ssem, st_rsem, fin_ssem, fin_rsem,
):
    s = lax.axis_index("src")
    c = lax.axis_index("cell")
    group_pairs = ps.shape[1]
    cells = gs.shape[1]
    models_count = models.shape[0]
    own = models_count // n_s
    share = group_pairs // n_c
    chunk = share * n_s
    pairs_all = group_pairs * n_s
    s_dev = gs.shape[0]
    r_dev = gr.shape[0]
    scale = 1.0 / math.sqrt(cells * n_c)

    def src_peer(j):
        return jnp.bitwise_xor(s, j)

    def cell_peer(j):
        return jnp.bitwise_xor(c, j)

    def to_src(src_ref, dst_ref, ssem, rsem, peer):
        return pltpu.make_async_remote_copy(
            src_ref=src_ref, dst_ref=dst_ref, send_sem=ssem, recv_sem=rsem,
            device_id={"src": peer}, device_id_type=MESH,
        )

    def to_cell(src_ref, dst_ref, ssem, rsem, peer):
        return pltpu.make_async_remote_copy(
            src_ref=src_ref, dst_ref=dst_ref, send_sem=ssem, recv_sem=rsem,
            device_id={"cell": peer}, device_id_type=MESH,
        )

    barrier = pltpu.get_barrier_semaphore()
    each(n_s, lambda j: pl.semaphore_signal(
        barrier, inc=1, device_id={"src": src_peer(j)}, device_id_type=MESH))
    each(n_c, lambda j: pl.semaphore_signal(
        barrier, inc=1, device_id={"cell": cell_peer(j)}, device_id_type=MESH))

    loads = [
        pltpu.make_async_copy(order, order_in, load.at[0]),
        pltpu.make_async_copy(gs, gs_in, load.at[1]),
        pltpu.make_async_copy(gr, gr_in, load.at[2]),
        pltpu.make_async_copy(ps, indices.at[s, 0], load.at[3]),
        pltpu.make_async_copy(pr, indices.at[s, 1], load.at[4]),
        pltpu.make_async_copy(
            noise.at[pl.ds(pl.multiple_of(c * share, share), share), :], noise_in, load.at[5]),
        pltpu.make_async_copy(
            models.at[pl.ds(pl.multiple_of(s * own, own), own), :], models_in, load.at[6]),
    ]
    for copy in loads:
        copy.start()
    for copy in loads:
        copy.wait()
    rows = lax.broadcasted_iota(jnp.int32, (cells, cells), 0)
    select = jnp.where(rows == order_in[...], 1.0, 0.0).astype(BF16)
    raw = jnp.concatenate([gs_in[...].astype(F32), gr_in[...].astype(F32)], axis=0).astype(BF16)
    fields[s] = jnp.dot(raw, select, preferred_element_type=F32).astype(BF16)
    nz_send[...] = noise_in[...].astype(F32).T.reshape(n_s, own, share).astype(BF16)
    nz_recv[s] = nz_send[s]

    pl.semaphore_wait(barrier, n_s + n_c - 2)

    def in_copies(j, slot, which=(0, 1, 2)):
        peer = src_peer(j)
        makers = [
            lambda: to_src(fields.at[slot], fields.at[slot], in_send.at[0, j], in_recv.at[0, j], peer),
            lambda: to_src(indices.at[slot], indices.at[slot], in_send.at[1, j], in_recv.at[1, j], peer),
            lambda: to_src(nz_send.at[peer], nz_recv.at[slot], in_send.at[2, j], in_recv.at[2, j], peer),
        ]
        return [makers[n]() for n in which]

    each(n_s, lambda j: in_copies(j, s, (1,))[0].start())
    each(n_s, lambda j: in_copies(j, s, (0,))[0].start())
    each(n_s, lambda j: in_copies(j, s, (2,))[0].start())

    dev_rows = s_dev + r_dev
    field_rows = n_s * dev_rows
    row = lax.broadcasted_iota(jnp.int32, (field_rows, 1), 0)
    group = jnp.zeros((field_rows, 1), jnp.int32)
    for k in range(1, n_s):
        group = group + jnp.where(row >= k * dev_rows, 1, 0)
    within = row - group * dev_rows
    is_source = within < s_dev
    source_id = jnp.where(is_source, group * s_dev + within, -1)
    receiver_id = jnp.where(is_source, -1, group * r_dev + within - s_dev)

    each(n_s, lambda j: in_copies(j, src_peer(j), (1,))[0].wait_recv())

    for k in range(n_s):
        hit = (source_id == indices[k, 0] + k * s_dev) | (receiver_id == indices[k, 1])
        pick = jnp.where(hit, 1.0, 0.0).T.astype(BF16)
        for t in range(n_c):
            at = t * chunk + k * share
            picks[at : at + share, :] = pick[t * share : (t + 1) * share]
    each(n_s, lambda j: in_copies(j, src_peer(j), (0,))[0].wait_recv())
    every = fields[...].astype(F32).reshape(field_rows, cells)
    source_cols = jnp.where(is_source, every, 0.0).astype(BF16)
    receiver_cols = jnp.where(is_source, 0.0, every).astype(BF16)

    def build(k):
        at = pl.multiple_of(k * chunk, chunk)
        pick = picks[pl.ds(at, chunk), :]
        block = (
            jnp.dot(pick, source_cols, preferred_element_type=F32)
            * jnp.dot(pick, receiver_cols, preferred_element_type=F32)
        ).astype(BF16)
        oper[pl.ds(at, chunk), :] = block
        return block

    def rs_copy(phase, j, target):
        return to_cell(
            rs_send.at[phase, target], rs_recv.at[phase, j],
            rs_ssem.at[phase, j], rs_rsem.at[phase, j], target,
        )

    def forward(phase, low, after_sends):
        def part(k):
            at = pl.multiple_of(k * chunk, chunk)
            block = build(k) if phase == 0 else oper[pl.ds(at, chunk), :]
            return lax.dot_general(low, block, NT, preferred_element_type=F32)

        def one(j):
            target = cell_peer(j)
            rs_send[phase, target] = part(target).astype(BF16)
            rs_copy(phase, j, target).start()

        each(n_c, one)
        after_sends()
        rs_total = part(c)
        each(n_c, lambda j: rs_copy(phase, j, cell_peer(j)).wait_recv())
        for j in range(1, n_c):
            rs_total = rs_total + rs_recv[phase, j].astype(F32)
        return rs_total * scale

    def ag_copy(phase, j, slot):
        return to_cell(
            ag.at[phase, slot], ag.at[phase, slot],
            ag_ssem.at[phase, j], ag_rsem.at[phase, j], cell_peer(j),
        )

    def gather(phase, value):
        ag[phase, c] = value.astype(BF16)
        each(n_c, lambda j: ag_copy(phase, j, c).start())
        each(n_c, lambda j: ag_copy(phase, j, cell_peer(j)).wait_recv())
        return ag[phase].astype(F32)

    def stat_copy(step, j):
        return to_cell(
            stat_send.at[step], stat_recv.at[step, j],
            st_ssem.at[step, j], st_rsem.at[step, j], cell_peer(j),
        )

    diagonal = lax.broadcasted_iota(jnp.int32, (own, own), 0) == lax.broadcasted_iota(
        jnp.int32, (own, own), 1
    )

    def to_row(column):
        return jnp.sum(jnp.where(diagonal, column, 0.0), axis=0, keepdims=True)

    def to_column(row):
        return jnp.sum(jnp.where(diagonal, row, 0.0), axis=1, keepdims=True)

    def stat_start(step, first, second):
        top = lax.broadcasted_iota(jnp.int32, (8, own), 0) == 0
        stat_send[step] = jnp.where(top, to_row(first), to_row(second))
        each(n_c, lambda j: stat_copy(step, j).start())

    def stat_total(step):
        each(n_c, lambda j: stat_copy(step, j).wait_recv())
        total = stat_send[step]
        for j in range(1, n_c):
            total = total + stat_recv[step, j]
        return to_column(total[0:1]), to_column(total[1:2])

    own_models = models_in[...]
    first_data = forward(0, own_models, lambda: None)
    each(n_s, lambda j: in_copies(j, src_peer(j), (2,))[0].wait_recv())
    own_noise = jnp.concatenate([nz_recv[k].astype(F32) for k in range(n_s)], axis=1)
    chunk_res = -(first_data + own_noise)
    res[...] = gather(0, chunk_res)

    def pair_sum(values):
        return jnp.sum(jnp.sum(values, axis=0), axis=1, keepdims=True)

    alphas = []
    for step in range(HSTEPS):
        last = step == HSTEPS - 1
        full = res[...]
        spread = pair_sum(full * full)
        delta = jnp.sqrt(spread / pairs_all + 1e-06)
        weight = delta[None] / jnp.maximum(jnp.abs(full), delta[None])
        weighted = weight * full
        for k in range(n_c):
            wlow[:, k * chunk : (k + 1) * chunk] = weighted[k].astype(BF16)
        grad = jnp.dot(wlow[...], oper[...], preferred_element_type=F32) * scale
        after = []

        def send_numer():
            grads[step] = grad
            numer_own = jnp.sum(grad * grad, axis=1, keepdims=True)
            after.append(numer_own)
            if last:
                after.append(delta / jnp.maximum(jnp.abs(chunk_res), delta))
            else:
                stat_start(step, numer_own, numer_own)

        image = forward(step + 1, grad.astype(BF16), send_numer)
        if last:
            curve_own = jnp.sum(after[1] * image * image, axis=1, keepdims=True)
            stat_start(step, after[0], curve_own)
            numer, curvature = stat_total(step)
            alpha = numer / (curvature + 1e-06)
        else:
            images = gather(step + 1, image)
            numer, _ = stat_total(step)
            curvature = pair_sum(weight * images * images)
            alpha = numer / (curvature + 1e-06)
            res[...] = full - alpha[None] * images
        chunk_res = chunk_res - alpha * image
        alphas.append(alpha)

    for k in range(n_s):
        fin_send[k] = chunk_res[:, k * share : (k + 1) * share]

    def fin_copy(j, slot):
        return to_src(
            fin_send.at[src_peer(j)], fin_recv.at[slot], fin_ssem.at[j], fin_rsem.at[j], src_peer(j)
        )

    each(n_s, lambda j: fin_copy(j, s).start())
    fin_recv[s] = fin_send[s]
    total_rec = -(alphas[0] * grads[0])
    for step in range(1, HSTEPS):
        total_rec = total_rec - alphas[step] * grads[step]
    rec_out[...] = total_rec

    def in_done(j):
        for copy in in_copies(j, s):
            copy.wait_send()

    each(n_s, in_done)
    for phase in range(HSTEPS + 1):
        each(n_c, lambda j, phase=phase: rs_copy(phase, j, cell_peer(j)).wait_send())
    for phase in range(HSTEPS):
        each(n_c, lambda j, phase=phase: ag_copy(phase, j, c).wait_send())
        each(n_c, lambda j, phase=phase: stat_copy(phase, j).wait_send())
    each(n_s, lambda j: fin_copy(j, src_peer(j)).wait_recv())
    res_out[...] = fin_recv[...].reshape(models_count, share).T
    each(n_s, lambda j: fin_copy(j, s).wait_send())


def split_pair(value, lanes):
    high = value.astype(BF16).astype(F32)
    lane = lax.broadcasted_iota(jnp.int32, value.shape, 1)
    return jnp.where(lane < lanes, high, value - high)


def gathered_body(
    n_s, n_c,
    gs, gr, ps, pr, order, models, noise,
    out,
    gs_in, gr_in, order_in, models_in, noise_in,
    fields, indices, nz_send, nz_recv, md_send, md_recv,
    gs_all, gs_low, gr_all, mask, onehot, pair_rows,
    noise_masked, x_send, x_recv, fin_send, fin_recv,
    load, f_ssem, f_rsem, i_ssem, i_rsem, m_ssem, m_rsem, x_ssem, x_rsem, fin_ssem, fin_rsem,
):
    s = lax.axis_index("src")
    c = lax.axis_index("cell")
    pairs = ps.shape[1]
    cells = gs.shape[1]
    s_dev = gs.shape[0]
    r_dev = gr.shape[0]
    own = models.shape[0] // n_s
    mine = own // n_c
    half = cells // 2
    sources = n_s * s_dev
    receivers = n_s * r_dev
    pairs_all = pairs * n_s
    scale = 1.0 / math.sqrt(cells * n_c)

    def src_peer(j):
        return jnp.bitwise_xor(s, j)

    def cell_peer(j):
        return jnp.bitwise_xor(c, j)

    def remote(src_ref, dst_ref, ssem, rsem, ds, dc):
        return pltpu.make_async_remote_copy(
            src_ref=src_ref, dst_ref=dst_ref, send_sem=ssem, recv_sem=rsem,
            device_id={"src": src_peer(ds), "cell": cell_peer(dc)}, device_id_type=MESH,
        )

    barrier = pltpu.get_barrier_semaphore()
    each(n_c, lambda j: pl.semaphore_signal(
        barrier, inc=1, device_id={"cell": cell_peer(j)}, device_id_type=MESH))
    each(n_s, lambda j: pl.semaphore_signal(
        barrier, inc=1, device_id={"src": src_peer(j)}, device_id_type=MESH))

    loads = [
        pltpu.make_async_copy(order, order_in, load.at[0]),
        pltpu.make_async_copy(gs, gs_in, load.at[1]),
        pltpu.make_async_copy(gr, gr_in, load.at[2]),
        pltpu.make_async_copy(ps, indices.at[s, 0], load.at[3]),
        pltpu.make_async_copy(pr, indices.at[s, 1], load.at[4]),
        pltpu.make_async_copy(
            models.at[pl.ds(pl.multiple_of(s * own, own), own), :], models_in, load.at[5]),
        pltpu.make_async_copy(noise, noise_in, load.at[6]),
    ]
    for copy in loads:
        copy.start()
    for copy in loads[:5]:
        copy.wait()
    rows = lax.broadcasted_iota(jnp.int32, (cells, cells), 0)
    select = jnp.where(rows == order_in[...], 1.0, 0.0).astype(BF16)
    raw = jnp.concatenate([gs_in[...].astype(F32), gr_in[...].astype(F32)], axis=0).astype(BF16)
    fields[c, s] = jnp.dot(raw, select, preferred_element_type=F32).astype(BF16)

    for copy in loads[5:]:
        copy.wait()
    wide = 2 * mine
    q = lax.broadcasted_iota(jnp.int32, (n_c * wide, own), 0)
    m = lax.broadcasted_iota(jnp.int32, (n_c * wide, own), 1)
    spread_rows = jnp.where((q % mine) * n_c + q // wide == m, 1.0, 0.0).astype(BF16)
    placed = jnp.dot(spread_rows, models_in[...], preferred_element_type=F32)
    low = lax.broadcasted_iota(jnp.int32, (n_c * wide, half), 0) % wide < mine
    placed = jnp.where(low, placed[:, :half], placed[:, half:])
    md_send[...] = placed.astype(BF16).reshape(n_c, wide, half)
    md_recv[c] = md_send[c]
    q = lax.broadcasted_iota(jnp.int32, (n_s * wide, models.shape[0]), 0)
    m = lax.broadcasted_iota(jnp.int32, (n_s * wide, models.shape[0]), 1)
    columns = jnp.where(
        ((q // wide) * own + (q % wide) * n_c + c == m) & (q % wide < mine), 1.0, 0.0).astype(BF16)
    nz = lax.dot_general(columns, noise_in[...], NT, preferred_element_type=F32)
    nz_send[...] = nz.astype(BF16).reshape(n_s, wide, pairs)
    nz_recv[s] = nz_send[s]

    pl.semaphore_wait(barrier, n_s + n_c - 2)

    done = []
    count = [0]

    def send_block(t, g, ds, dc):
        at = count[0]
        count[0] += 1
        copy = remote(fields.at[t, g], fields.at[t, g], f_ssem.at[at], f_rsem.at[t, g], ds, dc)
        copy.start()
        done.append(copy.wait_send)

    def got_block(t, g):
        remote(fields.at[t, g], fields.at[t, g], f_ssem.at[0], f_rsem.at[t, g], 0, 1).wait_recv()

    def index_copy(j, slot):
        return remote(indices.at[slot], indices.at[slot], i_ssem.at[0, j], i_rsem.at[0, j], j, 0)

    def noise_copy(j):
        return remote(
            nz_send.at[src_peer(j)], nz_recv.at[s], i_ssem.at[1, j], i_rsem.at[1, j], j, 0)

    def noise_got(j):
        g = src_peer(j)
        remote(nz_send.at[g], nz_recv.at[g], i_ssem.at[1, j], i_rsem.at[1, j], j, 0).wait_recv()

    def model_copy(j):
        return remote(md_send.at[cell_peer(j)], md_recv.at[c], m_ssem.at[j], m_rsem.at[j], 0, j)

    def model_got(j):
        t = cell_peer(j)
        remote(md_send.at[t], md_recv.at[t], m_ssem.at[j], m_rsem.at[j], 0, j).wait_recv()

    steps = range(2, n_c, 2)
    across = n_s - 1
    near = range(1, across)
    send_block(c, s, across, 0)
    for d in steps:
        send_block(c, s, 0, d)
    for j in near:
        send_block(c, s, j, 0)
    send_block(c, s, 0, 1)
    each(n_s, lambda j: index_copy(j, s).start())

    each(n_c, lambda j: model_copy(j).start())
    each(n_s, lambda j: noise_copy(j).start())

    g = src_peer(across)
    got_block(c, g)
    for d in steps:
        send_block(c, g, 0, d)
    send_block(c, g, 0, 1)
    twice = (n_c - 2,)
    got_block(cell_peer(1), s)
    for d in steps:
        t = cell_peer(d)
        got_block(t, s)
        for j in near:
            send_block(t, s, j, 0)
        if d in twice:
            for j in near:
                send_block(t, s, j, 1)
        send_block(t, s, 0, 1)

    each(n_s, lambda j: index_copy(j, src_peer(j)).wait_recv())
    row = lax.broadcasted_iota(jnp.int32, (2 * receivers, pairs), 0)
    row = jnp.where(row < receivers, row, row - receivers)
    source = lax.broadcasted_iota(jnp.int32, (s_dev, pairs), 0)
    for g in range(n_s):
        mask[g] = jnp.where(source == indices[g, 0], 1.0, 0.0)
        hit = jnp.where(row == indices[g, 1], 1.0, 0.0)
        onehot[g] = hit.astype(BF16)
        pair_rows[g] = hit.T.astype(BF16)

    def unpack(t):
        block = fields[t].astype(F32)
        gs_all[t] = block[:, :s_dev].reshape(sources, cells)
        gs_low[t] = block[:, :s_dev].reshape(sources, cells).astype(BF16)
        part = block[:, s_dev:].reshape(receivers, cells).astype(BF16)
        gr_all[t] = jnp.concatenate([part, part], axis=0)

    def forward(t, lines):
        base = gs_low[t]
        left = jnp.concatenate([base * line.astype(BF16) for line in lines], axis=0)
        return lax.dot_general(left, gr_all[t], NT, preferred_element_type=F32)

    data = [None]

    def first(d):
        t = cell_peer(d)
        unpack(t)
        if d:
            model_got(d)
        line = md_recv[t].astype(F32)
        lines = [
            jnp.concatenate([line[j : j + 1], line[mine + j : mine + j + 1]], axis=1)
            for j in range(mine)
        ]
        part = forward(t, lines)
        data[0] = part if data[0] is None else data[0] + part

    def own_core(d):
        t = cell_peer(d)
        for j in near if d == 0 else range(1, n_s):
            g = src_peer(j)
            got_block(t, g)
            if d not in twice or j == across:
                send_block(t, g, 0, 1)
        first(d)

    def other_core(d):
        t = cell_peer(d + 1)
        for j in range(1 if d == 0 else 0, n_s):
            got_block(t, src_peer(j))
        first(d + 1)

    own_core(0)
    each(n_s, noise_got)
    for g in range(n_s):
        line = nz_recv[g].astype(F32)
        for j in range(mine):
            noise_masked[g, j * s_dev : (j + 1) * s_dev] = line[j : j + 1] * mask[g]
    for d in steps:
        own_core(d)
        other_core(d - 2)
    other_core(n_c - 2)

    def to_pairs(value):
        mixed = split_pair(value * scale, receivers).reshape(mine, n_s, s_dev, 2 * receivers)
        out = []
        for g in range(n_s):
            left = mixed[:, g].reshape(mine * s_dev, 2 * receivers).astype(BF16)
            at_pairs = jnp.dot(left, onehot[g], preferred_element_type=F32)
            out.append(at_pairs.reshape(mine, s_dev, pairs) * mask[g][None])
        return out

    def from_pairs(values):
        out = [
            jnp.dot(
                values[g].reshape(mine * s_dev, pairs).astype(BF16), pair_rows[g],
                preferred_element_type=F32).reshape(mine, 1, s_dev, 2 * receivers)
            for g in range(n_s)
        ]
        whole = jnp.concatenate(out, axis=1).reshape(mine * sources, 2 * receivers)
        return split_pair(whole * scale, receivers).astype(BF16)

    def pair_sum(values):
        total = values[0]
        for value in values[1:]:
            total = total + value
        return jnp.sum(jnp.sum(total, axis=1, keepdims=True), axis=2, keepdims=True)

    def x_copy(step, j):
        return remote(
            x_send.at[step, cell_peer(j)], x_recv.at[step, c],
            x_ssem.at[step, j], x_rsem.at[step, j], 0, j)

    def x_got(step, j):
        t = cell_peer(j)
        remote(
            x_send.at[step, t], x_recv.at[step, t],
            x_ssem.at[step, j], x_rsem.at[step, j], 0, j).wait_recv()

    first_data = to_pairs(data[0])
    res = [-(value + noise_masked[g].reshape(mine, s_dev, pairs)) for g, value in enumerate(first_data)]

    place = lax.broadcasted_iota(jnp.int32, (wide, half), 0)
    farthest = [d + k for d in range(n_c - 2, -1, -2) for k in (1, 0)]
    alphas = []
    for step in range(HSTEPS):
        delta = jnp.sqrt(pair_sum([value * value for value in res]) / pairs_all + 1e-06)
        weight = [delta / jnp.maximum(jnp.abs(value), delta) for value in res]
        back = from_pairs([w * value for w, value in zip(weight, res)])
        numer = None
        data = None
        for d in farthest:
            t = cell_peer(d)
            fan = jnp.dot(back, gr_all[t], preferred_element_type=F32)
            grad = jnp.sum(
                fan.reshape(mine, sources, cells) * gs_all[t][None], axis=1, keepdims=True)
            square = grad * grad
            numer = square if numer is None else numer + square
            low = grad.astype(BF16).astype(F32)
            part = forward(t, [low[j] for j in range(mine)])
            data = part if data is None else data + part
            packed = jnp.zeros((wide, half), F32)
            for j in range(mine):
                packed = jnp.where(place == j, low[j][:, :half], packed)
                packed = jnp.where(place == mine + j, low[j][:, half:], packed)
            x_send[step, t] = packed.astype(BF16)
        x_recv[step, c] = x_send[step, c]
        image = to_pairs(data)
        curvature = pair_sum([w * value * value for w, value in zip(weight, image)])
        alpha = jnp.sum(numer, axis=2, keepdims=True) / (curvature + 1e-06)
        res = [value - alpha * other for value, other in zip(res, image)]
        alphas.append(alpha)
        if step < HSTEPS - 1:
            for d in farthest:
                if d:
                    x_copy(step, d).start()

    odd = c % 2
    two = 2 * (pairs // n_c)
    room = two // (2 * mine)
    lane = lax.broadcasted_iota(jnp.int32, (1, two), 1)
    marks = jnp.zeros((1, two), F32)
    for j in range(mine):
        for step in range(HSTEPS):
            marks = jnp.where(lane // room == 2 * j + step, alphas[step][j], marks)
    for g in range(n_s):
        lines = jnp.sum(res[g], axis=1, keepdims=True)
        for h in range(n_c // 2):
            fin_send[g, h] = jnp.concatenate(
                [lines[j][:, h * two : (h + 1) * two] for j in range(mine)] + [marks], axis=1)

    others = n_s * n_c

    def fin_start(i, carry):
        a, b = (others - i) // n_c, (others - i) % n_c
        remote(
            fin_send.at[src_peer(a), cell_peer(b) // 2], fin_recv.at[s * n_c + c],
            fin_ssem.at[0], fin_rsem.at[0], a, b).start()
        return carry

    lax.fori_loop(1, n_c * (n_s - 1) + 1, fin_start, 0)
    for d in farthest:
        if d:
            x_copy(HSTEPS - 1, d).start()
    lax.fori_loop(n_c * (n_s - 1) + 1, others, fin_start, 0)
    fin_recv[s * n_c + c] = fin_send[s, c // 2]

    m = lax.broadcasted_iota(jnp.int32, (own, n_c * wide), 0)
    q = lax.broadcasted_iota(jnp.int32, (own, n_c * wide), 1)
    at = (m % n_c) * wide + m // n_c
    rows_of = [jnp.where(q == at + k * mine, 1.0, 0.0).astype(BF16) for k in (0, 1)]
    grads = []
    for step in range(HSTEPS):
        for j in range(n_c - 1, 0, -1):
            x_got(step, j)
        blocks = x_recv[step].astype(F32).reshape(n_c * wide, half).astype(BF16)
        grads.append(jnp.concatenate(
            [jnp.dot(pick, blocks, preferred_element_type=F32) for pick in rows_of], axis=1))

    for wait in done:
        wait()
    each(n_s, lambda j: index_copy(j, s).wait_send())
    each(n_c, lambda j: model_copy(j).wait_send())
    each(n_s, lambda j: noise_copy(j).wait_send())
    for step in range(HSTEPS):
        each(n_c, lambda j, step=step: x_copy(step, j).wait_send())

    rest = fin_recv.at[pl.ds(0, n_s * n_c - 1)]
    fin_all = remote(rest, rest, fin_ssem.at[0], fin_rsem.at[0], 0, 1)
    fin_all.wait_recv()
    notes = fin_recv[pl.ds(s * n_c, n_c), 0, mine * two :]
    for j in range(mine):
        at = pl.ds(j * n_c, n_c)
        here = slice(j * n_c, (j + 1) * n_c)
        first_of, second_of = (
            notes[:, (2 * j + step) * room : (2 * j + step) * room + 1] for step in range(HSTEPS))
        out[at, :] = -(first_of * grads[0][here] + second_of * grads[1][here])
    lines = jnp.concatenate(
        [
            fin_recv[:, 0, j * two : (j + 1) * two].reshape(n_s, 1, n_c, two)
            for j in range(mine)
        ], axis=1).reshape(n_s * own, two).T
    lines = jnp.where(odd == 0, lines[: two // 2], lines[two // 2 :])
    tall = out.shape[0] - own
    for k in range(lines.shape[0] // tall):
        out[own:, k * lines.shape[1] : (k + 1) * lines.shape[1]] = lines[k * tall : (k + 1) * tall]
    fin_all.wait_send()


def gathered_call(n_s, n_c, *arrays):
    gs, gr, ps, _, order, models, noise = arrays
    s_dev, cells = gs.shape
    r_dev = gr.shape[0]
    pairs = ps.shape[1]
    models_count = models.shape[0]
    own = models_count // n_s
    wide = 2 * (own // n_c)
    share = pairs // n_c
    dma = pltpu.SemaphoreType.DMA
    tall = share * models_count // cells
    out = pl.pallas_call(
        functools.partial(gathered_body, n_s, n_c),
        out_shape=pltpu.VMEM((own + tall, cells), F32),
        in_specs=[pl.BlockSpec(memory_space=pltpu.HBM)] * 7,
        out_specs=pl.BlockSpec(memory_space=pltpu.VMEM),
        scratch_shapes=[
            pltpu.VMEM((s_dev, cells), BF16),
            pltpu.VMEM((r_dev, cells), BF16),
            pltpu.VMEM((1, cells), jnp.int32),
            pltpu.VMEM((own, cells), BF16),
            pltpu.VMEM((pairs, models_count), BF16),
            pltpu.VMEM((n_c, n_s, s_dev + r_dev, cells), BF16),
            pltpu.VMEM((n_s, 2, 1, pairs), jnp.int32),
            pltpu.VMEM((n_s, wide, pairs), BF16),
            pltpu.VMEM((n_s, wide, pairs), BF16),
            pltpu.VMEM((n_c, wide, cells // 2), BF16),
            pltpu.VMEM((n_c, wide, cells // 2), BF16),
            pltpu.VMEM((n_c, n_s * s_dev, cells), F32),
            pltpu.VMEM((n_c, n_s * s_dev, cells), BF16),
            pltpu.VMEM((n_c, 2 * n_s * r_dev, cells), BF16),
            pltpu.VMEM((n_s, s_dev, pairs), F32),
            pltpu.VMEM((n_s, 2 * n_s * r_dev, pairs), BF16),
            pltpu.VMEM((n_s, pairs, 2 * n_s * r_dev), BF16),
            pltpu.VMEM((n_s, wide // 2 * s_dev, pairs), F32),
            pltpu.VMEM((HSTEPS, n_c, wide, cells // 2), BF16),
            pltpu.VMEM((HSTEPS, n_c, wide, cells // 2), BF16),
            pltpu.VMEM((n_s, n_c // 2, 1, (wide // 2 + 1) * 2 * share), F32),
            pltpu.VMEM((n_s * n_c, 1, (wide // 2 + 1) * 2 * share), F32),
            dma((7,)), dma((n_s * n_c,)), dma((n_c, n_s)),
            dma((2, n_s)), dma((2, n_s)),
            dma((n_c,)), dma((n_c,)),
            dma((HSTEPS, n_c)), dma((HSTEPS, n_c)),
            dma((1,)), dma((1,)),
        ],
        compiler_params=pltpu.CompilerParams(
            collective_id=0, has_side_effects=True, vmem_limit_bytes=60 * 1024 * 1024
        ),
    )(*arrays)
    pieces = [
        out[own:, k * models_count : (k + 1) * models_count] for k in range(cells // models_count)
    ]
    return out[:own], jnp.concatenate(pieces, axis=0)


def fits_gathered(n_s, n_c, s_dev, r_dev, cells, pairs, models_count):
    return (
        n_c & (n_c - 1) == 0 and n_s == 4
        and models_count == 4 * n_s * n_c
        and s_dev == 8 and r_dev % 8 == 0 and 2 * n_s * r_dev == 128
        and pairs == 64 * n_c and cells % 256 == 0
        and cells % models_count == 0 and 64 * models_count == 8 * cells
    )


def shards(
    green_source, green_receiver, pair_source, pair_receiver, cell_order, test_models, data_noise
):
    n_s = lax.axis_size("src")
    n_c = lax.axis_size("cell")
    s_dev, cells = green_source.shape
    r_dev = green_receiver.shape[0]
    group_pairs = pair_source.shape[0]
    models_count = test_models.shape[0]
    own = models_count // n_s
    share = group_pairs // n_c
    chunk = share * n_s
    pairs_all = group_pairs * n_s
    arrays = (
        green_source, green_receiver, pair_source[None, :], pair_receiver[None, :],
        cell_order, test_models, data_noise,
    )
    if fits_gathered(n_s, n_c, s_dev, r_dev, cells, group_pairs, models_count):
        return gathered_call(n_s, n_c, *arrays)
    dma = pltpu.SemaphoreType.DMA
    return pl.pallas_call(
        functools.partial(kernel_body, n_s, n_c),
        out_shape=(
            pltpu.VMEM((own, cells), F32),
            pltpu.VMEM((share, models_count), F32),
        ),
        in_specs=[pl.BlockSpec(memory_space=pltpu.HBM)] * 7,
        out_specs=[pl.BlockSpec(memory_space=pltpu.VMEM)] * 2,
        scratch_shapes=[
            pltpu.VMEM((s_dev, cells), BF16),
            pltpu.VMEM((r_dev, cells), BF16),
            pltpu.VMEM((1, cells), jnp.int32),
            pltpu.VMEM((own, cells), BF16),
            pltpu.VMEM((share, models_count), BF16),
            pltpu.VMEM((n_s, s_dev + r_dev, cells), BF16),
            pltpu.VMEM((n_s, 2, 1, group_pairs), jnp.int32),
            pltpu.VMEM((n_s, own, share), BF16),
            pltpu.VMEM((n_s, own, share), BF16),
            pltpu.VMEM((pairs_all, n_s * (s_dev + r_dev)), BF16),
            pltpu.VMEM((pairs_all, cells), BF16),
            pltpu.VMEM((HSTEPS + 1, n_c, own, chunk), BF16),
            pltpu.VMEM((HSTEPS + 1, n_c, own, chunk), BF16),
            pltpu.VMEM((HSTEPS, n_c, own, chunk), BF16),
            pltpu.VMEM((HSTEPS, 8, own), F32),
            pltpu.VMEM((HSTEPS, n_c, 8, own), F32),
            pltpu.VMEM((n_s, own, share), F32),
            pltpu.VMEM((n_s, own, share), F32),
            pltpu.VMEM((own, pairs_all), BF16),
            pltpu.VMEM((n_c, own, chunk), F32),
            pltpu.VMEM((HSTEPS, own, cells), F32),
            dma((7,)), dma((3, n_s)), dma((3, n_s)),
            dma((HSTEPS + 1, n_c)), dma((HSTEPS + 1, n_c)),
            dma((HSTEPS, n_c)), dma((HSTEPS, n_c)),
            dma((HSTEPS, n_c)), dma((HSTEPS, n_c)),
            dma((n_s,)), dma((n_s,)),
        ],
        compiler_params=pltpu.CompilerParams(
            collective_id=0, has_side_effects=True, vmem_limit_bytes=60 * 1024 * 1024
        ),
    )(*arrays)


def solution(mesh):
    return jax.shard_map(
        shards,
        mesh=mesh,
        in_specs=(
            P("src", "cell"),
            P("src", "cell"),
            P("src"),
            P("src"),
            P("cell", None),
            P(None, "cell"),
            P("src", None),
        ),
        out_specs=(P("src", "cell"), P(("src", "cell"), None)),
        check_vma=False,
    )
```
